32 devices in a mesh: gx: 16 (over z, x, core), gy: 2 (over y).
Axes of the slice: x: 2, y: 2, z: 4, core: 2. Of those that a mesh axis runs over, the one named last changes fastest.
Arguments:
- fine_old: float32 [2, 3, 40, 32, 512], P(None, None, None, 'gx', 'gy'), may hold values from -6 to 6
- fine_now: float32 [2, 3, 40, 32, 512], P(None, None, None, 'gx', 'gy'), may hold values from -6 to 6
- coarse_old: float32 [2, 3, 80, 16, 256], P(None, None, None, 'gx', 'gy'), may hold values from -6 to 6
- coarse_now: float32 [2, 3, 80, 16, 256], P(None, None, None, 'gx', 'gy'), may hold values from -6 to 6
- shear_fine: float32 [40, 32, 512], P(None, 'gx', 'gy'), may hold values from 0.3 to 1.2
- lame_fine: float32 [40, 32, 512], P(None, 'gx', 'gy'), may hold values from 0.5 to 2
- shear_coarse: float32 [80, 16, 256], P(None, 'gx', 'gy'), may hold values from 0.3 to 1.2
- lame_coarse: float32 [80, 16, 256], P(None, 'gx', 'gy'), may hold values from 0.5 to 2
- topography: int32 [32, 512], P('gx', 'gy'), may hold values from 0 to 512
Outputs:
- fine_field: float32 [2, 3, 40, 32, 512], P(None, None, None, 'gx', 'gy')
- coarse_field: float32 [2, 3, 80, 16, 256], P(None, None, None, 'gx', 'gy')
- fine_kernel: float32 [40, 32, 512], P(None, 'gx', 'gy')
- coarse_kernel: float32 [80, 16, 256], P(None, 'gx', 'gy')
The draws below stay inside these ranges and needn't reach their ends.
All inputs are finite; a program needn't handle non-finite values.
Results may differ from the reference program's by a relative error of at most 0.0003.
Values sent between devices are 32-bit elements; how exact they have to be, the bound alone decides.
A program may use at most 64 MiB of HBM per device.

```python
import math
import jax
import jax.numpy as jnp
from jax import lax

FZ = 40
CZ = 80
FXD = 2
STEPS = 2
NX = 32
NY = 512
NXC = 16
NYC = 256


def plant(array, key, smallest, high):
    longest = array.shape.index(max(array.shape))
    spots = []
    for shift in (0, 1):
        where = [jax.random.randint(jax.random.fold_in(key, axis), (), 0, length) for axis, length in enumerate(array.shape)]
        where[longest] = (where[longest] + shift) % array.shape[longest]
        spots.append(tuple(where))
    return array.at[spots[0]].set(smallest).at[spots[1]].set(high)


def shard_levels(own_key, dims, split, least, largest):
    factor_of, own = 1.0, jax.random.fold_in(own_key, 6)
    for axis_at, parts in split:
        steps = jnp.exp(jax.random.uniform(jax.random.fold_in(own, axis_at), (parts,), jnp.float32, least / len(split), largest / len(split)))
        factor_of = factor_of * jnp.repeat(steps, dims[axis_at] // parts).reshape([-1 if axis == axis_at else 1 for axis in range(len(dims))])
    return factor_of


def gaussian(rng, extent, scale, reach, cuts=(), kind=jnp.bfloat16):
    array = scale * jax.random.normal(rng, extent, jnp.float32)
    if cuts:
        array = array * shard_levels(rng, extent, cuts, -0.22, 0.18)
    return jnp.clip(array, -reach, reach).astype(kind)


def setup_inputs(seed: int = 0) -> dict:
    keys = jax.random.split(jax.random.key(seed), 10)
    return {
        "fine_old": gaussian(keys[0], (2, 3, FZ, NX, NY), 1.0, 6.0, ((3, 16), (4, 2)), jnp.float32),
        "fine_now": gaussian(keys[1], (2, 3, FZ, NX, NY), 1.0, 6.0, ((3, 16), (4, 2)), jnp.float32),
        "coarse_old": gaussian(keys[2], (2, 3, CZ, NXC, NYC), 1.0, 6.0, ((3, 16), (4, 2)), jnp.float32),
        "coarse_now": gaussian(keys[3], (2, 3, CZ, NXC, NYC), 1.0, 6.0, ((3, 16), (4, 2)), jnp.float32),
        "shear_fine": jnp.clip(jnp.exp(math.log(1.2) - 1.3862944 * jax.random.uniform(keys[4], (FZ, NX, NY), jnp.float32) ** shard_levels(keys[4], (FZ, NX, NY), ((1, 16), (2, 2)), -0.2, 0.2)), 0.3, 1.2),
        "lame_fine": jnp.clip(jnp.exp(math.log(2.0) - 1.3862944 * jax.random.uniform(keys[5], (FZ, NX, NY), jnp.float32) ** shard_levels(keys[5], (FZ, NX, NY), ((1, 16), (2, 2)), -0.2, 0.2)), 0.5, 2.0),
        "shear_coarse": jnp.clip(jnp.exp(math.log(1.2) - 1.3862944 * jax.random.uniform(keys[6], (CZ, NXC, NYC), jnp.float32) ** shard_levels(keys[6], (CZ, NXC, NYC), ((1, 16), (2, 2)), -0.2, 0.2)), 0.3, 1.2),
        "lame_coarse": jnp.clip(jnp.exp(math.log(2.0) - 1.3862944 * jax.random.uniform(keys[7], (CZ, NXC, NYC), jnp.float32) ** shard_levels(keys[7], (CZ, NXC, NYC), ((1, 16), (2, 2)), -0.2, 0.2)), 0.5, 2.0),
        "topography": plant(jax.random.randint(keys[8], (NX, NY), 0, 513), jax.random.fold_in(keys[8], 1), 0, 512).astype(jnp.int32),
    }


STEP_SQUARED = 0.04


def offset(padded, up_down, along_x, along_y):
    depth_cells = padded.shape[2] - 2
    row_count = padded.shape[3] - 2
    column_count = padded.shape[4] - 2
    return padded[:, :, 1 + up_down:1 + up_down + depth_cells, 1 + along_x:1 + along_x + row_count, 1 + along_y:1 + along_y + column_count]


def accelerate(padded, spacing_pad, grid_step, shear, lame):
    center = offset(padded, 0, 0, 0)
    spacing = spacing_pad[1:-1, 1:-1]
    inverse_area = 1.0 / (grid_step * grid_step)
    curve_xx = (offset(padded, 0, 1, 0) - 2.0 * center + offset(padded, 0, -1, 0)) * inverse_area
    curve_yy = (offset(padded, 0, 0, 1) - 2.0 * center + offset(padded, 0, 0, -1)) * inverse_area
    curve_zz = (offset(padded, 1, 0, 0) - 2.0 * center + offset(padded, -1, 0, 0)) / (spacing * spacing)
    mixed_xy = (offset(padded, 0, 1, 1) - offset(padded, 0, 1, -1) - offset(padded, 0, -1, 1) + offset(padded, 0, -1, -1)) * (0.25 * inverse_area)
    east_side = (offset(padded, 1, 1, 0) - offset(padded, -1, 1, 0)) / (2.0 * spacing_pad[2:, 1:-1])
    west_side = (offset(padded, 1, -1, 0) - offset(padded, -1, -1, 0)) / (2.0 * spacing_pad[:-2, 1:-1])
    mixed_xz = (east_side - west_side) * (0.5 / grid_step)
    north_side = (offset(padded, 1, 0, 1) - offset(padded, -1, 0, 1)) / (2.0 * spacing_pad[1:-1, 2:])
    south_side = (offset(padded, 1, 0, -1) - offset(padded, -1, 0, -1)) / (2.0 * spacing_pad[1:-1, :-2])
    mixed_yz = (north_side - south_side) * (0.5 / grid_step)
    laplace = curve_xx + curve_yy + curve_zz
    grad_div = jnp.stack([
        curve_xx[:, 0] + mixed_xy[:, 1] + mixed_xz[:, 2],
        mixed_xy[:, 0] + curve_yy[:, 1] + mixed_yz[:, 2],
        mixed_xz[:, 0] + mixed_yz[:, 1] + curve_zz[:, 2]], axis=1)
    return shear * laplace + (lame + shear) * grad_div


def restrict(plane):
    row_sums = plane[..., 0::2, :] + plane[..., 1::2, :]
    summed = row_sums[..., 0::2] + row_sums[..., 1::2]
    return 0.25 * summed


def prolong(padded_plane):
    middle = 0.75 * padded_plane[..., 1:-1, :]
    even_rows = middle + 0.25 * padded_plane[..., :-2, :]
    odd_rows = middle + 0.25 * padded_plane[..., 2:, :]
    plane_dims = even_rows.shape
    row_pairs = jnp.stack([even_rows, odd_rows], axis=-2).reshape(plane_dims[:-2] + (2 * plane_dims[-2], plane_dims[-1]))
    center_cols = 0.75 * row_pairs[..., 1:-1]
    even_cols = center_cols + 0.25 * row_pairs[..., :-2]
    odd_cols = center_cols + 0.25 * row_pairs[..., 2:]
    col_dims = even_cols.shape
    return jnp.stack([even_cols, odd_cols], axis=-1).reshape(col_dims[:-1] + (2 * col_dims[-1],))


def pad_sides(block):
    return jnp.pad(block, ((0, 0), (0, 0), (0, 0), (1, 1), (1, 1)))


def blocked(padded, spacing_pad, grid_step, shear, lame, block_rows):
    block_count = (padded.shape[3] - 2) // block_rows

    def one_block(block_index):
        first_row = (block_index * block_rows).astype(jnp.int32)
        field_piece = lax.dynamic_slice_in_dim(padded, first_row, block_rows + 2, 3)
        space_piece = lax.dynamic_slice_in_dim(spacing_pad, first_row, block_rows + 2, 0)
        shear_piece = lax.dynamic_slice_in_dim(shear, first_row, block_rows, 1)
        lame_piece = lax.dynamic_slice_in_dim(lame, first_row, block_rows, 1)
        return accelerate(field_piece, space_piece, grid_step, shear_piece, lame_piece)

    pieces = lax.map(one_block, jnp.arange(block_count, dtype=jnp.int32))
    reordered = jnp.moveaxis(pieces, 0, 3)
    dims_now = reordered.shape
    return reordered.reshape(dims_now[:3] + (dims_now[3] * dims_now[4], dims_now[5]))


def reference(fine_old, fine_now, coarse_old, coarse_now, shear_fine, lame_fine, shear_coarse, lame_coarse, topography):
    heights = jnp.pad(topography.astype(jnp.float32), 1)
    fine_space = 1.0 + heights / 1024.0
    coarse_space = jnp.full((NXC + 2, NYC + 2), 2.0, jnp.float32)
    fine_kernel = jnp.zeros((FZ, NX, NY), jnp.float32)
    coarse_kernel = jnp.zeros((CZ, NXC, NYC), jnp.float32)
    for time_level in range(STEPS):
        ridge = restrict(fine_now[:, :, -1])
        floor_plane = jnp.zeros_like(ridge)
        coarse_ext = jnp.concatenate([ridge[:, :, None], coarse_now, floor_plane[:, :, None]], axis=2)
        coarse_pad = pad_sides(coarse_ext)
        ghost = prolong(coarse_pad[:, :, 1])
        fine_ext = jnp.concatenate([fine_now[:, :, :1], fine_now, ghost[:, :, None]], axis=2)
        fine_pad = pad_sides(fine_ext)
        fine_next = 2.0 * fine_now - fine_old + STEP_SQUARED * blocked(fine_pad, fine_space, 1.0, shear_fine, lame_fine, FXD)
        coarse_next = 2.0 * coarse_now - coarse_old + STEP_SQUARED * blocked(coarse_pad, coarse_space, 2.0, shear_coarse, lame_coarse, FXD // 2)
        fine_kernel = fine_kernel + jnp.sum(fine_next[0] * fine_next[1], axis=0)
        coarse_kernel = coarse_kernel + jnp.sum(coarse_next[0] * coarse_next[1], axis=0)
        fine_old, fine_now = fine_now, fine_next
        coarse_old, coarse_now = coarse_now, coarse_next
    return fine_now, coarse_now, fine_kernel, coarse_kernel
```

```python
import functools

import jax
import jax.numpy as jnp
from jax import lax
from jax.experimental import pallas as pl
from jax.experimental.pallas import tpu as pltpu
from jax.sharding import PartitionSpec as P

STEPS = 2
STEP_SQUARED = 0.04
LANES = 128
HALF = LANES // 2
TOP = 8


def stencil(ext, s, depth, own, grid_step, half_inv, inv_sq):
    total = ext.shape[-1]
    inverse_area = 1.0 / (grid_step * grid_step)
    tilt = 0.5 / grid_step

    def rows(slot, c, shift):
        return ext[slot, c, TOP + shift : TOP + shift + depth, :]

    def across(v):
        return pltpu.roll(v, total - 1, 1)[:, :own] - pltpu.roll(v, 1, 1)[:, :own]

    xx, yy, zz, mxy, mxz, myz = [], [], [], {}, {}, {}
    for c in range(3):
        wide = rows(s, c, 0)
        mid = wide[:, :own]
        east, west = rows(s + 1, c, 0), rows(s - 1, c, 0)
        down, up = rows(s, c, 1), rows(s, c, -1)
        twice = 2.0 * mid
        xx.append((east[:, :own] - twice + west[:, :own]) * inverse_area)
        yy.append(
            (pltpu.roll(wide, total - 1, 1)[:, :own] - twice + pltpu.roll(wide, 1, 1)[:, :own])
            * inverse_area
        )
        zz.append((down[:, :own] - twice + up[:, :own]) * inv_sq[s][:, :own])
        if c != 2:
            mxy[c] = across(east - west) * (0.25 * inverse_area)
        if c != 1:
            e = (rows(s + 1, c, 1) - rows(s + 1, c, -1))[:, :own] * half_inv[s + 1][:, :own]
            w = (rows(s - 1, c, 1) - rows(s - 1, c, -1))[:, :own] * half_inv[s - 1][:, :own]
            mxz[c] = (e - w) * tilt
        if c != 0:
            myz[c] = across((down - up) * half_inv[s]) * tilt
    laplace = [xx[c] + yy[c] + zz[c] for c in range(3)]
    grad_div = [
        xx[0] + mxy[1] + mxz[2],
        mxy[0] + yy[1] + myz[2],
        mxz[0] + myz[1] + zz[2],
    ]
    return laplace, grad_div


def body(
    nx, ny, fz, cz, fy, cy,
    fold, fnow, cold, cnow, shf, laf, shc, lac, topo,
    fout, cout, fker, cker,
    fn, cn, xf, xc, xg, pk, yr, mg, jown, jx, ext, extc, ghin, ghost,
    xs, xr, gs, gr, ys, yrs, js, jr,
):
    gx, gy = lax.axis_index("gx"), lax.axis_index("gy")
    has_x = (gx > 0, gx < nx - 1)
    has_y = (gy > 0, gy < ny - 1)
    tiles = fy // LANES
    rows_c = cn.shape[2]

    barrier = pltpu.get_barrier_semaphore()
    for side in range(2):
        step = 2 * side - 1

        @pl.when(has_x[side])
        def _():
            pl.semaphore_signal(barrier, inc=1, device_id={"gx": gx + step})

        @pl.when(has_y[side])
        def _():
            pl.semaphore_signal(barrier, inc=1, device_id={"gy": gy + step})

        @pl.when(jnp.logical_not(has_x[side]))
        def _():
            xf[:, side] = jnp.zeros(xf.shape[:1] + xf.shape[2:], jnp.float32)
            xc[:, side] = jnp.zeros(xc.shape[:1] + xc.shape[2:], jnp.float32)
            xg[:, side] = jnp.zeros(xg.shape[:1] + xg.shape[2:], jnp.float32)
            jx[side] = jnp.ones(jx.shape[1:], jnp.float32)

        @pl.when(jnp.logical_not(has_y[side]))
        def _():
            yr[:, side] = jnp.zeros(yr.shape[:1] + yr.shape[2:], jnp.float32)

    def x_copies(t, f, d):
        part = pl.ds(3 * f, 3)
        dev = {"gx": gx + 2 * d - 1}
        return (
            pltpu.make_async_remote_copy(
                cn.at[t, part], xc.at[t, 1 - d, part], xs.at[t, d, f, 0], xr.at[t, 1 - d, f, 0],
                device_id=dev,
            ),
            pltpu.make_async_remote_copy(
                fn.at[t, d, part], xf.at[t, 1 - d, part], xs.at[t, d, f, 1], xr.at[t, 1 - d, f, 1],
                device_id=dev,
            ),
        )

    def x_wait_copies(t, f, d):
        part = pl.ds(3 * f, 3)
        dev = {"gx": gx + 2 * d - 1}
        return (
            pltpu.make_async_remote_copy(
                cn.at[t, part], xc.at[t, d, part], xs.at[t, d, f, 0], xr.at[t, d, f, 0],
                device_id=dev,
            ),
            pltpu.make_async_remote_copy(
                fn.at[t, d, part], xf.at[t, d, part], xs.at[t, d, f, 1], xr.at[t, d, f, 1],
                device_id=dev,
            ),
        )

    def g_copy(t, d, land):
        return pltpu.make_async_remote_copy(
            mg.at[t], xg.at[t, land], gs.at[t, d], gr.at[t, land], device_id={"gx": gx + 2 * d - 1}
        )

    def y_copy(t, d, land):
        return pltpu.make_async_remote_copy(
            pk.at[t, d], yr.at[t, land], ys.at[t, d], yrs.at[t, land],
            device_id={"gy": gy + 2 * d - 1},
        )

    def j_copy(d, land):
        return pltpu.make_async_remote_copy(
            jown, jx.at[land], js.at[d], jr.at[land], device_id={"gx": gx + 2 * d - 1}
        )

    def each(flags, action):
        for d in range(2):
            pl.when(flags[d])(functools.partial(action, d))

    def send_x(t, f):
        def go(d):
            for copy in x_copies(t, f, d):
                copy.start()

        each(has_x, go)

    lane_f = lax.broadcasted_iota(jnp.int32, (fz, LANES), 1)
    lane_c = lax.broadcasted_iota(jnp.int32, (rows_c, LANES), 1)

    pair_row = lax.broadcasted_iota(jnp.int32, (fy, cy), 0)
    pair_col = lax.broadcasted_iota(jnp.int32, (fy, cy), 1)
    pairs = jnp.where(pair_row // 2 == pair_col, 0.25, 0.0).astype(jnp.float32)
    src = lax.broadcasted_iota(jnp.int32, (cy + LANES, fy + LANES), 0)
    dst = lax.broadcasted_iota(jnp.int32, (cy + LANES, fy + LANES), 1)
    src = jnp.where(src == cy + LANES - 1, -1, src)
    dst = jnp.where(dst == fy + LANES - 1, -1, dst)
    near = (dst + 2) // 2 - 1
    other = near + 2 * (dst + 2 - 2 * (near + 1)) - 1
    spread = jnp.where(src == near, 0.75, jnp.where(src == other, 0.25, 0.0)).astype(jnp.float32)

    def dot(a, b):
        return lax.dot_general(
            a, b, (((1,), (0,)), ((), ())),
            precision=lax.Precision.HIGHEST, preferred_element_type=jnp.float32,
        )

    def set_ridge(t, f):
        ghin[...] = jnp.zeros(ghin.shape, jnp.float32)
        for c in range(3):
            i = 3 * f + c
            ghin[c : c + 1, :fy] = fn[t, 0, i, fz - 1 : fz, :] + fn[t, 1, i, fz - 1 : fz, :]
        ridge = dot(ghin[0:8, :fy], pairs)
        for c in range(3):
            cn[t, 3 * f + c, cz : cz + 8, :] = jnp.broadcast_to(ridge[c : c + 1], (8, cy))

    jown[...] = jnp.ones(jown.shape, jnp.float32)
    jown[0:2, :] = 1.0 + topo[...].astype(jnp.float32) * (1.0 / 1024.0)
    for f in range(2):
        for i in range(3 * f, 3 * f + 3):
            cn[0, i, 0:cz, :] = cnow[i]
            for x in range(2):
                for y in range(tiles):
                    fn[0, x, i, :, y * LANES : (y + 1) * LANES] = fnow[
                        i, pl.ds(2 * y + x, fz, stride=2 * tiles), :
                    ]
        set_ridge(0, f)
    count = sum(h.astype(jnp.int32) for h in has_x + has_y)
    pl.semaphore_wait(barrier, count)
    each(has_x, lambda d: j_copy(d, 1 - d).start())
    send_x(0, 0)

    def pack(t):
        for d in range(2):
            base = HALF * (1 - d)
            at = (0, fy - 1)[d]
            fine = jnp.zeros((fz, LANES), jnp.float32)
            for i in range(6):
                for x in range(2):
                    fine = jnp.where(lane_f == base + 2 * i + x, fn[t, x, i, :, at : at + 1], fine)
            if t == 0:
                for x in range(2):
                    fine = jnp.where(
                        lane_f == base + 12 + x, jown[x : x + 1, at : at + 1], fine
                    )
            coarse = jnp.zeros((rows_c, LANES), jnp.float32)
            at = (0, cy - 1)[d]
            for i in range(6):
                coarse = jnp.where(lane_c == base + i, cn[t, i, :, at : at + 1], coarse)
            pk[t, d, 0:fz, :] = fine
            pk[t, d, fz : fz + rows_c, :] = coarse

    def exchange_columns(t):
        pack(t)
        each(has_y, lambda d: y_copy(t, d, 1 - d).start())
        each(has_y, lambda d: y_copy(t, d, d).wait_recv())
        low = lax.broadcasted_iota(jnp.int32, mg.shape[1:], 1) < HALF
        mg[t] = jnp.where(low, yr[t, 0], yr[t, 1])
        each(has_x, lambda d: g_copy(t, d, 1 - d).start())

    exchange_columns(0)
    send_x(0, 1)

    def halo_tile(v, k, lane):
        return jnp.where(
            lane == 0,
            v[:, HALF + k : HALF + k + 1],
            jnp.where(lane == LANES - 1, v[:, k : k + 1], 0.0),
        )

    each(has_x, lambda d: j_copy(d, d).wait_recv())
    lane_1 = lax.broadcasted_iota(jnp.int32, (1, LANES), 1)
    half_inv, inv_sq = {}, {}
    for q in range(4):
        if q in (0, 3):
            row = jx[0, 1:2, :] if q == 0 else jx[1, 0:1, :]
            edge = jnp.ones((1, LANES), jnp.float32)
        else:
            row = jown[q - 1 : q, :]
            head = mg[0, 0:8, :][0:1]
            edge = halo_tile(head, 12 + q - 1, lane_1)
            edge = jnp.where(edge == 0.0, 1.0, edge)
        row = jnp.concatenate([row, edge], axis=1)
        half_inv[q] = 0.5 / row
        inv_sq[q] = 1.0 / (row * row)
    half_c = {q: jnp.full((1, cy + LANES), 0.25, jnp.float32) for q in range(3)}
    sq_c = {q: jnp.full((1, cy + LANES), 0.25, jnp.float32) for q in range(3)}

    lane_g = lax.broadcasted_iota(jnp.int32, (16, fy + LANES), 1)
    row_g = lax.broadcasted_iota(jnp.int32, (16, fy + LANES), 0)
    keep = (lane_g < fy)
    keep = keep | ((lane_g == fy) & has_y[1]) | ((lane_g == fy + LANES - 1) & has_y[0])
    keep = keep & ((row_g >= 3) | has_x[0]) & ((row_g < 9) | has_x[1])

    for t in range(STEPS):
        for f in range(2):
            if t > 0 and f == 0:
                exchange_columns(t)
                send_x(t, 1)

            def coarse_in(d):
                x_wait_copies(t, f, d)[0].wait_recv()
                if f == 0:
                    g_copy(t, d, d).wait_recv()

            each(has_x, coarse_in)
            for q in range(3):
                cols = mg.at[t] if q == 1 else xg.at[t, q // 2]
                cols = cols[fz : fz + rows_c, :]
                for c in range(3):
                    i = 3 * f + c
                    plane = cn[t, i] if q == 1 else xc[t, q // 2, i]
                    whole = jnp.concatenate([plane, halo_tile(cols, i, lane_c)], axis=1)
                    extc[q, c, TOP : TOP + cz, :] = whole[0:cz]
                    extc[q, c, TOP - 1 : TOP, :] = whole[cz : cz + 1]
                    extc[q, c, TOP + cz : TOP + cz + 1, :] = jnp.zeros((1, cy + LANES), jnp.float32)
            laplace, grad_div = stencil(extc, 1, cz, cy, 2.0, half_c, sq_c)
            for c in range(3):
                i = 3 * f + c
                before = cold[i] if t == 0 else cn[t - 1, i, 0:cz, :]
                mu = shc[...]
                new = 2.0 * cn[t, i, 0:cz, :] - before + STEP_SQUARED * (
                    mu * laplace[c] + (lac[...] + mu) * grad_div[c]
                )
                if t < STEPS - 1:
                    cn[t + 1, i, 0:cz, :] = new
                else:
                    cout[i] = new

            ghin[...] = jnp.zeros(ghin.shape, jnp.float32)
            for c in range(3):
                low, mid, high = (extc[q, c, TOP : TOP + 1, :] for q in range(3))
                quads = (
                    0.75 * low + 0.25 * mid,
                    0.75 * mid + 0.25 * low,
                    0.75 * mid + 0.25 * high,
                    0.75 * high + 0.25 * mid,
                )
                for q in range(4):
                    ghin[3 * q + c : 3 * q + c + 1, : cy + LANES] = quads[q]
            ghost[...] = jnp.where(keep, dot(ghin[:, : cy + LANES], spread), 0.0)

            each(has_x, lambda d: x_wait_copies(t, f, d)[1].wait_recv())
            for q in range(4):
                cols = xg[t, q // 3, 0:fz, :] if q in (0, 3) else mg[t, 0:fz, :]
                x = (1, 0, 1, 0)[q]
                for c in range(3):
                    i = 3 * f + c
                    plane = xf[t, q // 3, i] if q in (0, 3) else fn[t, x, i]
                    whole = jnp.concatenate([plane, halo_tile(cols, 2 * i + x, lane_f)], axis=1)
                    ext[q, c, TOP : TOP + fz, :] = whole
                    ext[q, c, TOP - 1 : TOP, :] = whole[0:1]
                    ext[q, c, TOP + fz : TOP + fz + 1, :] = ghost[3 * q + c : 3 * q + c + 1, :]
            for x in range(2):
                laplace, grad_div = stencil(ext, x + 1, fz, fy, 1.0, half_inv, inv_sq)
                picks = [pl.ds(2 * y + x, fz, stride=2 * tiles) for y in range(tiles)]

                def fetch(*at):
                    return jnp.concatenate([at[0][at[1:] + (p, slice(None))] for p in picks], axis=1)

                mu = fetch(shf)
                both = fetch(laf) + mu
                for c in range(3):
                    i = 3 * f + c
                    before = fetch(fold, i) if t == 0 else fn[t - 1, x, i]
                    new = 2.0 * fn[t, x, i] - before + STEP_SQUARED * (
                        mu * laplace[c] + both * grad_div[c]
                    )
                    fn[t + 1, x, i] = new
                    if t == STEPS - 1:
                        for y in range(tiles):
                            fout[i, picks[y], :] = new[:, y * LANES : (y + 1) * LANES]
            if t < STEPS - 1:
                set_ridge(t + 1, f)
                if f == 0:
                    send_x(t + 1, 0)

        def later(i):
            return cn[t + 1, i, 0:cz, :] if t < STEPS - 1 else cout[i]

        prod = later(0) * later(3) + later(1) * later(4) + later(2) * later(5)
        cker[...] = prod if t == 0 else cker[...] + prod
        for x in range(2):
            prod = sum(fn[t + 1, x, c] * fn[t + 1, x, c + 3] for c in range(3))
            for y in range(tiles):
                piece = prod[:, y * LANES : (y + 1) * LANES]
                pick = pl.ds(2 * y + x, fz, stride=2 * tiles)
                fker[pick, :] = piece if t == 0 else fker[pick, :] + piece

    def finish_x(d):
        j_copy(d, d).wait_send()
        for t in range(STEPS):
            g_copy(t, d, d).wait_send()
            for f in range(2):
                for copy in x_wait_copies(t, f, d):
                    copy.wait_send()

    def finish_y(d):
        for t in range(STEPS):
            y_copy(t, d, d).wait_send()

    each(has_x, finish_x)
    each(has_y, finish_y)


def rows_view(a):
    lead = a.shape[:-3]
    fz, fx, fy = a.shape[-3:]
    n = len(lead)
    a = a.reshape(lead + (fz, fx, fy // LANES, LANES))
    a = a.transpose(tuple(range(n)) + (n, n + 2, n + 1, n + 3))
    return a.reshape(((6,) if lead else ()) + (fz * fx * fy // LANES, LANES))


def rows_back(a, shape):
    lead = shape[:-3]
    fz, fx, fy = shape[-3:]
    n = len(lead)
    a = a.reshape(lead + (fz, fy // LANES, fx, LANES))
    a = a.transpose(tuple(range(n)) + (n, n + 2, n + 1, n + 3))
    return a.reshape(shape)


def on_device(fold, fnow, cold, cnow, shf, laf, shc, lac, topo):
    nx, ny = lax.axis_size("gx"), lax.axis_size("gy")
    fz, fx, fy = shf.shape
    cz, cx, cy = shc.shape
    if fx != 2 or cx != 1 or cy != LANES or fy != 2 * cy:
        raise ValueError("unsupported tile")
    rows_c = cz + 8
    f32 = jnp.float32
    dma = pltpu.SemaphoreType.DMA
    nrows = fz * fx * fy // LANES
    vm = pl.BlockSpec(memory_space=pltpu.VMEM)
    fout, cout, fker, cker = pl.pallas_call(
        functools.partial(body, nx, ny, fz, cz, fy, cy),
        out_shape=(
            pltpu.VMEM((6, nrows, LANES), f32),
            pltpu.VMEM((6, cz, cy), f32),
            pltpu.VMEM((nrows, LANES), f32),
            pltpu.VMEM((cz, cy), f32),
        ),
        in_specs=[vm] * 9,
        out_specs=(vm,) * 4,
        scratch_shapes=[
            pltpu.VMEM((STEPS + 1, 2, 6, fz, fy), f32),
            pltpu.VMEM((STEPS, 6, rows_c, cy), f32),
            pltpu.VMEM((STEPS, 2, 6, fz, fy), f32),
            pltpu.VMEM((STEPS, 2, 6, rows_c, cy), f32),
            pltpu.VMEM((STEPS, 2, fz + rows_c, LANES), f32),
            pltpu.VMEM((STEPS, 2, fz + rows_c, LANES), f32),
            pltpu.VMEM((STEPS, 2, fz + rows_c, LANES), f32),
            pltpu.VMEM((STEPS, fz + rows_c, LANES), f32),
            pltpu.VMEM((8, fy), f32),
            pltpu.VMEM((2, 8, fy), f32),
            pltpu.VMEM((4, 3, fz + 16, fy + LANES), f32),
            pltpu.VMEM((3, 3, cz + 16, cy + LANES), f32),
            pltpu.VMEM((16, max(fy, cy + LANES)), f32),
            pltpu.VMEM((16, fy + LANES), f32),
            dma((STEPS, 2, 2, 2)),
            dma((STEPS, 2, 2, 2)),
            dma((STEPS, 2)),
            dma((STEPS, 2)),
            dma((STEPS, 2)),
            dma((STEPS, 2)),
            dma((2,)),
            dma((2,)),
        ],
        compiler_params=pltpu.CompilerParams(collective_id=0, has_side_effects=True, vmem_limit_bytes=32 << 20),
        name="wave",
    )(*[pltpu.with_memory_space_constraint(a, pltpu.HBM) for a in (
        rows_view(fold),
        rows_view(fnow),
        cold.reshape(6, cz, cy),
        cnow.reshape(6, cz, cy),
        rows_view(shf),
        rows_view(laf),
        shc.reshape(cz, cy),
        lac.reshape(cz, cy),
        topo,
    )])
    def copy_body(*refs):
        ins, outs, sem = refs[:4], refs[4:8], refs[8]
        cs = [pltpu.make_async_copy(a, b, sem.at[i]) for i, (a, b) in enumerate(zip(ins, outs))]
        for c in cs:
            c.start()
        for c in cs:
            c.wait()

    fout, cout, fker, cker = pl.pallas_call(
        copy_body,
        out_shape=tuple(jax.ShapeDtypeStruct(a.shape, f32) for a in (fout, cout, fker, cker)),
        in_specs=[vm] * 4,
        out_specs=(pl.BlockSpec(memory_space=pl.ANY),) * 4,
        scratch_shapes=[dma((4,))],
        name="put",
        compiler_params=pltpu.CompilerParams(vmem_limit_bytes=1 << 20),
    )(*[pltpu.with_memory_space_constraint(a, pltpu.VMEM) for a in (fout, cout, fker, cker)])
    return (
        rows_back(fout, fold.shape),
        cout.reshape(cold.shape),
        rows_back(fker, shf.shape),
        cker.reshape(shc.shape),
    )


def solution(mesh):
    field, coef = P(None, None, None, "gx", "gy"), P(None, "gx", "gy")
    return jax.shard_map(
        on_device,
        mesh=mesh,
        in_specs=(field,) * 4 + (coef,) * 4 + (P("gx", "gy"),),
        out_specs=(field, field, coef, coef),
        check_vma=False,
    )
```

```python
import functools

import jax
import jax.numpy as jnp
from jax import lax
from jax.experimental import pallas as pl
from jax.experimental.pallas import tpu as pltpu
from jax.sharding import PartitionSpec as P

STEPS = 2
STEP_SQUARED = 0.04
LANES = 128
TOP = 8


def body(
    nx, ny, fz, cz,
    fold, fnow, cold, cnow, shf, laf, shc, lac, topo,
    fout, cout, fker, cker,
    fin, fo, co, sf, lf, sc, lc, tp,
    fn, cn, xf, xc, jm, jx, pk, yr, xk,
    rj, rj2, rjh, rjl, qs, gt, tt, gs, cor,
    ins, xs, xr, js, jr, ys, yrs,
):
    f32 = jnp.float32
    gx, gy = lax.axis_index("gx"), lax.axis_index("gy")
    has_x = (gx > 0, gx < nx - 1)
    has_y = (gy > 0, gy < ny - 1)
    rows_c = cz + 8
    rows_f = fz + 8
    low_c, low_f = TOP + cz, TOP + fz

    def each(flags, action):
        for d in range(2):
            pl.when(flags[d])(functools.partial(action, d))

    def half(f):
        return pl.ds(3 * f, 3)

    loads = {
        "f0": (fnow.at[half(0)], fin.at[half(0)]),
        "c0": (cnow.at[half(0)], cn.at[0, half(0), pl.ds(TOP, cz)]),
        "topo": (topo, tp),
        "f1": (fnow.at[half(1)], fin.at[half(1)]),
        "c1": (cnow.at[half(1)], cn.at[0, half(1), pl.ds(TOP, cz)]),
        "co": (cold, co),
        "sc": (shc, sc),
        "lc": (lac, lc),
        "fo": (fold, fo),
        "sf": (shf, sf),
        "lf": (laf, lf),
    }
    loads = {
        k: pltpu.make_async_copy(a, b, ins.at[n]) for n, (k, (a, b)) in enumerate(loads.items())
    }
    for copy in loads.values():
        copy.start()

    barrier = pltpu.get_barrier_semaphore()
    each(has_x, lambda d: pl.semaphore_signal(barrier, inc=1, device_id={"gx": gx + 2 * d - 1}))
    each(has_y, lambda d: pl.semaphore_signal(barrier, inc=1, device_id={"gy": gy + 2 * d - 1}))

    def x_copy(t, f, kind, d, land):
        if kind == 0:
            rows = pl.ds(TOP - 1, cz + 1)
            src, dst = cn.at[t, half(f), rows], xc.at[t, land, half(f), rows]
        elif kind == 1:
            rows = pl.ds(TOP, fz)
            src, dst = fn.at[t, d, half(f), :, rows], xf.at[t, land, half(f), :, rows]
        else:
            src, dst = yr.at[t, f, :, pl.ds(8 * d, 8)], xk.at[t, f, land]
        return pltpu.make_async_remote_copy(
            src, dst, xs.at[t, f, kind, d], xr.at[t, f, kind, land],
            device_id={"gx": gx + 2 * d - 1},
        )

    def y_copy(t, f, d, land):
        return pltpu.make_async_remote_copy(
            pk.at[t, f, pl.ds(16 * d, 16)], yr.at[t, f, land], ys.at[t, f, d], yrs.at[t, f, land],
            device_id={"gy": gy + 2 * d - 1},
        )

    def j_copy(d, land):
        return pltpu.make_async_remote_copy(
            jm.at[d], jx.at[land], js.at[d], jr.at[land], device_id={"gx": gx + 2 * d - 1}
        )

    def x_send(t, f, *kinds):
        def go(d):
            for kind in kinds:
                x_copy(t, f, kind, d, 1 - d).start()

        each(has_x, go)

    def x_wait(t, f, kind):
        each(has_x, lambda d: x_copy(t, f, kind, d, d).wait_recv())

    def y_send(t, f):
        each(has_y, lambda d: y_copy(t, f, d, 1 - d).start())

    def y_wait(t, f):
        each(has_y, lambda d: y_copy(t, f, d, d).wait_recv())

    lane = lax.broadcasted_iota(jnp.int32, (8, LANES), 1)
    sub = lax.broadcasted_iota(jnp.int32, (8, LANES), 0)
    first, last = lane == 0, lane == LANES - 1
    left = lane < LANES // 2
    even = lane - 2 * (lane // 2) == 0
    pair_of = lane * 2 - jnp.where(left, 0, LANES)
    half_of = (lane // 2, lane // 2 + LANES // 2)
    y_edge = (first & has_y[0]) | (last & has_y[1])

    def north(v):
        return pltpu.roll(v, LANES - 1, 1)

    def south(v):
        return pltpu.roll(v, 1, 1)

    def take(v, index):
        return jnp.take_along_axis(v, index, axis=1, mode="promise_in_bounds")

    def spread(v, at, rows):
        return jnp.broadcast_to(v[:, at : at + 1], (rows, LANES))

    for t in range(STEPS):
        for i in range(6):
            row = jnp.zeros((1, LANES), f32)
            cn[t, i, low_c : low_c + 1, :] = row
            xc[t, 0, i, low_c : low_c + 1, :] = row
            xc[t, 1, i, low_c : low_c + 1, :] = row
    cor[...] = jnp.zeros(cor.shape, f32)
    gt[...] = jnp.zeros(gt.shape, f32)
    qs[...] = jnp.zeros(qs.shape, f32)
    gs[...] = jnp.zeros(gs.shape, f32)
    jm[...] = jnp.ones(jm.shape, f32)
    for d in range(2):

        @pl.when(jnp.logical_not(has_x[d]))
        def _():
            for t in range(STEPS):
                xf[t, d] = jnp.zeros(xf.shape[2:], f32)
                xc[t, d] = jnp.zeros(xc.shape[2:], f32)
                for f in range(2):
                    xk[t, f, d] = jnp.zeros(xk.shape[3:], f32)
            jx[d] = jnp.ones(jx.shape[1:], f32)

        @pl.when(jnp.logical_not(has_y[d]))
        def _():
            for t in range(STEPS):
                for f in range(2):
                    yr[t, f, d] = jnp.zeros(yr.shape[3:], f32)

    def ridge(t, f):
        for c in range(3):
            i = 3 * f + c
            for y in range(2):
                gs[y, c : c + 1] = (
                    fn[t, 0, i, y, low_f - 1 : low_f, :] + fn[t, 1, i, y, low_f - 1 : low_f, :]
                )
        a, b = gs[0], gs[1]
        a, b = take(a + north(a), pair_of), take(b + north(b), pair_of)
        mean = 0.25 * jnp.where(left, a, b)
        for c in range(3):
            cn[t, 3 * f + c, TOP - 1 : TOP, :] = mean[c : c + 1]

    def copy_top(t, x, i):
        for y in range(2):
            fn[t, x, i, y, TOP - 1 : TOP, :] = fn[t, x, i, y, TOP : TOP + 1, :]

    def pack(t, f):
        wide = lax.broadcasted_iota(jnp.int32, (rows_c, LANES), 1)
        thin = lax.broadcasted_iota(jnp.int32, (rows_f, LANES), 1)
        out = jnp.zeros((rows_c, LANES), f32)
        fine = jnp.zeros((rows_f, LANES), f32)
        for d in range(2):
            at = (0, LANES - 1)[d]
            for c in range(3):
                i, j = 3 * f + c, 16 * d + 3 + c
                v = spread(cn[t, i, TOP - 1 : TOP - 1 + rows_c, :], at, rows_c)
                out = jnp.where((wide == j) | (wide == j + 8), v, out)
                for x in range(2):
                    v = spread(fn[t, x, i, d, TOP - 1 : TOP - 1 + rows_f, :], at, rows_f)
                    fine = jnp.where(thin == 16 * d + 8 * x + c, v, fine)
            if t == 0 and f == 0:
                for x in range(2):
                    v = jnp.broadcast_to(jm[x, d : d + 1, at : at + 1], (rows_f, LANES))
                    fine = jnp.where(thin == 16 * d + 8 * x + 6, v, fine)
        of_fine = thin - 8 * (thin // 8)
        of_fine = (of_fine < 3) | (of_fine == 6)
        qs[0:rows_f, :] = jnp.where(of_fine, fine, out[0:rows_f])
        qs[rows_f:rows_c, :] = out[rows_f:]
        pk[t, f] = jnp.transpose(qs[...])[0:32]

    def begin(f):
        loads["f%d" % f].wait()
        for c in range(3):
            i = 3 * f + c
            for x in range(2):
                for y in range(2):
                    fn[0, x, i, y, TOP : TOP + fz, :] = fin[i, pl.ds(2 * y + x, fz, stride=4), :]
                copy_top(0, x, i)
        ridge(0, f)
        loads["c%d" % f].wait()

    begin(0)
    loads["topo"].wait()
    for x in range(2):
        for y in range(2):
            jm[x, y : y + 1] = 1.0 + tp[x : x + 1, y * LANES : (y + 1) * LANES].astype(f32) * (1.0 / 1024.0)
    count = sum(h.astype(jnp.int32) for h in has_x + has_y)
    pl.semaphore_wait(barrier, count)
    each(has_x, lambda d: j_copy(d, 1 - d).start())
    x_send(0, 0, 0, 1)
    pack(0, 0)
    y_send(0, 0)
    begin(1)
    pack(0, 1)
    y_send(0, 1)
    y_wait(0, 0)
    x_send(0, 0, 2)
    x_send(0, 1, 0, 1)
    y_wait(0, 1)
    x_send(0, 1, 2)

    each(has_x, lambda d: j_copy(d, d).wait_recv())
    for q in range(4):
        for y in range(2):
            row = jx[q // 3, y : y + 1] if q in (0, 3) else jm[q - 1, y : y + 1]
            inv = jnp.broadcast_to(1.0 / row, (8, LANES))
            rj[q, y] = inv
            if q in (1, 2):
                rj2[q - 1, y] = inv * inv
    for x in range(2):
        sides = []
        for s in range(2):
            row = yr[0, 0, s, 8 * x + 6 : 8 * x + 7, 0:1]
            row = jnp.broadcast_to(1.0 / jnp.where(row == 0.0, 1.0, row), (8, LANES))
            rjh[s, x] = row
            sides.append(row)
        rjl[x] = jnp.where(left, sides[0], sides[1])

    def halos(t, f):
        inside = lane <= fz
        for s in range(2):
            own = [yr[t, f, s, 8 * x : 8 * x + 8] for x in range(2)]
            west, east = xk[t, f, 0, s], xk[t, f, 1, s]
            cross = (own[1] - west, east - own[0], east - west)

            def put(k, row):
                at = 2 * k + 1 - s
                gt[at : at + 1, :] = row

            d = north(own[0]) - south(own[0])
            for c in range(3):
                put(c, own[0][3 + c : 4 + c])
            put(3, cross[2][4:5])
            put(4, cross[2][3:4] + d[5:6])
            put(5, d[4:5])
            for x in range(2):
                v = jnp.where(inside, own[x], 0.0)
                d = (north(v) - south(v)) * rjh[s, x]
                k = 6 + 6 * x
                for c in range(3):
                    put(k + c, own[x][c : c + 1])
                put(k + 3, cross[x][1:2])
                put(k + 4, cross[x][0:1] + d[2:3])
                put(k + 5, d[1:2])
        tt[...] = jnp.transpose(gt[...])

    def item(v, k):
        return pltpu.roll(v, LANES - 1 - 2 * k, 1)

    def coarse(t, f):
        for v in range(cz // 8):
            r = TOP + 8 * v
            th = tt[8 * v + 1 : 8 * v + 9, :]
            mu = (0.25 * STEP_SQUARED) * sc[8 * v : 8 * v + 8, :]
            both = (0.25 * STEP_SQUARED) * lc[8 * v : 8 * v + 8, :] + mu
            xx, yy, zz, cross, rise, tilt, twice = [], [], [], [], [], [], []
            for c in range(3):
                i = 3 * f + c
                u = cn[t, i, r : r + 8, :]
                e, w = xc[t, 1, i, r : r + 8, :], xc[t, 0, i, r : r + 8, :]
                dn, up = cn[t, i, r + 1 : r + 9, :], cn[t, i, r - 1 : r + 7, :]
                h = item(th, c)
                u2 = 2.0 * u
                twice.append(u2)
                xx.append(e + w - u2)
                yy.append(jnp.where(last, h, north(u)) + jnp.where(first, h, south(u)) - u2)
                zz.append(dn + up - u2)
                cross.append(e - w)
                rise.append(dn - up)
                if c == 1:
                    tilt.append(None)
                else:
                    ed, eu = xc[t, 1, i, r + 1 : r + 9, :], xc[t, 1, i, r - 1 : r + 7, :]
                    wd, wu = xc[t, 0, i, r + 1 : r + 9, :], xc[t, 0, i, r - 1 : r + 7, :]
                    tilt.append((ed - eu) - (wd - wu))
            ac = []
            for k, a in enumerate((cross[1], cross[0] + rise[2], rise[1])):
                h = item(th, 3 + k)
                ac.append(jnp.where(last, h, north(a)) - jnp.where(first, h, south(a)))
            grad = (
                xx[0] + 0.25 * (ac[0] + tilt[2]),
                yy[1] + 0.25 * ac[1],
                zz[2] + 0.25 * (ac[2] + tilt[0]),
            )
            prod = None
            for c in range(3):
                i = 3 * f + c
                before = co[i, 8 * v : 8 * v + 8, :] if t == 0 else cn[t - 1, i, r : r + 8, :]
                new = (twice[c] - before) + (mu * (xx[c] + yy[c] + zz[c]) + both * grad[c])
                if t < STEPS - 1:
                    cn[t + 1, i, r : r + 8, :] = new
                else:
                    cout[i, 8 * v : 8 * v + 8, :] = new
                if f == 1:
                    if t < STEPS - 1:
                        pair = cn[t + 1, c, r : r + 8, :]
                    else:
                        pair = cout[c, 8 * v : 8 * v + 8, :]
                    prod = pair * new if prod is None else prod + pair * new
            if f == 1:
                if t > 0:
                    prod = prod + cker[8 * v : 8 * v + 8, :]
                cker[8 * v : 8 * v + 8, :] = prod

    def ghost(t, f):
        for c in range(3):
            i = 3 * f + c
            gs[0, 3 + c : 4 + c] = xc[t, 0, i, TOP : TOP + 1, :]
            gs[1, 3 + c : 4 + c] = cn[t, i, TOP : TOP + 1, :]
            gs[2, 3 + c : 4 + c] = xc[t, 1, i, TOP : TOP + 1, :]
        flat = [gs[k] for k in range(3)]
        rim = []
        for tiles in (
            [xk[t, f, 0, s] for s in range(2)],
            [yr[t, f, s, 0:8] for s in range(2)],
            [xk[t, f, 1, s] for s in range(2)],
        ):
            rim.append(jnp.where(left, spread(tiles[0], 1, 8), spread(tiles[1], 1, 8)))

        def mix(v):
            lo, mid, hi = v
            return (
                0.75 * lo + 0.25 * mid,
                0.75 * mid + 0.25 * lo,
                0.75 * mid + 0.25 * hi,
                0.75 * hi + 0.25 * mid,
            )

        for q, (v, h) in enumerate(zip(mix(flat), mix(rim))):
            a = 0.75 * v + 0.25 * jnp.where(first, h, south(v))
            b = 0.75 * v + 0.25 * jnp.where(last, h, north(v))
            for y in range(2):
                g = jnp.where(even, take(a, half_of[y]), take(b, half_of[y]))
                if q in (0, 3):
                    g = jnp.where(has_x[q // 3], g, 0.0)
                for c in range(3):
                    i = 3 * f + c
                    if q in (0, 3):
                        xf[t, q // 3, i, y, low_f : low_f + 1, :] = g[3 + c : 4 + c]
                    else:
                        fn[t, q - 1, i, y, low_f : low_f + 1, :] = g[3 + c : 4 + c]
            if q in (1, 2):
                g = jnp.where(y_edge, 0.75 * h + 0.25 * v, 0.0) * rjl[q - 1]
                cor[q - 1, 0, 7:8] = g[5:6]
                cor[q - 1, 1, 7:8] = g[4:5]

    def fine(t, f):
        for side in range(2):
            for c in (0, 2):
                for y in range(2):
                    xf[t, side, 3 * f + c, y, TOP - 1 : TOP, :] = xf[
                        t, side, 3 * f + c, y, TOP : TOP + 1, :
                    ]

        def plane(q, i, y, r):
            if q in (0, 3):
                return xf[t, q // 3, i, y, r : r + 8, :]
            return fn[t, q - 1, i, y, r : r + 8, :]

        for v in range(fz // 8):
            r = TOP + 8 * v
            th = tt[8 * v + 1 : 8 * v + 9, :]
            for x in range(2):
                q = x + 1
                xx, yy, zz, up_down, twice = {}, {}, {}, {}, {}
                va = [[None, None] for _ in range(3)]
                tilt = {}
                mid = {}
                for y in range(2):
                    inv = rj[q, y]
                    cross, rise = [], []
                    for c in range(3):
                        i = 3 * f + c
                        u = plane(q, i, y, r)
                        e, w = plane(q + 1, i, y, r), plane(q - 1, i, y, r)
                        dn, up = plane(q, i, y, r + 1), plane(q, i, y, r - 1)
                        mid[c, y] = u
                        u2 = 2.0 * u
                        twice[c, y] = u2
                        xx[c, y] = e + w - u2
                        zz[c, y] = (dn + up - u2) * rj2[x, y]
                        cross.append(e - w)
                        rise.append((dn - up) * inv if c else None)
                        if c != 1:
                            ed, eu = plane(q + 1, i, y, r + 1), plane(q + 1, i, y, r - 1)
                            wd, wu = plane(q - 1, i, y, r + 1), plane(q - 1, i, y, r - 1)
                            tilt[c, y] = (ed - eu) * rj[q + 1, y] - (wd - wu) * rj[q - 1, y]
                    va[0][y] = cross[1]
                    va[1][y] = cross[0] + rise[2]
                    va[2][y] = rise[1]

                def ends(a, b, h):
                    na, nb, sa, sb = north(a), north(b), south(a), south(b)
                    return (
                        (jnp.where(last, nb, na), jnp.where(first, h, sa)),
                        (jnp.where(last, h, nb), jnp.where(first, sa, sb)),
                    )

                k = 6 + 6 * x
                for c in range(3):
                    for y, (n, s) in enumerate(ends(mid[c, 0], mid[c, 1], item(th, k + c))):
                        yy[c, y] = n + s - twice[c, y]
                ac = {}
                for c in range(3):
                    h = item(th, k + 3 + c)
                    if c and v == fz // 8 - 1:
                        h = h + cor[x, c - 1]
                    for y, (n, s) in enumerate(ends(va[c][0], va[c][1], h)):
                        ac[c, y] = n - s
                for y in range(2):
                    pick = pl.ds(32 * v + 2 * y + x, 8, stride=4)
                    mu = STEP_SQUARED * sf[pick, :]
                    both = STEP_SQUARED * lf[pick, :] + mu
                    grad = (
                        xx[0, y] + 0.25 * (ac[0, y] + tilt[2, y]),
                        yy[1, y] + 0.25 * ac[1, y],
                        zz[2, y] + 0.25 * (ac[2, y] + tilt[0, y]),
                    )
                    prod = None
                    for c in range(3):
                        i = 3 * f + c
                        before = fo[i, pick, :] if t == 0 else fn[t - 1, x, i, y, r : r + 8, :]
                        new = (twice[c, y] - before) + (
                            mu * (xx[c, y] + yy[c, y] + zz[c, y]) + both * grad[c]
                        )
                        if t < STEPS - 1:
                            fn[t + 1, x, i, y, r : r + 8, :] = new
                        else:
                            fout[i, pick, :] = new
                        if f == 1:
                            if t < STEPS - 1:
                                pair = fn[t + 1, x, c, y, r : r + 8, :]
                            else:
                                pair = fout[c, pick, :]
                            prod = pair * new if prod is None else prod + pair * new
                    if f == 1:
                        if t > 0:
                            prod = prod + fker[pick, :]
                        fker[pick, :] = prod

    def finish_level(t, f):
        for c in range(3):
            for x in range(2):
                copy_top(t, x, 3 * f + c)
        ridge(t, f)
        x_send(t, f, 0, 1)
        pack(t, f)
        y_send(t, f)

    for t in range(STEPS):
        for f in range(2):
            x_wait(t, f, 0)
            if t == 0 and f == 0:
                for k in ("co", "sc", "lc"):
                    loads[k].wait()
            x_wait(t, f, 2)
            halos(t, f)
            coarse(t, f)
            if t > 0 and f == 0:
                y_wait(t, 1)
                x_send(t, 1, 2)
            if t < STEPS - 1 and f == 1:
                y_wait(t + 1, 0)
                x_send(t + 1, 0, 2)
            ghost(t, f)
            x_wait(t, f, 1)
            if t == 0 and f == 0:
                for k in ("fo", "sf", "lf"):
                    loads[k].wait()
            fine(t, f)
            if t < STEPS - 1:
                finish_level(t + 1, f)

    def finish_x(d):
        j_copy(d, d).wait_send()
        for t in range(STEPS):
            for f in range(2):
                for kind in range(3):
                    x_copy(t, f, kind, d, d).wait_send()

    def finish_y(d):
        for t in range(STEPS):
            for f in range(2):
                y_copy(t, f, d, d).wait_send()

    each(has_x, finish_x)
    each(has_y, finish_y)


def put_body(*refs):
    ins, outs, sem = refs[:4], refs[4:8], refs[8]
    copies = [
        pltpu.make_async_copy(a, b, sem.at[i]) for i, (a, b) in enumerate(zip(ins, outs))
    ]
    for copy in copies:
        copy.start()
    for copy in copies:
        copy.wait()


def rows_view(a):
    lead = a.shape[:-3]
    fz, fx, fy = a.shape[-3:]
    n = len(lead)
    a = a.reshape(lead + (fz, fx, fy // LANES, LANES))
    a = a.transpose(tuple(range(n)) + (n, n + 2, n + 1, n + 3))
    return a.reshape(((6,) if lead else ()) + (fz * fx * fy // LANES, LANES))


def rows_back(a, shape):
    lead = shape[:-3]
    fz, fx, fy = shape[-3:]
    n = len(lead)
    a = a.reshape(lead + (fz, fy // LANES, fx, LANES))
    a = a.transpose(tuple(range(n)) + (n, n + 2, n + 1, n + 3))
    return a.reshape(shape)


def on_device(fold, fnow, cold, cnow, shf, laf, shc, lac, topo):
    nx, ny = lax.axis_size("gx"), lax.axis_size("gy")
    fz, fx, fy = shf.shape
    cz, cx, cy = shc.shape
    if fx != 2 or cx != 1 or cy != LANES or fy != 2 * cy or fz % 8 or cz % 8 or cz + 8 > LANES:
        raise ValueError("unsupported tile")
    f32 = jnp.float32
    dma = pltpu.SemaphoreType.DMA
    nrows = fz * fx * fy // LANES
    vm = pl.BlockSpec(memory_space=pltpu.VMEM)
    hbm = pl.BlockSpec(memory_space=pl.ANY)
    shapes = ((6, nrows, LANES), (6, cz, cy), (nrows, LANES), (cz, cy))
    args = (
        rows_view(fold),
        rows_view(fnow),
        cold.reshape(6, cz, cy),
        cnow.reshape(6, cz, cy),
        rows_view(shf),
        rows_view(laf),
        shc.reshape(cz, cy),
        lac.reshape(cz, cy),
        topo,
    )
    inner = pl.pallas_call(
        functools.partial(body, nx, ny, fz, cz),
        out_shape=tuple(pltpu.VMEM(s, f32) for s in shapes),
        in_specs=[hbm] * 9,
        out_specs=(vm,) * 4,
        scratch_shapes=[
            pltpu.VMEM((6, nrows, LANES), f32),
            pltpu.VMEM((6, nrows, LANES), f32),
            pltpu.VMEM((6, cz, cy), f32),
            pltpu.VMEM((nrows, LANES), f32),
            pltpu.VMEM((nrows, LANES), f32),
            pltpu.VMEM((cz, cy), f32),
            pltpu.VMEM((cz, cy), f32),
            pltpu.VMEM((fx, fy), jnp.int32),
            pltpu.VMEM((STEPS, 2, 6, 2, fz + 16, LANES), f32),
            pltpu.VMEM((STEPS, 6, cz + 16, LANES), f32),
            pltpu.VMEM((STEPS, 2, 6, 2, fz + 16, LANES), f32),
            pltpu.VMEM((STEPS, 2, 6, cz + 16, LANES), f32),
            pltpu.VMEM((2, 8, LANES), f32),
            pltpu.VMEM((2, 8, LANES), f32),
            pltpu.VMEM((STEPS, 2, 32, LANES), f32),
            pltpu.VMEM((STEPS, 2, 2, 16, LANES), f32),
            pltpu.VMEM((STEPS, 2, 2, 2, 8, LANES), f32),
            pltpu.VMEM((4, 2, 8, LANES), f32),
            pltpu.VMEM((2, 2, 8, LANES), f32),
            pltpu.VMEM((2, 2, 8, LANES), f32),
            pltpu.VMEM((2, 8, LANES), f32),
            pltpu.VMEM((LANES, LANES), f32),
            pltpu.VMEM((LANES, LANES), f32),
            pltpu.VMEM((LANES, LANES), f32),
            pltpu.VMEM((3, 8, LANES), f32),
            pltpu.VMEM((2, 2, 8, LANES), f32),
            dma((11,)),
            dma((STEPS, 2, 3, 2)),
            dma((STEPS, 2, 3, 2)),
            dma((2,)),
            dma((2,)),
            dma((STEPS, 2, 2)),
            dma((STEPS, 2, 2)),
        ],
        compiler_params=pltpu.CompilerParams(
            collective_id=0, has_side_effects=True, vmem_limit_bytes=32 << 20
        ),
        name="wave",
    )(*[pltpu.with_memory_space_constraint(a, pltpu.HBM) for a in args])
    fout, cout, fker, cker = pl.pallas_call(
        put_body,
        out_shape=tuple(jax.ShapeDtypeStruct(s, f32) for s in shapes),
        in_specs=[vm] * 4,
        out_specs=(hbm,) * 4,
        scratch_shapes=[dma((4,))],
        compiler_params=pltpu.CompilerParams(vmem_limit_bytes=1 << 20),
        name="put",
    )(*[pltpu.with_memory_space_constraint(a, pltpu.VMEM) for a in inner])
    return (
        rows_back(fout, fold.shape),
        cout.reshape(cold.shape),
        rows_back(fker, shf.shape),
        cker.reshape(shc.shape),
    )


def solution(mesh):
    field, coef = P(None, None, None, "gx", "gy"), P(None, "gx", "gy")
    return jax.shard_map(
        on_device,
        mesh=mesh,
        in_specs=(field,) * 4 + (coef,) * 4 + (P("gx", "gy"),),
        out_specs=(field, field, coef, coef),
        check_vma=False,
    )
```

```python
import functools

import jax
import jax.numpy as jnp
from jax import lax
from jax.experimental import pallas as pl
from jax.experimental.pallas import tpu as pltpu
from jax.sharding import PartitionSpec as P

STEPS = 2
STEP_SQUARED = 0.04
LANES = 128
TOP = 8


def body(
    nx, ny, fz, cz,
    fold, fnow, cold, cnow, shf, laf, shc, lac, topo,
    fout, cout, fker, cker,
    fin, fo, co, sf, lf, sc, lc, tp,
    fn, cn, xf, xc, jm, jx, pk, yr, xk,
    rj, rj2, rjh, rjl, qs, gt, tt, gs, cor, span, via_f, via_c,
    ins, xs, xr, jr, ys, yrs, vs, vr,
):
    f32 = jnp.float32
    gx, gy = lax.axis_index("gx"), lax.axis_index("gy")
    has_x = (gx > 0, gx < nx - 1)
    has_y = (gy > 0, gy < ny - 1)
    rows_c = cz + 8
    rows_f = fz + 8
    low_c, low_f = TOP + cz, TOP + fz

    def each(flags, action):
        for d in range(2):
            pl.when(flags[d])(functools.partial(action, d))

    def half(f):
        return pl.ds(3 * f, 3)

    loads = {
        "f0": (fnow.at[half(0)], fin.at[half(0)]),
        "c0": (cnow.at[half(0)], cn.at[0, half(0), pl.ds(TOP, cz)]),
        "topo": (topo, tp),
        "f1": (fnow.at[half(1)], fin.at[half(1)]),
        "c1": (cnow.at[half(1)], cn.at[0, half(1), pl.ds(TOP, cz)]),
        "co": (cold, co),
        "sc": (shc, sc),
        "lc": (lac, lc),
        "fo": (fold, fo),
        "sf": (shf, sf),
        "lf": (laf, lf),
    }
    slots = {"f0": 0, "c0": 1, "topo": 2, "f1": 3, "c1": 4, "co": 5, "sc": 5, "lc": 5}
    loads = {
        k: pltpu.make_async_copy(a, b, ins.at[slots.get(k, 6)]) for k, (a, b) in loads.items()
    }
    for copy in loads.values():
        copy.start()

    def drain(sem, rows):
        part = span.at[pl.ds(0, rows)]
        pltpu.make_async_copy(part, part, sem).wait()

    planes = nx // 4 if nx % 4 == 0 else 0
    share = [min(3, (8 * (planes - 1 - z) + planes) // (2 * planes)) for z in range(planes - 1)]
    route = [{1: 3, 2: 2, 3: 1}, {0: 2, 1: 1, 2: 3}]
    reach = [{m: sum(n >= least for n in share) for m, least in r.items()} for r in route]
    at4, plane = lax.rem(gx, 4), gx // 4
    rank = jnp.where((at4 == 1) | (at4 == 3), plane, planes - 1 - plane)
    outer = ((at4 == 0), (at4 == 3))
    middle = (at4 == 1) | (at4 == 2)
    detour = [{(m, d): outer[d] & (rank < r[m]) for m in r for d in range(2)} for r in reach]
    passes = [{m: middle & (rank < r[m]) for m in r} for r in reach]
    from_left = at4 == 2
    even_x = lax.rem(gx, 2) == 0

    barrier = pltpu.get_barrier_semaphore()
    each(has_x, lambda d: pl.semaphore_signal(barrier, inc=1, device_id={"gx": gx + 2 * d - 1}))
    each(has_y, lambda d: pl.semaphore_signal(barrier, inc=1, device_id={"gy": gy + 2 * d - 1}))

    @pl.when(middle & (rank < len(share)))
    def _():
        source = gx + jnp.where(from_left, -2, 2)
        pl.semaphore_signal(barrier, inc=1, device_id={"gx": source})

    def x_copy(t, f, kind, d, land):
        if kind == 0:
            rows = pl.ds(TOP - 1, cz + 1)
            src, dst = cn.at[t, half(f), rows], xc.at[t, land, half(f), rows]
        elif kind == 1:
            rows = pl.ds(TOP, fz)
            src, dst = fn.at[t, d, half(f), :, rows], xf.at[t, land, half(f), :, rows]
        else:
            src, dst = yr.at[t, f, :, pl.ds(8 * d, 8)], xk.at[t, f, land]
        return pltpu.make_async_remote_copy(
            src, dst, xs.at[d], xr.at[t, f, kind, land], device_id={"gx": gx + 2 * d - 1}
        )

    def stop(t, m):
        if m - 2 * (m // 2) == 1:
            return via_f.at[t, m // 2]
        return via_c.at[t, m // 2, :, pl.ds(0, cz + 1)]

    def detour_copy(t, f, kind, d):
        m = 2 * f + kind
        if kind == 0:
            src = cn.at[t, half(f), pl.ds(TOP - 1, cz + 1)]
        else:
            src = fn.at[t, d, half(f), :, pl.ds(TOP, fz)]
        return pltpu.make_async_remote_copy(
            src, stop(t, m), xs.at[d], vr.at[t, m], device_id={"gx": gx + 2 - 4 * d}
        )

    def pass_copy(t, m, land):
        f, kind = m // 2, m - 2 * (m // 2)
        if kind == 0:
            dst = xc.at[t, land, half(f), pl.ds(TOP - 1, cz + 1)]
        else:
            dst = xf.at[t, land, half(f), :, pl.ds(TOP, fz)]
        return pltpu.make_async_remote_copy(
            stop(t, m), dst, vs.at[t, m], xr.at[t, f, kind, land],
            device_id={"gx": gx + 3 - 6 * land},
        )

    def pass_on(t, m):
        @pl.when(passes[t][m])
        def _():
            part = stop(t, m)
            pltpu.make_async_copy(part, part, vr.at[t, m]).wait()
            for land in range(2):
                pl.when((at4 == 1 + land))(pass_copy(t, m, land).start)

    def y_copy(t, f, d, land):
        return pltpu.make_async_remote_copy(
            pk.at[t, f, pl.ds(16 * d, 16)], yr.at[t, f, land], ys.at[d], yrs.at[t, f, land],
            device_id={"gy": gy + 2 * d - 1},
        )

    def j_copy(d, land):
        return pltpu.make_async_remote_copy(
            jm.at[d], jx.at[land], xs.at[d], jr.at[land], device_id={"gx": gx + 2 * d - 1}
        )

    def x_send(t, f, *kinds):
        def go(d):
            for kind in kinds:
                m = 2 * f + kind
                if kind == 2 or m not in route[t]:
                    x_copy(t, f, kind, d, 1 - d).start()
                else:
                    pl.when(detour[t][m, d])(detour_copy(t, f, kind, d).start)
                    pl.when(jnp.logical_not(detour[t][m, d]))(x_copy(t, f, kind, d, 1 - d).start)

        pl.when(has_x[1] & even_x)(functools.partial(go, 1))
        pl.when(has_x[0])(functools.partial(go, 0))
        pl.when(has_x[1] & jnp.logical_not(even_x))(functools.partial(go, 1))

    def x_wait(t, f, kind):
        each(has_x, lambda d: x_copy(t, f, kind, d, d).wait_recv())

    def y_send(t, f):
        each(has_y, lambda d: y_copy(t, f, d, 1 - d).start())

    def y_wait(t, f):
        each(has_y, lambda d: y_copy(t, f, d, d).wait_recv())

    lane = lax.broadcasted_iota(jnp.int32, (8, LANES), 1)
    sub = lax.broadcasted_iota(jnp.int32, (8, LANES), 0)
    first, last = lane == 0, lane == LANES - 1
    left = lane < LANES // 2
    even = lane - 2 * (lane // 2) == 0
    pair_of = lane * 2 - jnp.where(left, 0, LANES)
    half_of = (lane // 2, lane // 2 + LANES // 2)
    y_edge = (first & has_y[0]) | (last & has_y[1])

    def north(v):
        return pltpu.roll(v, LANES - 1, 1)

    def south(v):
        return pltpu.roll(v, 1, 1)

    def take(v, index):
        return jnp.take_along_axis(v, index, axis=1, mode="promise_in_bounds")

    def spread(v, at, rows):
        return jnp.broadcast_to(v[:, at : at + 1], (rows, LANES))

    for t in range(STEPS):
        for i in range(6):
            row = jnp.zeros((1, LANES), f32)
            cn[t, i, low_c : low_c + 1, :] = row
            xc[t, 0, i, low_c : low_c + 1, :] = row
            xc[t, 1, i, low_c : low_c + 1, :] = row
    cor[...] = jnp.zeros(cor.shape, f32)
    gt[...] = jnp.zeros(gt.shape, f32)
    qs[...] = jnp.zeros(qs.shape, f32)
    gs[...] = jnp.zeros(gs.shape, f32)
    jm[...] = jnp.ones(jm.shape, f32)
    for d in range(2):

        @pl.when(jnp.logical_not(has_x[d]))
        def _():
            for t in range(STEPS):
                xf[t, d] = jnp.zeros(xf.shape[2:], f32)
                xc[t, d] = jnp.zeros(xc.shape[2:], f32)
                for f in range(2):
                    xk[t, f, d] = jnp.zeros(xk.shape[3:], f32)
            jx[d] = jnp.ones(jx.shape[1:], f32)

        @pl.when(jnp.logical_not(has_y[d]))
        def _():
            for t in range(STEPS):
                for f in range(2):
                    yr[t, f, d] = jnp.zeros(yr.shape[3:], f32)

    def ridge(t, f):
        for c in range(3):
            i = 3 * f + c
            for y in range(2):
                gs[y, c : c + 1] = (
                    fn[t, 0, i, y, low_f - 1 : low_f, :] + fn[t, 1, i, y, low_f - 1 : low_f, :]
                )
        a, b = gs[0], gs[1]
        a, b = take(a + north(a), pair_of), take(b + north(b), pair_of)
        mean = 0.25 * jnp.where(left, a, b)
        for c in range(3):
            cn[t, 3 * f + c, TOP - 1 : TOP, :] = mean[c : c + 1]

    def copy_top(t, x, i):
        for y in range(2):
            fn[t, x, i, y, TOP - 1 : TOP, :] = fn[t, x, i, y, TOP : TOP + 1, :]

    def pack(t, f):
        wide = lax.broadcasted_iota(jnp.int32, (rows_c, LANES), 1)
        thin = lax.broadcasted_iota(jnp.int32, (rows_f, LANES), 1)
        out = jnp.zeros((rows_c, LANES), f32)
        fine = jnp.zeros((rows_f, LANES), f32)
        for d in range(2):
            at = (0, LANES - 1)[d]
            for c in range(3):
                i, j = 3 * f + c, 16 * d + 3 + c
                v = spread(cn[t, i, TOP - 1 : TOP - 1 + rows_c, :], at, rows_c)
                out = jnp.where((wide == j) | (wide == j + 8), v, out)
                for x in range(2):
                    v = spread(fn[t, x, i, d, TOP - 1 : TOP - 1 + rows_f, :], at, rows_f)
                    fine = jnp.where(thin == 16 * d + 8 * x + c, v, fine)
            if t == 0 and f == 0:
                for x in range(2):
                    v = jnp.broadcast_to(jm[x, d : d + 1, at : at + 1], (rows_f, LANES))
                    fine = jnp.where(thin == 16 * d + 8 * x + 6, v, fine)
        of_fine = thin - 8 * (thin // 8)
        of_fine = (of_fine < 3) | (of_fine == 6)
        qs[0:rows_f, :] = jnp.where(of_fine, fine, out[0:rows_f])
        qs[rows_f:rows_c, :] = out[rows_f:]
        pk[t, f] = jnp.transpose(qs[...])[0:32]

    def begin(f):
        loads["f%d" % f].wait()
        for c in range(3):
            i = 3 * f + c
            for x in range(2):
                for y in range(2):
                    fn[0, x, i, y, TOP : TOP + fz, :] = fin[i, pl.ds(2 * y + x, fz, stride=4), :]
                copy_top(0, x, i)
        ridge(0, f)
        loads["c%d" % f].wait()

    begin(0)
    loads["topo"].wait()
    for x in range(2):
        for y in range(2):
            jm[x, y : y + 1] = 1.0 + tp[x : x + 1, y * LANES : (y + 1) * LANES].astype(f32) * (1.0 / 1024.0)
    count = sum(h.astype(jnp.int32) for h in has_x + has_y + tuple(side & (rank < len(share)) for side in outer))
    pl.semaphore_wait(barrier, count)
    each(has_x, lambda d: j_copy(d, 1 - d).start())
    x_send(0, 0, 0, 1)
    pack(0, 0)
    y_send(0, 0)
    begin(1)
    pack(0, 1)
    y_send(0, 1)
    y_wait(0, 0)
    x_send(0, 0, 2)
    x_send(0, 1, 0, 1)
    y_wait(0, 1)
    x_send(0, 1, 2)

    each(has_x, lambda d: j_copy(d, d).wait_recv())
    for q in range(4):
        for y in range(2):
            row = jx[q // 3, y : y + 1] if q in (0, 3) else jm[q - 1, y : y + 1]
            inv = jnp.broadcast_to(1.0 / row, (8, LANES))
            rj[q, y] = inv
            if q in (1, 2):
                rj2[q - 1, y] = inv * inv
    for x in range(2):
        sides = []
        for s in range(2):
            row = yr[0, 0, s, 8 * x + 6 : 8 * x + 7, 0:1]
            row = jnp.broadcast_to(1.0 / jnp.where(row == 0.0, 1.0, row), (8, LANES))
            rjh[s, x] = row
            sides.append(row)
        rjl[x] = jnp.where(left, sides[0], sides[1])

    def halos(t, f):
        inside = lane <= fz
        for s in range(2):
            own = [yr[t, f, s, 8 * x : 8 * x + 8] for x in range(2)]
            west, east = xk[t, f, 0, s], xk[t, f, 1, s]
            cross = (own[1] - west, east - own[0], east - west)

            def put(k, row):
                at = 2 * k + 1 - s
                gt[at : at + 1, :] = row

            d = north(own[0]) - south(own[0])
            for c in range(3):
                put(c, own[0][3 + c : 4 + c])
            put(3, cross[2][4:5])
            put(4, cross[2][3:4] + d[5:6])
            put(5, d[4:5])
            for x in range(2):
                v = jnp.where(inside, own[x], 0.0)
                d = (north(v) - south(v)) * rjh[s, x]
                k = 6 + 6 * x
                for c in range(3):
                    put(k + c, own[x][c : c + 1])
                put(k + 3, cross[x][1:2])
                put(k + 4, cross[x][0:1] + d[2:3])
                put(k + 5, d[1:2])
        tt[...] = jnp.transpose(gt[...])

    def item(v, k):
        return pltpu.roll(v, LANES - 1 - 2 * k, 1)

    def coarse(t, f):
        for v in range(cz // 8):
            r = TOP + 8 * v
            th = tt[8 * v + 1 : 8 * v + 9, :]
            mu = (0.25 * STEP_SQUARED) * sc[8 * v : 8 * v + 8, :]
            both = (0.25 * STEP_SQUARED) * lc[8 * v : 8 * v + 8, :] + mu
            xx, yy, zz, cross, rise, tilt, twice = [], [], [], [], [], [], []
            for c in range(3):
                i = 3 * f + c
                u = cn[t, i, r : r + 8, :]
                e, w = xc[t, 1, i, r : r + 8, :], xc[t, 0, i, r : r + 8, :]
                dn, up = cn[t, i, r + 1 : r + 9, :], cn[t, i, r - 1 : r + 7, :]
                h = item(th, c)
                u2 = 2.0 * u
                twice.append(u2)
                xx.append(e + w - u2)
                yy.append(jnp.where(last, h, north(u)) + jnp.where(first, h, south(u)) - u2)
                zz.append(dn + up - u2)
                cross.append(e - w)
                rise.append(dn - up)
                if c == 1:
                    tilt.append(None)
                else:
                    ed, eu = xc[t, 1, i, r + 1 : r + 9, :], xc[t, 1, i, r - 1 : r + 7, :]
                    wd, wu = xc[t, 0, i, r + 1 : r + 9, :], xc[t, 0, i, r - 1 : r + 7, :]
                    tilt.append((ed - eu) - (wd - wu))
            ac = []
            for k, a in enumerate((cross[1], cross[0] + rise[2], rise[1])):
                h = item(th, 3 + k)
                ac.append(jnp.where(last, h, north(a)) - jnp.where(first, h, south(a)))
            grad = (
                xx[0] + 0.25 * (ac[0] + tilt[2]),
                yy[1] + 0.25 * ac[1],
                zz[2] + 0.25 * (ac[2] + tilt[0]),
            )
            prod = None
            for c in range(3):
                i = 3 * f + c
                before = co[i, 8 * v : 8 * v + 8, :] if t == 0 else cn[t - 1, i, r : r + 8, :]
                new = (twice[c] - before) + (mu * (xx[c] + yy[c] + zz[c]) + both * grad[c])
                if t < STEPS - 1:
                    cn[t + 1, i, r : r + 8, :] = new
                else:
                    cout[i, 8 * v : 8 * v + 8, :] = new
                if f == 1:
                    if t < STEPS - 1:
                        pair = cn[t + 1, c, r : r + 8, :]
                    else:
                        pair = cout[c, 8 * v : 8 * v + 8, :]
                    prod = pair * new if prod is None else prod + pair * new
            if f == 1:
                if t > 0:
                    prod = prod + cker[8 * v : 8 * v + 8, :]
                cker[8 * v : 8 * v + 8, :] = prod

    def ghost(t, f):
        for c in range(3):
            i = 3 * f + c
            gs[0, 3 + c : 4 + c] = xc[t, 0, i, TOP : TOP + 1, :]
            gs[1, 3 + c : 4 + c] = cn[t, i, TOP : TOP + 1, :]
            gs[2, 3 + c : 4 + c] = xc[t, 1, i, TOP : TOP + 1, :]
        flat = [gs[k] for k in range(3)]
        rim = []
        for tiles in (
            [xk[t, f, 0, s] for s in range(2)],
            [yr[t, f, s, 0:8] for s in range(2)],
            [xk[t, f, 1, s] for s in range(2)],
        ):
            rim.append(jnp.where(left, spread(tiles[0], 1, 8), spread(tiles[1], 1, 8)))

        def mix(v):
            lo, mid, hi = v
            return (
                0.75 * lo + 0.25 * mid,
                0.75 * mid + 0.25 * lo,
                0.75 * mid + 0.25 * hi,
                0.75 * hi + 0.25 * mid,
            )

        for q, (v, h) in enumerate(zip(mix(flat), mix(rim))):
            a = 0.75 * v + 0.25 * jnp.where(first, h, south(v))
            b = 0.75 * v + 0.25 * jnp.where(last, h, north(v))
            for y in range(2):
                g = jnp.where(even, take(a, half_of[y]), take(b, half_of[y]))
                if q in (0, 3):
                    g = jnp.where(has_x[q // 3], g, 0.0)
                for c in range(3):
                    i = 3 * f + c
                    if q in (0, 3):
                        xf[t, q // 3, i, y, low_f : low_f + 1, :] = g[3 + c : 4 + c]
                    else:
                        fn[t, q - 1, i, y, low_f : low_f + 1, :] = g[3 + c : 4 + c]
            if q in (1, 2):
                g = jnp.where(y_edge, 0.75 * h + 0.25 * v, 0.0) * rjl[q - 1]
                cor[q - 1, 0, 7:8] = g[5:6]
                cor[q - 1, 1, 7:8] = g[4:5]

    def fine(t, f):
        for side in range(2):
            for c in (0, 2):
                for y in range(2):
                    xf[t, side, 3 * f + c, y, TOP - 1 : TOP, :] = xf[
                        t, side, 3 * f + c, y, TOP : TOP + 1, :
                    ]

        def plane(q, i, y, r):
            if q in (0, 3):
                return xf[t, q // 3, i, y, r : r + 8, :]
            return fn[t, q - 1, i, y, r : r + 8, :]

        for v in range(fz // 8):
            r = TOP + 8 * v
            th = tt[8 * v + 1 : 8 * v + 9, :]
            for x in range(2):
                q = x + 1
                xx, yy, zz, up_down, twice = {}, {}, {}, {}, {}
                va = [[None, None] for _ in range(3)]
                tilt = {}
                mid = {}
                for y in range(2):
                    inv = rj[q, y]
                    cross, rise = [], []
                    for c in range(3):
                        i = 3 * f + c
                        u = plane(q, i, y, r)
                        e, w = plane(q + 1, i, y, r), plane(q - 1, i, y, r)
                        dn, up = plane(q, i, y, r + 1), plane(q, i, y, r - 1)
                        mid[c, y] = u
                        u2 = 2.0 * u
                        twice[c, y] = u2
                        xx[c, y] = e + w - u2
                        zz[c, y] = (dn + up - u2) * rj2[x, y]
                        cross.append(e - w)
                        rise.append((dn - up) * inv if c else None)
                        if c != 1:
                            ed, eu = plane(q + 1, i, y, r + 1), plane(q + 1, i, y, r - 1)
                            wd, wu = plane(q - 1, i, y, r + 1), plane(q - 1, i, y, r - 1)
                            tilt[c, y] = (ed - eu) * rj[q + 1, y] - (wd - wu) * rj[q - 1, y]
                    va[0][y] = cross[1]
                    va[1][y] = cross[0] + rise[2]
                    va[2][y] = rise[1]

                def ends(a, b, h):
                    na, nb, sa, sb = north(a), north(b), south(a), south(b)
                    return (
                        (jnp.where(last, nb, na), jnp.where(first, h, sa)),
                        (jnp.where(last, h, nb), jnp.where(first, sa, sb)),
                    )

                k = 6 + 6 * x
                for c in range(3):
                    for y, (n, s) in enumerate(ends(mid[c, 0], mid[c, 1], item(th, k + c))):
                        yy[c, y] = n + s - twice[c, y]
                ac = {}
                for c in range(3):
                    h = item(th, k + 3 + c)
                    if c and v == fz // 8 - 1:
                        h = h + cor[x, c - 1]
                    for y, (n, s) in enumerate(ends(va[c][0], va[c][1], h)):
                        ac[c, y] = n - s
                for y in range(2):
                    pick = pl.ds(32 * v + 2 * y + x, 8, stride=4)
                    mu = STEP_SQUARED * sf[pick, :]
                    both = STEP_SQUARED * lf[pick, :] + mu
                    grad = (
                        xx[0, y] + 0.25 * (ac[0, y] + tilt[2, y]),
                        yy[1, y] + 0.25 * ac[1, y],
                        zz[2, y] + 0.25 * (ac[2, y] + tilt[0, y]),
                    )
                    prod = None
                    for c in range(3):
                        i = 3 * f + c
                        before = fo[i, pick, :] if t == 0 else fn[t - 1, x, i, y, r : r + 8, :]
                        new = (twice[c, y] - before) + (
                            mu * (xx[c, y] + yy[c, y] + zz[c, y]) + both * grad[c]
                        )
                        if t < STEPS - 1:
                            fn[t + 1, x, i, y, r : r + 8, :] = new
                        else:
                            fout[i, pick, :] = new
                        if f == 1:
                            if t < STEPS - 1:
                                pair = fn[t + 1, x, c, y, r : r + 8, :]
                            else:
                                pair = fout[c, pick, :]
                            prod = pair * new if prod is None else prod + pair * new
                    if f == 1:
                        if t > 0:
                            prod = prod + fker[pick, :]
                        fker[pick, :] = prod

    def finish_level(t, f):
        for c in range(3):
            for x in range(2):
                copy_top(t, x, 3 * f + c)
        ridge(t, f)
        x_send(t, f, 0, 1)
        pack(t, f)
        y_send(t, f)

    for t in range(STEPS):
        for f in range(2):
            if f == 1:
                pass_on(t, (2, 1)[t])
            x_wait(t, f, 0)
            if t == 0 and f == 0:
                drain(ins.at[5], 8 * cz)
            x_wait(t, f, 2)
            halos(t, f)
            coarse(t, f)
            if t > 0 and f == 0:
                y_wait(t, 1)
                x_send(t, 1, 2)
            if t < STEPS - 1 and f == 1:
                y_wait(t + 1, 0)
                x_send(t + 1, 0, 2)
            ghost(t, f)
            pass_on(t, ((1, 3), (0, 2))[t][f])
            x_wait(t, f, 1)
            if t == 0 and f == 0:
                drain(ins.at[6], 32 * fz)
            fine(t, f)
            if t < STEPS - 1:
                finish_level(t + 1, f)

    sent = 8 + 2 * STEPS * (3 * (cz + 1) + 6 * fz + 16)
    each(has_x, lambda d: drain(xs.at[d], sent))
    each(has_y, lambda d: drain(ys.at[d], 32 * STEPS))
    for t in range(STEPS):
        for m in route[t]:
            pl.when(passes[t][m])(pass_copy(t, m, 0).wait_send)


def put_body(*refs):
    ins, outs, sem = refs[:4], refs[4:8], refs[8]
    copies = [
        pltpu.make_async_copy(a, b, sem.at[i]) for i, (a, b) in enumerate(zip(ins, outs))
    ]
    for copy in copies:
        copy.start()
    for copy in copies:
        copy.wait()


def rows_view(a):
    lead = a.shape[:-3]
    fz, fx, fy = a.shape[-3:]
    n = len(lead)
    a = a.reshape(lead + (fz, fx, fy // LANES, LANES))
    a = a.transpose(tuple(range(n)) + (n, n + 2, n + 1, n + 3))
    return a.reshape(((6,) if lead else ()) + (fz * fx * fy // LANES, LANES))


def rows_back(a, shape):
    lead = shape[:-3]
    fz, fx, fy = shape[-3:]
    n = len(lead)
    a = a.reshape(lead + (fz, fy // LANES, fx, LANES))
    a = a.transpose(tuple(range(n)) + (n, n + 2, n + 1, n + 3))
    return a.reshape(shape)


def on_device(fold, fnow, cold, cnow, shf, laf, shc, lac, topo):
    nx, ny = lax.axis_size("gx"), lax.axis_size("gy")
    fz, fx, fy = shf.shape
    cz, cx, cy = shc.shape
    if fx != 2 or cx != 1 or cy != LANES or fy != 2 * cy or fz % 8 or cz % 8 or cz + 8 > LANES:
        raise ValueError("unsupported tile")
    f32 = jnp.float32
    dma = pltpu.SemaphoreType.DMA
    nrows = fz * fx * fy // LANES
    vm = pl.BlockSpec(memory_space=pltpu.VMEM)
    hbm = pl.BlockSpec(memory_space=pl.ANY)
    shapes = ((6, nrows, LANES), (6, cz, cy), (nrows, LANES), (cz, cy))
    args = (
        rows_view(fold),
        rows_view(fnow),
        cold.reshape(6, cz, cy),
        cnow.reshape(6, cz, cy),
        rows_view(shf),
        rows_view(laf),
        shc.reshape(cz, cy),
        lac.reshape(cz, cy),
        topo,
    )
    inner = pl.pallas_call(
        functools.partial(body, nx, ny, fz, cz),
        out_shape=tuple(pltpu.VMEM(s, f32) for s in shapes),
        in_specs=[hbm] * 9,
        out_specs=(vm,) * 4,
        scratch_shapes=[
            pltpu.VMEM((6, nrows, LANES), f32),
            pltpu.VMEM((6, nrows, LANES), f32),
            pltpu.VMEM((6, cz, cy), f32),
            pltpu.VMEM((nrows, LANES), f32),
            pltpu.VMEM((nrows, LANES), f32),
            pltpu.VMEM((cz, cy), f32),
            pltpu.VMEM((cz, cy), f32),
            pltpu.VMEM((fx, fy), jnp.int32),
            pltpu.VMEM((STEPS, 2, 6, 2, fz + 16, LANES), f32),
            pltpu.VMEM((STEPS, 6, cz + 16, LANES), f32),
            pltpu.VMEM((STEPS, 2, 6, 2, fz + 16, LANES), f32),
            pltpu.VMEM((STEPS, 2, 6, cz + 16, LANES), f32),
            pltpu.VMEM((2, 8, LANES), f32),
            pltpu.VMEM((2, 8, LANES), f32),
            pltpu.VMEM((STEPS, 2, 32, LANES), f32),
            pltpu.VMEM((STEPS, 2, 2, 16, LANES), f32),
            pltpu.VMEM((STEPS, 2, 2, 2, 8, LANES), f32),
            pltpu.VMEM((4, 2, 8, LANES), f32),
            pltpu.VMEM((2, 2, 8, LANES), f32),
            pltpu.VMEM((2, 2, 8, LANES), f32),
            pltpu.VMEM((2, 8, LANES), f32),
            pltpu.VMEM((LANES, LANES), f32),
            pltpu.VMEM((LANES, LANES), f32),
            pltpu.VMEM((LANES, LANES), f32),
            pltpu.VMEM((3, 8, LANES), f32),
            pltpu.VMEM((2, 2, 8, LANES), f32),
            pltpu.VMEM((4 * STEPS * (3 * cz + 6 * fz + 32), LANES), f32),
            pltpu.VMEM((STEPS, 2, 3, 2, fz, LANES), f32),
            pltpu.VMEM((STEPS, 2, 3, cz + 8, LANES), f32),
            dma((7,)),
            dma((2,)),
            dma((STEPS, 2, 3, 2)),
            dma((2,)),
            dma((2,)),
            dma((STEPS, 2, 2)),
            dma((STEPS, 4)),
            dma((STEPS, 4)),
        ],
        compiler_params=pltpu.CompilerParams(
            collective_id=0, has_side_effects=True, vmem_limit_bytes=32 << 20
        ),
        name="wave",
    )(*[pltpu.with_memory_space_constraint(a, pltpu.HBM) for a in args])
    fout, cout, fker, cker = pl.pallas_call(
        put_body,
        out_shape=tuple(jax.ShapeDtypeStruct(s, f32) for s in shapes),
        in_specs=[vm] * 4,
        out_specs=(hbm,) * 4,
        scratch_shapes=[dma((4,))],
        compiler_params=pltpu.CompilerParams(vmem_limit_bytes=1 << 20),
        name="put",
    )(*[pltpu.with_memory_space_constraint(a, pltpu.VMEM) for a in inner])
    return (
        rows_back(fout, fold.shape),
        cout.reshape(cold.shape),
        rows_back(fker, shf.shape),
        cker.reshape(shc.shape),
    )


def solution(mesh):
    field, coef = P(None, None, None, "gx", "gy"), P(None, "gx", "gy")
    return jax.shard_map(
        on_device,
        mesh=mesh,
        in_specs=(field,) * 4 + (coef,) * 4 + (P("gx", "gy"),),
        out_specs=(field, field, coef, coef),
        check_vma=False,
    )
```

```python
import functools

import jax
import jax.numpy as jnp
from jax import lax
from jax.experimental import pallas as pl
from jax.experimental.pallas import tpu as pltpu
from jax.sharding import PartitionSpec as P

STEPS = 2
STEP_SQUARED = 0.04
LANES = 128
TOP = 8


def body(
    nx, ny, fz, cz,
    fold, fnow, cold, cnow, shf, laf, shc, lac, topo,
    fout, cout, fker, cker,
    fin, fo, co, sf, lf, sc, lc, tp,
    fn, cn, xf, xc, jm, jx, pk, yr, xk,
    rj, rj2, rjh, rjl, qs, gt, tt, gs, cor, span, via_f, via_c,
    ins, xs, xr, jr, ys, yrs, vs, vr,
):
    f32 = jnp.float32
    gx, gy = lax.axis_index("gx"), lax.axis_index("gy")
    has_x = (gx > 0, gx < nx - 1)
    has_y = (gy > 0, gy < ny - 1)
    rows_c = cz + 8
    rows_f = fz + 8
    low_c, low_f = TOP + cz, TOP + fz

    def each(flags, action):
        for d in range(2):
            pl.when(flags[d])(functools.partial(action, d))

    def half(f):
        return pl.ds(3 * f, 3)

    loads = {
        "f0": (fnow.at[half(0)], fin.at[half(0)]),
        "c0": (cnow.at[half(0)], cn.at[0, half(0), pl.ds(TOP, cz)]),
        "topo": (topo, tp),
        "f1": (fnow.at[half(1)], fin.at[half(1)]),
        "c1": (cnow.at[half(1)], cn.at[0, half(1), pl.ds(TOP, cz)]),
        "co": (cold, co),
        "sc": (shc, sc),
        "lc": (lac, lc),
        "fo": (fold, fo),
        "sf": (shf, sf),
        "lf": (laf, lf),
    }
    slots = {"f0": 0, "c0": 1, "topo": 2, "f1": 3, "c1": 4, "co": 5, "sc": 5, "lc": 5}
    loads = {
        k: pltpu.make_async_copy(a, b, ins.at[slots.get(k, 6)]) for k, (a, b) in loads.items()
    }
    for copy in loads.values():
        copy.start()

    def drain(sem, rows):
        part = span.at[pl.ds(0, rows)]
        pltpu.make_async_copy(part, part, sem).wait()

    planes = nx // 4 if nx % 4 == 0 else 0
    share = [min(3, (8 * (planes - 1 - z) + planes) // (2 * planes)) for z in range(planes - 1)]
    route = [{1: 3, 2: 2, 3: 1}, {0: 2, 1: 1, 2: 3}]
    reach = [{m: sum(n >= least for n in share) for m, least in r.items()} for r in route]
    at4, plane = lax.rem(gx, 4), gx // 4
    rank = jnp.where((at4 == 1) | (at4 == 3), plane, planes - 1 - plane)
    outer = ((at4 == 0), (at4 == 3))
    middle = (at4 == 1) | (at4 == 2)
    detour = [{(m, d): outer[d] & (rank < r[m]) for m in r for d in range(2)} for r in reach]
    passes = [{m: middle & (rank < r[m]) for m in r} for r in reach]
    from_left = at4 == 2
    even_x = lax.rem(gx, 2) == 0

    barrier = pltpu.get_barrier_semaphore()
    each(has_x, lambda d: pl.semaphore_signal(barrier, inc=1, device_id={"gx": gx + 2 * d - 1}))
    each(has_y, lambda d: pl.semaphore_signal(barrier, inc=1, device_id={"gy": gy + 2 * d - 1}))

    @pl.when(middle & (rank < len(share)))
    def _():
        source = gx + jnp.where(from_left, -2, 2)
        pl.semaphore_signal(barrier, inc=1, device_id={"gx": source})

    def x_copy(t, f, kind, d, land):
        if kind == 0:
            rows = pl.ds(TOP - 1, cz + 1)
            src, dst = cn.at[t, half(f), rows], xc.at[t, land, half(f), rows]
        elif kind == 1:
            rows = pl.ds(TOP, fz)
            src, dst = fn.at[t, d, half(f), :, rows], xf.at[t, land, half(f), :, rows]
        else:
            src, dst = yr.at[t, f, :, pl.ds(8 * d, 8)], xk.at[t, f, land]
        return pltpu.make_async_remote_copy(
            src, dst, xs.at[d], xr.at[t, f, kind, land], device_id={"gx": gx + 2 * d - 1}
        )

    def stop(t, m):
        if m - 2 * (m // 2) == 1:
            return via_f.at[t, m // 2]
        return via_c.at[t, m // 2, :, pl.ds(0, cz + 1)]

    def detour_copy(t, f, kind, d):
        m = 2 * f + kind
        if kind == 0:
            src = cn.at[t, half(f), pl.ds(TOP - 1, cz + 1)]
        else:
            src = fn.at[t, d, half(f), :, pl.ds(TOP, fz)]
        return pltpu.make_async_remote_copy(
            src, stop(t, m), xs.at[d], vr.at[t, m], device_id={"gx": gx + 2 - 4 * d}
        )

    def pass_copy(t, m, land):
        f, kind = m // 2, m - 2 * (m // 2)
        if kind == 0:
            dst = xc.at[t, land, half(f), pl.ds(TOP - 1, cz + 1)]
        else:
            dst = xf.at[t, land, half(f), :, pl.ds(TOP, fz)]
        return pltpu.make_async_remote_copy(
            stop(t, m), dst, vs.at[t, m], xr.at[t, f, kind, land],
            device_id={"gx": gx + 3 - 6 * land},
        )

    def pass_on(t, m):
        @pl.when(passes[t][m])
        def _():
            part = stop(t, m)
            pltpu.make_async_copy(part, part, vr.at[t, m]).wait()
            for land in range(2):
                pl.when((at4 == 1 + land))(pass_copy(t, m, land).start)

    def y_copy(t, f, d, land):
        return pltpu.make_async_remote_copy(
            pk.at[t, f, pl.ds(16 * d, 16)], yr.at[t, f, land], ys.at[d], yrs.at[t, f, land],
            device_id={"gy": gy + 2 * d - 1},
        )

    def j_copy(d, land):
        return pltpu.make_async_remote_copy(
            jm.at[d], jx.at[land], xs.at[d], jr.at[land], device_id={"gx": gx + 2 * d - 1}
        )

    def x_send(t, f, *kinds):
        def go(d):
            for kind in kinds:
                m = 2 * f + kind
                if kind == 2 or m not in route[t]:
                    x_copy(t, f, kind, d, 1 - d).start()
                else:
                    pl.when(detour[t][m, d])(detour_copy(t, f, kind, d).start)
                    pl.when(jnp.logical_not(detour[t][m, d]))(x_copy(t, f, kind, d, 1 - d).start)

        pl.when(has_x[1] & even_x)(functools.partial(go, 1))
        pl.when(has_x[0])(functools.partial(go, 0))
        pl.when(has_x[1] & jnp.logical_not(even_x))(functools.partial(go, 1))

    def x_wait(t, f, kind):
        each(has_x, lambda d: x_copy(t, f, kind, d, d).wait_recv())

    def y_send(t, f):
        each(has_y, lambda d: y_copy(t, f, d, 1 - d).start())

    def y_wait(t, f):
        each(has_y, lambda d: y_copy(t, f, d, d).wait_recv())

    lane = lax.broadcasted_iota(jnp.int32, (8, LANES), 1)
    sub = lax.broadcasted_iota(jnp.int32, (8, LANES), 0)
    first, last = lane == 0, lane == LANES - 1
    left = lane < LANES // 2
    even = lane - 2 * (lane // 2) == 0
    pair_of = lane * 2 - jnp.where(left, 0, LANES)
    half_of = (lane // 2, lane // 2 + LANES // 2)
    y_edge = (first & has_y[0]) | (last & has_y[1])

    def north(v):
        return pltpu.roll(v, LANES - 1, 1)

    def south(v):
        return pltpu.roll(v, 1, 1)

    def take(v, index):
        return jnp.take_along_axis(v, index, axis=1, mode="promise_in_bounds")

    def spread(v, at, rows):
        return jnp.broadcast_to(v[:, at : at + 1], (rows, LANES))

    for t in range(STEPS):
        for i in range(6):
            row = jnp.zeros((1, LANES), f32)
            cn[t, i, low_c : low_c + 1, :] = row
            xc[t, 0, i, low_c : low_c + 1, :] = row
            xc[t, 1, i, low_c : low_c + 1, :] = row
    cor[...] = jnp.zeros(cor.shape, f32)
    gt[...] = jnp.zeros(gt.shape, f32)
    qs[...] = jnp.zeros(qs.shape, f32)
    gs[...] = jnp.zeros(gs.shape, f32)
    jm[...] = jnp.ones(jm.shape, f32)
    for d in range(2):

        @pl.when(jnp.logical_not(has_x[d]))
        def _():
            for t in range(STEPS):
                xf[t, d] = jnp.zeros(xf.shape[2:], f32)
                xc[t, d] = jnp.zeros(xc.shape[2:], f32)
                for f in range(2):
                    xk[t, f, d] = jnp.zeros(xk.shape[3:], f32)
            jx[d] = jnp.ones(jx.shape[1:], f32)

        @pl.when(jnp.logical_not(has_y[d]))
        def _():
            for t in range(STEPS):
                for f in range(2):
                    yr[t, f, d] = jnp.zeros(yr.shape[3:], f32)

    def ridge(t, f):
        for c in range(3):
            i = 3 * f + c
            for y in range(2):
                gs[y, c : c + 1] = (
                    fn[t, 0, i, y, low_f - 1 : low_f, :] + fn[t, 1, i, y, low_f - 1 : low_f, :]
                )
        a, b = gs[0], gs[1]
        a, b = take(a + north(a), pair_of), take(b + north(b), pair_of)
        mean = 0.25 * jnp.where(left, a, b)
        for c in range(3):
            cn[t, 3 * f + c, TOP - 1 : TOP, :] = mean[c : c + 1]

    def copy_top(t, x, i):
        for y in range(2):
            fn[t, x, i, y, TOP - 1 : TOP, :] = fn[t, x, i, y, TOP : TOP + 1, :]

    def pack(t, f):
        wide = lax.broadcasted_iota(jnp.int32, (rows_c, LANES), 1)
        thin = lax.broadcasted_iota(jnp.int32, (rows_f, LANES), 1)
        out = jnp.zeros((rows_c, LANES), f32)
        fine = jnp.zeros((rows_f, LANES), f32)
        for d in range(2):
            at = (0, LANES - 1)[d]
            for c in range(3):
                i, j = 3 * f + c, 16 * d + 3 + c
                v = spread(cn[t, i, TOP - 1 : TOP - 1 + rows_c, :], at, rows_c)
                out = jnp.where((wide == j) | (wide == j + 8), v, out)
                for x in range(2):
                    v = spread(fn[t, x, i, d, TOP - 1 : TOP - 1 + rows_f, :], at, rows_f)
                    fine = jnp.where(thin == 16 * d + 8 * x + c, v, fine)
            if t == 0 and f == 0:
                for x in range(2):
                    v = jnp.broadcast_to(jm[x, d : d + 1, at : at + 1], (rows_f, LANES))
                    fine = jnp.where(thin == 16 * d + 8 * x + 6, v, fine)
        of_fine = thin - 8 * (thin // 8)
        of_fine = (of_fine < 3) | (of_fine == 6)
        qs[0:rows_f, :] = jnp.where(of_fine, fine, out[0:rows_f])
        qs[rows_f:rows_c, :] = out[rows_f:]
        pk[t, f] = jnp.transpose(qs[...])[0:32]

    def begin(f):
        loads["f%d" % f].wait()
        for c in range(3):
            i = 3 * f + c
            for x in range(2):
                for y in range(2):
                    fn[0, x, i, y, TOP : TOP + fz, :] = fin[i, pl.ds(2 * y + x, fz, stride=4), :]
                copy_top(0, x, i)
        ridge(0, f)
        loads["c%d" % f].wait()

    begin(0)
    loads["topo"].wait()
    for x in range(2):
        for y in range(2):
            jm[x, y : y + 1] = 1.0 + tp[x : x + 1, y * LANES : (y + 1) * LANES].astype(f32) * (1.0 / 1024.0)
    count = sum(h.astype(jnp.int32) for h in has_x + has_y + tuple(side & (rank < len(share)) for side in outer))
    pl.semaphore_wait(barrier, count)
    each(has_x, lambda d: j_copy(d, 1 - d).start())
    x_send(0, 0, 0, 1)
    pack(0, 0)
    y_send(0, 0)
    begin(1)
    pack(0, 1)
    y_send(0, 1)
    y_wait(0, 0)
    x_send(0, 0, 2)
    x_send(0, 1, 0, 1)
    y_wait(0, 1)
    x_send(0, 1, 2)

    each(has_x, lambda d: j_copy(d, d).wait_recv())
    for q in range(4):
        for y in range(2):
            row = jx[q // 3, y : y + 1] if q in (0, 3) else jm[q - 1, y : y + 1]
            inv = jnp.broadcast_to(1.0 / row, (8, LANES))
            rj[q, y] = inv
            if q in (1, 2):
                rj2[q - 1, y] = inv * inv
    for x in range(2):
        sides = []
        for s in range(2):
            row = yr[0, 0, s, 8 * x + 6 : 8 * x + 7, 0:1]
            row = jnp.broadcast_to(1.0 / jnp.where(row == 0.0, 1.0, row), (8, LANES))
            rjh[s, x] = row
            sides.append(row)
        rjl[x] = jnp.where(left, sides[0], sides[1])

    def halos(t, f):
        inside = lane <= fz
        for s in range(2):
            own = [yr[t, f, s, 8 * x : 8 * x + 8] for x in range(2)]
            west, east = xk[t, f, 0, s], xk[t, f, 1, s]
            cross = (own[1] - west, east - own[0], east - west)

            def put(k, row):
                at = 2 * k + 1 - s
                gt[at : at + 1, :] = row

            d = north(own[0]) - south(own[0])
            for c in range(3):
                put(c, own[0][3 + c : 4 + c])
            put(3, cross[2][4:5])
            put(4, cross[2][3:4] + d[5:6])
            put(5, d[4:5])
            for x in range(2):
                v = jnp.where(inside, own[x], 0.0)
                d = (north(v) - south(v)) * rjh[s, x]
                k = 6 + 6 * x
                for c in range(3):
                    put(k + c, own[x][c : c + 1])
                put(k + 3, cross[x][1:2])
                put(k + 4, cross[x][0:1] + d[2:3])
                put(k + 5, d[1:2])
        tt[...] = jnp.transpose(gt[...])

    def item(v, k):
        return pltpu.roll(v, LANES - 1 - 2 * k, 1)

    def coarse(t, f):
        for v in range(cz // 8):
            r = TOP + 8 * v
            th = tt[8 * v + 1 : 8 * v + 9, :]
            mu = (0.25 * STEP_SQUARED) * sc[8 * v : 8 * v + 8, :]
            both = (0.25 * STEP_SQUARED) * lc[8 * v : 8 * v + 8, :] + mu
            xx, yy, zz, cross, rise, tilt, twice = [], [], [], [], [], [], []
            for c in range(3):
                i = 3 * f + c
                u = cn[t, i, r : r + 8, :]
                e, w = xc[t, 1, i, r : r + 8, :], xc[t, 0, i, r : r + 8, :]
                dn, up = cn[t, i, r + 1 : r + 9, :], cn[t, i, r - 1 : r + 7, :]
                h = item(th, c)
                u2 = 2.0 * u
                twice.append(u2)
                xx.append(e + w - u2)
                yy.append(jnp.where(last, h, north(u)) + jnp.where(first, h, south(u)) - u2)
                zz.append(dn + up - u2)
                cross.append(e - w)
                rise.append(dn - up)
                if c == 1:
                    tilt.append(None)
                else:
                    ed, eu = xc[t, 1, i, r + 1 : r + 9, :], xc[t, 1, i, r - 1 : r + 7, :]
                    wd, wu = xc[t, 0, i, r + 1 : r + 9, :], xc[t, 0, i, r - 1 : r + 7, :]
                    tilt.append((ed - eu) - (wd - wu))
            ac = []
            for k, a in enumerate((cross[1], cross[0] + rise[2], rise[1])):
                h = item(th, 3 + k)
                ac.append(jnp.where(last, h, north(a)) - jnp.where(first, h, south(a)))
            grad = (
                xx[0] + 0.25 * (ac[0] + tilt[2]),
                yy[1] + 0.25 * ac[1],
                zz[2] + 0.25 * (ac[2] + tilt[0]),
            )
            prod = None
            for c in range(3):
                i = 3 * f + c
                before = co[i, 8 * v : 8 * v + 8, :] if t == 0 else cn[t - 1, i, r : r + 8, :]
                new = (twice[c] - before) + (mu * (xx[c] + yy[c] + zz[c]) + both * grad[c])
                if t < STEPS - 1:
                    cn[t + 1, i, r : r + 8, :] = new
                else:
                    cout[i, 8 * v : 8 * v + 8, :] = new
                if f == 1:
                    if t < STEPS - 1:
                        pair = cn[t + 1, c, r : r + 8, :]
                    else:
                        pair = cout[c, 8 * v : 8 * v + 8, :]
                    prod = pair * new if prod is None else prod + pair * new
            if f == 1:
                if t > 0:
                    prod = prod + cker[8 * v : 8 * v + 8, :]
                cker[8 * v : 8 * v + 8, :] = prod

    def ghost(t, f):
        for c in range(3):
            i = 3 * f + c
            gs[0, 3 + c : 4 + c] = xc[t, 0, i, TOP : TOP + 1, :]
            gs[1, 3 + c : 4 + c] = cn[t, i, TOP : TOP + 1, :]
            gs[2, 3 + c : 4 + c] = xc[t, 1, i, TOP : TOP + 1, :]
        flat = [gs[k] for k in range(3)]
        rim = []
        for tiles in (
            [xk[t, f, 0, s] for s in range(2)],
            [yr[t, f, s, 0:8] for s in range(2)],
            [xk[t, f, 1, s] for s in range(2)],
        ):
            rim.append(jnp.where(left, spread(tiles[0], 1, 8), spread(tiles[1], 1, 8)))

        def mix(v):
            lo, mid, hi = v
            return (
                0.75 * lo + 0.25 * mid,
                0.75 * mid + 0.25 * lo,
                0.75 * mid + 0.25 * hi,
                0.75 * hi + 0.25 * mid,
            )

        for q, (v, h) in enumerate(zip(mix(flat), mix(rim))):
            a = 0.75 * v + 0.25 * jnp.where(first, h, south(v))
            b = 0.75 * v + 0.25 * jnp.where(last, h, north(v))
            for y in range(2):
                g = jnp.where(even, take(a, half_of[y]), take(b, half_of[y]))
                if q in (0, 3):
                    g = jnp.where(has_x[q // 3], g, 0.0)
                for c in range(3):
                    i = 3 * f + c
                    if q in (0, 3):
                        xf[t, q // 3, i, y, low_f : low_f + 1, :] = g[3 + c : 4 + c]
                    else:
                        fn[t, q - 1, i, y, low_f : low_f + 1, :] = g[3 + c : 4 + c]
            if q in (1, 2):
                g = jnp.where(y_edge, 0.75 * h + 0.25 * v, 0.0) * rjl[q - 1]
                cor[q - 1, 0, 7:8] = g[5:6]
                cor[q - 1, 1, 7:8] = g[4:5]

    def fine(t, f):
        for side in range(2):
            for c in (0, 2):
                for y in range(2):
                    xf[t, side, 3 * f + c, y, TOP - 1 : TOP, :] = xf[
                        t, side, 3 * f + c, y, TOP : TOP + 1, :
                    ]

        def plane(q, i, y, r):
            if q in (0, 3):
                return xf[t, q // 3, i, y, r : r + 8, :]
            return fn[t, q - 1, i, y, r : r + 8, :]

        for v in range(fz // 8):
            r = TOP + 8 * v
            th = tt[8 * v + 1 : 8 * v + 9, :]
            for x in range(2):
                q = x + 1
                xx, yy, zz, up_down, twice = {}, {}, {}, {}, {}
                va = [[None, None] for _ in range(3)]
                tilt = {}
                mid = {}
                for y in range(2):
                    inv = rj[q, y]
                    cross, rise = [], []
                    for c in range(3):
                        i = 3 * f + c
                        u = plane(q, i, y, r)
                        e, w = plane(q + 1, i, y, r), plane(q - 1, i, y, r)
                        dn, up = plane(q, i, y, r + 1), plane(q, i, y, r - 1)
                        mid[c, y] = u
                        u2 = 2.0 * u
                        twice[c, y] = u2
                        xx[c, y] = e + w - u2
                        zz[c, y] = (dn + up - u2) * rj2[x, y]
                        cross.append(e - w)
                        rise.append((dn - up) * inv if c else None)
                        if c != 1:
                            ed, eu = plane(q + 1, i, y, r + 1), plane(q + 1, i, y, r - 1)
                            wd, wu = plane(q - 1, i, y, r + 1), plane(q - 1, i, y, r - 1)
                            tilt[c, y] = (ed - eu) * rj[q + 1, y] - (wd - wu) * rj[q - 1, y]
                    va[0][y] = cross[1]
                    va[1][y] = cross[0] + rise[2]
                    va[2][y] = rise[1]

                def ends(a, b, h):
                    na, nb, sa, sb = north(a), north(b), south(a), south(b)
                    return (
                        (jnp.where(last, nb, na), jnp.where(first, h, sa)),
                        (jnp.where(last, h, nb), jnp.where(first, sa, sb)),
                    )

                k = 6 + 6 * x
                for c in range(3):
                    for y, (n, s) in enumerate(ends(mid[c, 0], mid[c, 1], item(th, k + c))):
                        yy[c, y] = n + s - twice[c, y]
                ac = {}
                for c in range(3):
                    h = item(th, k + 3 + c)
                    if c and v == fz // 8 - 1:
                        h = h + cor[x, c - 1]
                    for y, (n, s) in enumerate(ends(va[c][0], va[c][1], h)):
                        ac[c, y] = n - s
                for y in range(2):
                    pick = pl.ds(32 * v + 2 * y + x, 8, stride=4)
                    mu = STEP_SQUARED * sf[pick, :]
                    both = STEP_SQUARED * lf[pick, :] + mu
                    grad = (
                        xx[0, y] + 0.25 * (ac[0, y] + tilt[2, y]),
                        yy[1, y] + 0.25 * ac[1, y],
                        zz[2, y] + 0.25 * (ac[2, y] + tilt[0, y]),
                    )
                    prod = None
                    for c in range(3):
                        i = 3 * f + c
                        before = fo[i, pick, :] if t == 0 else fn[t - 1, x, i, y, r : r + 8, :]
                        new = (twice[c, y] - before) + (
                            mu * (xx[c, y] + yy[c, y] + zz[c, y]) + both * grad[c]
                        )
                        if t < STEPS - 1:
                            fn[t + 1, x, i, y, r : r + 8, :] = new
                        else:
                            fout[i, pick, :] = new
                        if f == 1:
                            if t < STEPS - 1:
                                pair = fn[t + 1, x, c, y, r : r + 8, :]
                            else:
                                pair = fout[c, pick, :]
                            prod = pair * new if prod is None else prod + pair * new
                    if f == 1:
                        if t > 0:
                            prod = prod + fker[pick, :]
                        fker[pick, :] = prod

    def finish_level(t, f):
        for c in range(3):
            for x in range(2):
                copy_top(t, x, 3 * f + c)
        ridge(t, f)
        x_send(t, f, 0, 1)
        pack(t, f)
        y_send(t, f)

    for t in range(STEPS):
        for f in range(2):
            if (t, f) != (0, 0):
                pass_on(t, {(0, 1): 2, (1, 0): 0, (1, 1): 2}[t, f])
            x_wait(t, f, 0)
            if t == 0:
                pass_on(0, (1, 3)[f])
            if t == 0 and f == 0:
                drain(ins.at[5], 8 * cz)
            x_wait(t, f, 2)
            if t == 1 and f == 0:
                pass_on(1, 1)
            halos(t, f)
            coarse(t, f)
            if t > 0 and f == 0:
                y_wait(t, 1)
                x_send(t, 1, 2)
            if t < STEPS - 1 and f == 1:
                y_wait(t + 1, 0)
                x_send(t + 1, 0, 2)
            ghost(t, f)
            x_wait(t, f, 1)
            if t == 0 and f == 0:
                drain(ins.at[6], 32 * fz)
            fine(t, f)
            if t < STEPS - 1:
                finish_level(t + 1, f)

    sent = 8 + 2 * STEPS * (3 * (cz + 1) + 6 * fz + 16)
    each(has_x, lambda d: drain(xs.at[d], sent))
    each(has_y, lambda d: drain(ys.at[d], 32 * STEPS))
    for t in range(STEPS):
        for m in route[t]:
            pl.when(passes[t][m])(pass_copy(t, m, 0).wait_send)


def put_body(*refs):
    ins, outs, sem = refs[:4], refs[4:8], refs[8]
    copies = [
        pltpu.make_async_copy(a, b, sem.at[i]) for i, (a, b) in enumerate(zip(ins, outs))
    ]
    for copy in copies:
        copy.start()
    for copy in copies:
        copy.wait()


def rows_view(a):
    lead = a.shape[:-3]
    fz, fx, fy = a.shape[-3:]
    n = len(lead)
    a = a.reshape(lead + (fz, fx, fy // LANES, LANES))
    a = a.transpose(tuple(range(n)) + (n, n + 2, n + 1, n + 3))
    return a.reshape(((6,) if lead else ()) + (fz * fx * fy // LANES, LANES))


def rows_back(a, shape):
    lead = shape[:-3]
    fz, fx, fy = shape[-3:]
    n = len(lead)
    a = a.reshape(lead + (fz, fy // LANES, fx, LANES))
    a = a.transpose(tuple(range(n)) + (n, n + 2, n + 1, n + 3))
    return a.reshape(shape)


def on_device(fold, fnow, cold, cnow, shf, laf, shc, lac, topo):
    nx, ny = lax.axis_size("gx"), lax.axis_size("gy")
    fz, fx, fy = shf.shape
    cz, cx, cy = shc.shape
    if fx != 2 or cx != 1 or cy != LANES or fy != 2 * cy or fz % 8 or cz % 8 or cz + 8 > LANES:
        raise ValueError("unsupported tile")
    f32 = jnp.float32
    dma = pltpu.SemaphoreType.DMA
    nrows = fz * fx * fy // LANES
    vm = pl.BlockSpec(memory_space=pltpu.VMEM)
    hbm = pl.BlockSpec(memory_space=pl.ANY)
    shapes = ((6, nrows, LANES), (6, cz, cy), (nrows, LANES), (cz, cy))
    args = (
        rows_view(fold),
        rows_view(fnow),
        cold.reshape(6, cz, cy),
        cnow.reshape(6, cz, cy),
        rows_view(shf),
        rows_view(laf),
        shc.reshape(cz, cy),
        lac.reshape(cz, cy),
        topo,
    )
    inner = pl.pallas_call(
        functools.partial(body, nx, ny, fz, cz),
        out_shape=tuple(pltpu.VMEM(s, f32) for s in shapes),
        in_specs=[hbm] * 9,
        out_specs=(vm,) * 4,
        scratch_shapes=[
            pltpu.VMEM((6, nrows, LANES), f32),
            pltpu.VMEM((6, nrows, LANES), f32),
            pltpu.VMEM((6, cz, cy), f32),
            pltpu.VMEM((nrows, LANES), f32),
            pltpu.VMEM((nrows, LANES), f32),
            pltpu.VMEM((cz, cy), f32),
            pltpu.VMEM((cz, cy), f32),
            pltpu.VMEM((fx, fy), jnp.int32),
            pltpu.VMEM((STEPS, 2, 6, 2, fz + 16, LANES), f32),
            pltpu.VMEM((STEPS, 6, cz + 16, LANES), f32),
            pltpu.VMEM((STEPS, 2, 6, 2, fz + 16, LANES), f32),
            pltpu.VMEM((STEPS, 2, 6, cz + 16, LANES), f32),
            pltpu.VMEM((2, 8, LANES), f32),
            pltpu.VMEM((2, 8, LANES), f32),
            pltpu.VMEM((STEPS, 2, 32, LANES), f32),
            pltpu.VMEM((STEPS, 2, 2, 16, LANES), f32),
            pltpu.VMEM((STEPS, 2, 2, 2, 8, LANES), f32),
            pltpu.VMEM((4, 2, 8, LANES), f32),
            pltpu.VMEM((2, 2, 8, LANES), f32),
            pltpu.VMEM((2, 2, 8, LANES), f32),
            pltpu.VMEM((2, 8, LANES), f32),
            pltpu.VMEM((LANES, LANES), f32),
            pltpu.VMEM((LANES, LANES), f32),
            pltpu.VMEM((LANES, LANES), f32),
            pltpu.VMEM((3, 8, LANES), f32),
            pltpu.VMEM((2, 2, 8, LANES), f32),
            pltpu.VMEM((4 * STEPS * (3 * cz + 6 * fz + 32), LANES), f32),
            pltpu.VMEM((STEPS, 2, 3, 2, fz, LANES), f32),
            pltpu.VMEM((STEPS, 2, 3, cz + 8, LANES), f32),
            dma((7,)),
            dma((2,)),
            dma((STEPS, 2, 3, 2)),
            dma((2,)),
            dma((2,)),
            dma((STEPS, 2, 2)),
            dma((STEPS, 4)),
            dma((STEPS, 4)),
        ],
        compiler_params=pltpu.CompilerParams(
            collective_id=0, has_side_effects=True, vmem_limit_bytes=32 << 20
        ),
        name="wave",
    )(*[pltpu.with_memory_space_constraint(a, pltpu.HBM) for a in args])
    fout, cout, fker, cker = pl.pallas_call(
        put_body,
        out_shape=tuple(jax.ShapeDtypeStruct(s, f32) for s in shapes),
        in_specs=[vm] * 4,
        out_specs=(hbm,) * 4,
        scratch_shapes=[dma((4,))],
        compiler_params=pltpu.CompilerParams(vmem_limit_bytes=1 << 20),
        name="put",
    )(*[pltpu.with_memory_space_constraint(a, pltpu.VMEM) for a in inner])
    return (
        rows_back(fout, fold.shape),
        cout.reshape(cold.shape),
        rows_back(fker, shf.shape),
        cker.reshape(shc.shape),
    )


def solution(mesh):
    field, coef = P(None, None, None, "gx", "gy"), P(None, "gx", "gy")
    return jax.shard_map(
        on_device,
        mesh=mesh,
        in_specs=(field,) * 4 + (coef,) * 4 + (P("gx", "gy"),),
        out_specs=(field, field, coef, coef),
        check_vma=False,
    )
```

```python
import functools

import jax
import jax.numpy as jnp
from jax import lax
from jax.experimental import pallas as pl
from jax.experimental.pallas import tpu as pltpu
from jax.sharding import PartitionSpec as P

STEPS = 2
STEP_SQUARED = 0.04
LANES = 128
TOP = 8


def body(
    nx, ny, fz, cz,
    fold, fnow, cold, cnow, shf, laf, shc, lac, topo,
    fout, cout, fker, cker,
    fin, fo, co, sf, lf, sc, lc, tp,
    fn, cn, xf, xc, jm, jx, pk, yr, xk,
    rj, rj2, rjh, rjl, qs, gt, tt, gs, cor, span, via_f, via_c,
    ins, xs, xr, ys, yrs, vs, vr,
):
    f32 = jnp.float32
    gx, gy = lax.axis_index("gx"), lax.axis_index("gy")
    has_x = (gx > 0, gx < nx - 1)
    has_y = (gy > 0, gy < ny - 1)
    rows_c = cz + 8
    rows_f = fz + 8
    low_c, low_f = TOP + cz, TOP + fz

    def each(flags, action):
        for d in range(2):
            pl.when(flags[d])(functools.partial(action, d))

    def half(f):
        return pl.ds(3 * f, 3)

    loads = {
        "f0": (fnow.at[half(0)], fin.at[half(0)]),
        "c0": (cnow.at[half(0)], cn.at[0, half(0), pl.ds(TOP, cz)]),
        "topo": (topo, tp),
        "f1": (fnow.at[half(1)], fin.at[half(1)]),
        "c1": (cnow.at[half(1)], cn.at[0, half(1), pl.ds(TOP, cz)]),
        "co": (cold, co),
        "sc": (shc, sc),
        "lc": (lac, lc),
        "fo": (fold, fo),
        "sf": (shf, sf),
        "lf": (laf, lf),
    }
    slots = {"f0": 0, "c0": 0, "topo": 0, "f1": 1, "c1": 1, "co": 2, "sc": 2, "lc": 2}
    for k, (a, b) in loads.items():
        pltpu.make_async_copy(a, b, ins.at[slots.get(k, 3)]).start()

    def drain(sem, rows):
        part = span.at[pl.ds(0, rows)]
        pltpu.make_async_copy(part, part, sem).wait()

    planes = nx // 4 if nx % 4 == 0 else 0
    share = [min(3, (8 * (planes - 1 - z) + planes) // (2 * planes)) for z in range(planes - 1)]
    route = [{1: 3, 2: 2, 3: 1}, {0: 2, 1: 1}]
    reach = [{m: sum(n >= least for n in share) for m, least in r.items()} for r in route]
    at4, plane = lax.rem(gx, 4), gx // 4
    rank = jnp.where((at4 == 1) | (at4 == 3), plane, planes - 1 - plane)
    outer = ((at4 == 0), (at4 == 3))
    middle = (at4 == 1) | (at4 == 2)
    detour = [{(m, d): outer[d] & (rank < r[m]) for m in r for d in range(2)} for r in reach]
    passes = [{m: middle & (rank < r[m]) for m in r} for r in reach]
    from_left = at4 == 2
    even_x = lax.rem(gx, 2) == 0
    turn = jnp.where((outer[0] & has_x[0]) | (outer[1] & has_x[1]), 1, 0) if share else 0

    barrier = pltpu.get_barrier_semaphore()
    each(has_x, lambda d: pl.semaphore_signal(barrier, inc=1, device_id={"gx": gx + 2 * d - 1}))
    each(has_y, lambda d: pl.semaphore_signal(barrier, inc=1, device_id={"gy": gy + 2 * d - 1}))

    @pl.when(middle & (rank < len(share)))
    def _():
        source = gx + jnp.where(from_left, -2, 2)
        pl.semaphore_signal(barrier, inc=1, device_id={"gx": source})

    def x_copy(t, f, kind, d, land):
        if kind == 0:
            rows = pl.ds(TOP - 1, cz + 1)
            src, dst = cn.at[t, half(f), rows], xc.at[t, land, half(f), rows]
        elif kind == 1:
            rows = pl.ds(TOP, fz)
            src, dst = fn.at[t, d, half(f), :, rows], xf.at[t, land, half(f), :, rows]
        else:
            src, dst = yr.at[t, f, :, pl.ds(8 * d, 4)], xk.at[t, f, land, :, pl.ds(0, 4)]
        return pltpu.make_async_remote_copy(
            src, dst, xs.at[d], xr.at[t, f, kind % 2, land], device_id={"gx": gx + 2 * d - 1}
        )

    def stop(t, m):
        if m - 2 * (m // 2) == 1:
            return via_f.at[t, m // 2]
        return via_c.at[t, m // 2, :, pl.ds(0, cz + 1)]

    def detour_copy(t, f, kind, d):
        m = 2 * f + kind
        if kind == 0:
            src = cn.at[t, half(f), pl.ds(TOP - 1, cz + 1)]
        else:
            src = fn.at[t, d, half(f), :, pl.ds(TOP, fz)]
        return pltpu.make_async_remote_copy(
            src, stop(t, m), xs.at[d], vr.at[4 * t + m], device_id={"gx": gx + 2 - 4 * d}
        )

    def pass_copy(t, m, land):
        f, kind = m // 2, m - 2 * (m // 2)
        if kind == 0:
            dst = xc.at[t, land, half(f), pl.ds(TOP - 1, cz + 1)]
        else:
            dst = xf.at[t, land, half(f), :, pl.ds(TOP, fz)]
        return pltpu.make_async_remote_copy(
            stop(t, m), dst, vs.at[0], xr.at[t, f, kind, land],
            device_id={"gx": gx + 3 - 6 * land},
        )

    def pass_on(t, m):
        @pl.when(passes[t][m])
        def _():
            part = stop(t, m)
            pltpu.make_async_copy(part, part, vr.at[4 * t + m]).wait()
            for land in range(2):
                pl.when((at4 == 1 + land))(pass_copy(t, m, land).start)

    def y_copy(t, f, d, land):
        return pltpu.make_async_remote_copy(
            pk.at[t, f, pl.ds(16 * d, 16)], yr.at[t, f, land], ys.at[d], yrs.at[t, f, land],
            device_id={"gy": gy + 2 * d - 1},
        )

    def j_copy(d, land):
        return pltpu.make_async_remote_copy(
            jm.at[d], jx.at[land], xs.at[d], xr.at[0, 0, 0, land], device_id={"gx": gx + 2 * d - 1}
        )

    def x_send(t, f, *kinds, where=True):
        def go(d):
            for kind in kinds:
                m = 2 * f + kind
                if kind == 2 or m not in route[t]:
                    x_copy(t, f, kind, d, 1 - d).start()
                else:
                    pl.when(detour[t][m, d])(detour_copy(t, f, kind, d).start)
                    pl.when(jnp.logical_not(detour[t][m, d]))(x_copy(t, f, kind, d, 1 - d).start)

        pl.when(has_x[1] & even_x & where)(functools.partial(go, 1))
        pl.when(has_x[0] & where)(functools.partial(go, 0))
        pl.when(has_x[1] & jnp.logical_not(even_x) & where)(functools.partial(go, 1))

    def x_wait(t, f, kind):
        rows = 6 * fz if kind else 3 * (cz + 1) + 8 + (8 if t == 0 and f == 0 else 0)
        each(has_x, lambda d: drain(xr.at[t, f, kind, d], rows))

    def y_send(t, f):
        each(has_y, lambda d: y_copy(t, f, d, 1 - d).start())

    def y_wait(t, f):
        each(has_y, lambda d: y_copy(t, f, d, d).wait_recv())

    lane = lax.broadcasted_iota(jnp.int32, (8, LANES), 1)
    sub = lax.broadcasted_iota(jnp.int32, (8, LANES), 0)
    first, last = lane == 0, lane == LANES - 1
    left = lane < LANES // 2
    even = lane - 2 * (lane // 2) == 0
    pair_of = lane * 2 - jnp.where(left, 0, LANES)
    half_of = (lane // 2, lane // 2 + LANES // 2)
    y_edge = (first & has_y[0]) | (last & has_y[1])

    def north(v):
        return pltpu.roll(v, LANES - 1, 1)

    def south(v):
        return pltpu.roll(v, 1, 1)

    def take(v, index):
        return jnp.take_along_axis(v, index, axis=1, mode="promise_in_bounds")

    def spread(v, at, rows):
        return jnp.broadcast_to(v[:, at : at + 1], (rows, LANES))

    for t in range(STEPS):
        for i in range(6):
            row = jnp.zeros((1, LANES), f32)
            cn[t, i, low_c : low_c + 1, :] = row
            xc[t, 0, i, low_c : low_c + 1, :] = row
            xc[t, 1, i, low_c : low_c + 1, :] = row
    cor[...] = jnp.zeros(cor.shape, f32)
    gt[...] = jnp.zeros(gt.shape, f32)
    qs[...] = jnp.zeros(qs.shape, f32)
    gs[...] = jnp.zeros(gs.shape, f32)
    jm[...] = jnp.ones(jm.shape, f32)
    for d in range(2):

        @pl.when(jnp.logical_not(has_x[d]))
        def _():
            for t in range(STEPS):
                xf[t, d] = jnp.zeros(xf.shape[2:], f32)
                xc[t, d] = jnp.zeros(xc.shape[2:], f32)
                for f in range(2):
                    xk[t, f, d] = jnp.zeros(xk.shape[3:], f32)
            jx[d] = jnp.ones(jx.shape[1:], f32)

        @pl.when(jnp.logical_not(has_y[d]))
        def _():
            for t in range(STEPS):
                for f in range(2):
                    yr[t, f, d] = jnp.zeros(yr.shape[3:], f32)

    def ridge(t, f):
        for c in range(3):
            i = 3 * f + c
            for y in range(2):
                gs[y, c : c + 1] = (
                    fn[t, 0, i, y, low_f - 1 : low_f, :] + fn[t, 1, i, y, low_f - 1 : low_f, :]
                )
        a, b = gs[0], gs[1]
        a, b = take(a + north(a), pair_of), take(b + north(b), pair_of)
        mean = 0.25 * jnp.where(left, a, b)
        for c in range(3):
            cn[t, 3 * f + c, TOP - 1 : TOP, :] = mean[c : c + 1]

    def copy_top(t, x, i):
        for y in range(2):
            fn[t, x, i, y, TOP - 1 : TOP, :] = fn[t, x, i, y, TOP : TOP + 1, :]

    def pack(t, f):
        wide = lax.broadcasted_iota(jnp.int32, (rows_c, LANES), 1)
        one = lax.broadcasted_iota(jnp.int32, (1, LANES), 1)
        spare = jnp.zeros((1, LANES), f32)
        thin = lax.broadcasted_iota(jnp.int32, (rows_f, LANES), 1)
        out = jnp.zeros((rows_c, LANES), f32)
        fine = jnp.zeros((rows_f, LANES), f32)
        for d in range(2):
            at = (0, LANES - 1)[d]
            for c in range(3):
                i, j = 3 * f + c, 16 * d + (2, 3, 5)[c]
                v = spread(cn[t, i, TOP - 1 : TOP - 1 + rows_c, :], at, rows_c)
                out = jnp.where((wide == j) | (wide == j + 8), v, out)
                for x in range(2):
                    v = spread(fn[t, x, i, d, TOP - 1 : TOP - 1 + rows_f, :], at, rows_f)
                    fine = jnp.where(thin == 16 * d + 8 * x + (0, 1, 4)[c], v, fine)
            j, v = 16 * d, spread(cn[t, 3 * f + 2, TOP : TOP + 1, :], at, 1)
            spare = jnp.where((one == j) | (one == j + 8), v, spare)
            if t == 0 and f == 0:
                for x in range(2):
                    v = jnp.broadcast_to(jm[x, d : d + 1, at : at + 1], (rows_f, LANES))
                    fine = jnp.where(thin == 16 * d + 8 * x + 6, v, fine)
        of_fine = thin - 8 * (thin // 8)
        of_fine = (of_fine < 2) | (of_fine == 4) | (of_fine == 6)
        qs[0:rows_f, :] = jnp.where(of_fine, fine, out[0:rows_f])
        qs[rows_f:rows_c, :] = out[rows_f:]
        qs[LANES - 1 :, :] = spare
        pk[t, f] = jnp.transpose(qs[...])[0:32]

    def begin(f):
        drain(ins.at[f], 12 * fz + 3 * cz + (0 if f else 4))
        for c in range(3):
            i = 3 * f + c
            for x in range(2):
                for y in range(2):
                    fn[0, x, i, y, TOP : TOP + fz, :] = fin[i, pl.ds(2 * y + x, fz, stride=4), :]
                copy_top(0, x, i)
        ridge(0, f)

    begin(0)
    for x in range(2):
        for y in range(2):
            jm[x, y : y + 1] = 1.0 + tp[x : x + 1, y * LANES : (y + 1) * LANES].astype(f32) * (1.0 / 1024.0)
    count = sum(h.astype(jnp.int32) for h in has_x + has_y + tuple(side & (rank < len(share)) for side in outer))
    pl.semaphore_wait(barrier, count)
    each(has_x, lambda d: j_copy(d, 1 - d).start())
    x_send(0, 0, 0, 1)
    pack(0, 0)
    y_send(0, 0)
    begin(1)
    pack(0, 1)
    y_send(0, 1)
    y_wait(0, 0)
    x_send(0, 0, 2)
    x_send(0, 1, 0, 1)
    y_wait(0, 1)
    x_send(0, 1, 2)

    def spacings():
        for q in range(4):
            for y in range(2):
                row = jx[q // 3, y : y + 1] if q in (0, 3) else jm[q - 1, y : y + 1]
                inv = jnp.broadcast_to(1.0 / row, (8, LANES))
                rj[q, y] = inv
                if q in (1, 2):
                    rj2[q - 1, y] = inv * inv
        for x in range(2):
            sides = []
            for s in range(2):
                row = yr[0, 0, s, 8 * x + 6 : 8 * x + 7, 0:1]
                row = jnp.broadcast_to(1.0 / jnp.where(row == 0.0, 1.0, row), (8, LANES))
                rjh[s, x] = row
                sides.append(row)
            rjl[x] = jnp.where(left, sides[0], sides[1])

    def halos(t, f):
        inside = lane <= fz
        for s in range(2):
            own = [yr[t, f, s, 8 * x : 8 * x + 8] for x in range(2)]
            west, east = xk[t, f, 0, s], xk[t, f, 1, s]
            cross = (own[1] - west, east - own[0], east - west)

            def put(k, row):
                at = 2 * k + 1 - s
                gt[at : at + 1, :] = row

            d = north(own[0]) - south(own[0])
            for c in range(3):
                put(c, own[0][(2, 3, 5)[c] :][0:1])
            put(3, cross[2][3:4])
            put(4, cross[2][2:3] + d[5:6])
            put(5, d[3:4])
            for x in range(2):
                v = jnp.where(inside, own[x], 0.0)
                d = (north(v) - south(v)) * rjh[s, x]
                k = 6 + 6 * x
                for c in range(3):
                    put(k + c, own[x][(0, 1, 4)[c] :][0:1])
                put(k + 3, cross[x][1:2])
                put(k + 4, cross[x][0:1] + d[4:5])
                put(k + 5, d[1:2])
        tt[...] = jnp.transpose(gt[...])

    def item(v, k):
        return pltpu.roll(v, LANES - 1 - 2 * k, 1)

    def coarse(t, f, other):
        for v in range(cz // 8):
            r = TOP + 8 * v
            th = tt[8 * v + 1 : 8 * v + 9, :]
            mu = (0.25 * STEP_SQUARED) * sc[8 * v : 8 * v + 8, :]
            both = (0.25 * STEP_SQUARED) * lc[8 * v : 8 * v + 8, :] + mu
            xx, yy, zz, cross, rise, tilt, twice = [], [], [], [], [], [], []
            for c in range(3):
                i = 3 * f + c
                u = cn[t, i, r : r + 8, :]
                e, w = xc[t, 1, i, r : r + 8, :], xc[t, 0, i, r : r + 8, :]
                dn, up = cn[t, i, r + 1 : r + 9, :], cn[t, i, r - 1 : r + 7, :]
                h = item(th, c)
                u2 = 2.0 * u
                twice.append(u2)
                xx.append(e + w - u2)
                yy.append(jnp.where(last, h, north(u)) + jnp.where(first, h, south(u)) - u2)
                zz.append(dn + up - u2)
                cross.append(e - w)
                rise.append(dn - up)
                if c == 1:
                    tilt.append(None)
                else:
                    ed, eu = xc[t, 1, i, r + 1 : r + 9, :], xc[t, 1, i, r - 1 : r + 7, :]
                    wd, wu = xc[t, 0, i, r + 1 : r + 9, :], xc[t, 0, i, r - 1 : r + 7, :]
                    tilt.append((ed - eu) - (wd - wu))
            ac = []
            for k, a in enumerate((cross[1], cross[0] + rise[2], rise[1])):
                h = item(th, 3 + k)
                ac.append(jnp.where(last, h, north(a)) - jnp.where(first, h, south(a)))
            grad = (
                xx[0] + 0.25 * (ac[0] + tilt[2]),
                yy[1] + 0.25 * ac[1],
                zz[2] + 0.25 * (ac[2] + tilt[0]),
            )
            prod = None
            for c in range(3):
                i = 3 * f + c
                before = co[i, 8 * v : 8 * v + 8, :] if t == 0 else cn[t - 1, i, r : r + 8, :]
                new = (twice[c] - before) + (mu * (xx[c] + yy[c] + zz[c]) + both * grad[c])
                if t < STEPS - 1:
                    cn[t + 1, i, r : r + 8, :] = new
                else:
                    cout[i, 8 * v : 8 * v + 8, :] = new
                if other is not None:
                    o = 3 * other + c
                    if t < STEPS - 1:
                        pair = cn[t + 1, o, r : r + 8, :]
                    else:
                        pair = cout[o, 8 * v : 8 * v + 8, :]
                    prod = pair * new if prod is None else prod + pair * new
            if other is not None:
                if t > 0:
                    prod = prod + cker[8 * v : 8 * v + 8, :]
                cker[8 * v : 8 * v + 8, :] = prod

    def ghost(t, f):
        at = (2, 3, 0)
        for c in range(3):
            i = 3 * f + c
            gs[0, at[c] : at[c] + 1] = xc[t, 0, i, TOP : TOP + 1, :]
            gs[1, at[c] : at[c] + 1] = cn[t, i, TOP : TOP + 1, :]
            gs[2, at[c] : at[c] + 1] = xc[t, 1, i, TOP : TOP + 1, :]
        flat = [gs[k] for k in range(3)]
        rim = []
        for tiles in (
            [xk[t, f, 0, s] for s in range(2)],
            [yr[t, f, s, 0:8] for s in range(2)],
            [xk[t, f, 1, s] for s in range(2)],
        ):
            ends = [
                jnp.where(sub == 0, spread(v, LANES - 1, 8), spread(v, 1, 8)) for v in tiles
            ]
            rim.append(jnp.where(left, ends[0], ends[1]))

        def mix(v):
            lo, mid, hi = v
            return (
                0.75 * lo + 0.25 * mid,
                0.75 * mid + 0.25 * lo,
                0.75 * mid + 0.25 * hi,
                0.75 * hi + 0.25 * mid,
            )

        for q, (v, h) in enumerate(zip(mix(flat), mix(rim))):
            a = 0.75 * v + 0.25 * jnp.where(first, h, south(v))
            b = 0.75 * v + 0.25 * jnp.where(last, h, north(v))
            for y in range(2):
                g = jnp.where(even, take(a, half_of[y]), take(b, half_of[y]))
                if q in (0, 3):
                    g = jnp.where(has_x[q // 3], g, 0.0)
                for c in range(3):
                    i = 3 * f + c
                    if q in (0, 3):
                        xf[t, q // 3, i, y, low_f : low_f + 1, :] = g[at[c] : at[c] + 1]
                    else:
                        fn[t, q - 1, i, y, low_f : low_f + 1, :] = g[at[c] : at[c] + 1]
            if q in (1, 2):
                g = jnp.where(y_edge, 0.75 * h + 0.25 * v, 0.0) * rjl[q - 1]
                cor[q - 1, 0, 7:8] = g[0:1]
                cor[q - 1, 1, 7:8] = g[3:4]

    def fine(t, f, other):
        for side in range(2):
            for c in (0, 2):
                for y in range(2):
                    xf[t, side, 3 * f + c, y, TOP - 1 : TOP, :] = xf[
                        t, side, 3 * f + c, y, TOP : TOP + 1, :
                    ]

        def plane(q, i, y, r):
            if q in (0, 3):
                return xf[t, q // 3, i, y, r : r + 8, :]
            return fn[t, q - 1, i, y, r : r + 8, :]

        for v in range(fz // 8):
            r = TOP + 8 * v
            th = tt[8 * v + 1 : 8 * v + 9, :]
            for x in range(2):
                q = x + 1
                xx, yy, zz, up_down, twice = {}, {}, {}, {}, {}
                va = [[None, None] for _ in range(3)]
                tilt = {}
                mid = {}
                for y in range(2):
                    inv = rj[q, y]
                    cross, rise = [], []
                    for c in range(3):
                        i = 3 * f + c
                        u = plane(q, i, y, r)
                        e, w = plane(q + 1, i, y, r), plane(q - 1, i, y, r)
                        dn, up = plane(q, i, y, r + 1), plane(q, i, y, r - 1)
                        mid[c, y] = u
                        u2 = 2.0 * u
                        twice[c, y] = u2
                        xx[c, y] = e + w - u2
                        zz[c, y] = (dn + up - u2) * rj2[x, y]
                        cross.append(e - w)
                        rise.append((dn - up) * inv if c else None)
                        if c != 1:
                            ed, eu = plane(q + 1, i, y, r + 1), plane(q + 1, i, y, r - 1)
                            wd, wu = plane(q - 1, i, y, r + 1), plane(q - 1, i, y, r - 1)
                            tilt[c, y] = (ed - eu) * rj[q + 1, y] - (wd - wu) * rj[q - 1, y]
                    va[0][y] = cross[1]
                    va[1][y] = cross[0] + rise[2]
                    va[2][y] = rise[1]

                def ends(a, b, h):
                    na, nb, sa, sb = north(a), north(b), south(a), south(b)
                    return (
                        (jnp.where(last, nb, na), jnp.where(first, h, sa)),
                        (jnp.where(last, h, nb), jnp.where(first, sa, sb)),
                    )

                k = 6 + 6 * x
                for c in range(3):
                    for y, (n, s) in enumerate(ends(mid[c, 0], mid[c, 1], item(th, k + c))):
                        yy[c, y] = n + s - twice[c, y]
                ac = {}
                for c in range(3):
                    h = item(th, k + 3 + c)
                    if c and v == fz // 8 - 1:
                        h = h + cor[x, c - 1]
                    for y, (n, s) in enumerate(ends(va[c][0], va[c][1], h)):
                        ac[c, y] = n - s
                for y in range(2):
                    pick = pl.ds(32 * v + 2 * y + x, 8, stride=4)
                    mu = STEP_SQUARED * sf[pick, :]
                    both = STEP_SQUARED * lf[pick, :] + mu
                    grad = (
                        xx[0, y] + 0.25 * (ac[0, y] + tilt[2, y]),
                        yy[1, y] + 0.25 * ac[1, y],
                        zz[2, y] + 0.25 * (ac[2, y] + tilt[0, y]),
                    )
                    prod = None
                    for c in range(3):
                        i = 3 * f + c
                        before = fo[i, pick, :] if t == 0 else fn[t - 1, x, i, y, r : r + 8, :]
                        new = (twice[c, y] - before) + (
                            mu * (xx[c, y] + yy[c, y] + zz[c, y]) + both * grad[c]
                        )
                        if t < STEPS - 1:
                            fn[t + 1, x, i, y, r : r + 8, :] = new
                        else:
                            fout[i, pick, :] = new
                        if other is not None:
                            o = 3 * other + c
                            if t < STEPS - 1:
                                pair = fn[t + 1, x, o, y, r : r + 8, :]
                            else:
                                pair = fout[o, pick, :]
                            prod = pair * new if prod is None else prod + pair * new
                    if other is not None:
                        if t > 0:
                            prod = prod + fker[pick, :]
                        fker[pick, :] = prod

    def finish_level(t, f):
        for c in range(3):
            for x in range(2):
                copy_top(t, x, 3 * f + c)
        ridge(t, f)
        x_send(t, f, 0)
        x_send(t, f, 1, where=f == 0 or jnp.logical_not(middle))
        pack(t, f)
        y_send(t, f)

    for t in range(STEPS):
        for n in range(2):
            for m in {(0, 0): (1,), (0, 1): (2, 3), (1, 0): (0,), (1, 1): ()}[t, n]:
                pass_on(t, m)
            if t > 0 and n == 0:
                y_wait(t, 1)
                x_send(t, 1, 2)
                x_send(t, 1, 1, where=middle)
            f = n if t < STEPS - 1 else (turn, 1 - turn)[n]
            other = None if n == 0 else 1 - f
            x_wait(t, f, 0)
            if t == 0 and n == 0:
                spacings()
                drain(ins.at[2], 8 * cz)
            if t > 0 and n == 0:
                pass_on(1, 1)
            halos(t, f)
            coarse(t, f, other)
            if t < STEPS - 1 and n == 1:
                y_wait(t + 1, 0)
                x_send(t + 1, 0, 2)
            ghost(t, f)
            x_wait(t, f, 1)
            if t == 0 and n == 0:
                drain(ins.at[3], 32 * fz)
            fine(t, f, other)
            if t < STEPS - 1:
                finish_level(t + 1, f)

    sent = 8 + 2 * STEPS * (3 * (cz + 1) + 6 * fz + 8)
    each(has_x, lambda d: drain(xs.at[d], sent))
    each(has_y, lambda d: drain(ys.at[d], 32 * STEPS))
    for k, n in enumerate(share):
        taken = [m for r in route for m, least in r.items() if n >= least]
        rows = sum(6 * fz if m % 2 else 3 * (cz + 1) for m in taken)
        pl.when(middle & (rank == k))(functools.partial(drain, vs.at[0], rows))


def put_body(*refs):
    ins, outs, sem = refs[:4], refs[4:8], refs[8]
    copies = [
        pltpu.make_async_copy(a, b, sem.at[i]) for i, (a, b) in enumerate(zip(ins, outs))
    ]
    for copy in copies:
        copy.start()
    for copy in copies:
        copy.wait()


def rows_view(a):
    lead = a.shape[:-3]
    fz, fx, fy = a.shape[-3:]
    n = len(lead)
    a = a.reshape(lead + (fz, fx, fy // LANES, LANES))
    a = a.transpose(tuple(range(n)) + (n, n + 2, n + 1, n + 3))
    return a.reshape(((6,) if lead else ()) + (fz * fx * fy // LANES, LANES))


def rows_back(a, shape):
    lead = shape[:-3]
    fz, fx, fy = shape[-3:]
    n = len(lead)
    a = a.reshape(lead + (fz, fy // LANES, fx, LANES))
    a = a.transpose(tuple(range(n)) + (n, n + 2, n + 1, n + 3))
    return a.reshape(shape)


def on_device(fold, fnow, cold, cnow, shf, laf, shc, lac, topo):
    nx, ny = lax.axis_size("gx"), lax.axis_size("gy")
    fz, fx, fy = shf.shape
    cz, cx, cy = shc.shape
    if fx != 2 or cx != 1 or cy != LANES or fy != 2 * cy or fz % 8 or cz % 8 or cz + 8 > LANES:
        raise ValueError("unsupported tile")
    f32 = jnp.float32
    dma = pltpu.SemaphoreType.DMA
    nrows = fz * fx * fy // LANES
    vm = pl.BlockSpec(memory_space=pltpu.VMEM)
    hbm = pl.BlockSpec(memory_space=pl.ANY)
    shapes = ((6, nrows, LANES), (6, cz, cy), (nrows, LANES), (cz, cy))
    args = (
        rows_view(fold),
        rows_view(fnow),
        cold.reshape(6, cz, cy),
        cnow.reshape(6, cz, cy),
        rows_view(shf),
        rows_view(laf),
        shc.reshape(cz, cy),
        lac.reshape(cz, cy),
        topo,
    )
    inner = pl.pallas_call(
        functools.partial(body, nx, ny, fz, cz),
        out_shape=tuple(pltpu.VMEM(s, f32) for s in shapes),
        in_specs=[hbm] * 9,
        out_specs=(vm,) * 4,
        scratch_shapes=[
            pltpu.VMEM((6, nrows, LANES), f32),
            pltpu.VMEM((6, nrows, LANES), f32),
            pltpu.VMEM((6, cz, cy), f32),
            pltpu.VMEM((nrows, LANES), f32),
            pltpu.VMEM((nrows, LANES), f32),
            pltpu.VMEM((cz, cy), f32),
            pltpu.VMEM((cz, cy), f32),
            pltpu.VMEM((fx, fy), jnp.int32),
            pltpu.VMEM((STEPS, 2, 6, 2, fz + 16, LANES), f32),
            pltpu.VMEM((STEPS, 6, cz + 16, LANES), f32),
            pltpu.VMEM((STEPS, 2, 6, 2, fz + 16, LANES), f32),
            pltpu.VMEM((STEPS, 2, 6, cz + 16, LANES), f32),
            pltpu.VMEM((2, 8, LANES), f32),
            pltpu.VMEM((2, 8, LANES), f32),
            pltpu.VMEM((STEPS, 2, 32, LANES), f32),
            pltpu.VMEM((STEPS, 2, 2, 16, LANES), f32),
            pltpu.VMEM((STEPS, 2, 2, 2, 8, LANES), f32),
            pltpu.VMEM((4, 2, 8, LANES), f32),
            pltpu.VMEM((2, 2, 8, LANES), f32),
            pltpu.VMEM((2, 2, 8, LANES), f32),
            pltpu.VMEM((2, 8, LANES), f32),
            pltpu.VMEM((LANES, LANES), f32),
            pltpu.VMEM((LANES, LANES), f32),
            pltpu.VMEM((LANES, LANES), f32),
            pltpu.VMEM((3, 8, LANES), f32),
            pltpu.VMEM((2, 2, 8, LANES), f32),
            pltpu.VMEM((4 * STEPS * (3 * cz + 6 * fz + 32), LANES), f32),
            pltpu.VMEM((STEPS, 2, 3, 2, fz, LANES), f32),
            pltpu.VMEM((STEPS, 2, 3, cz + 8, LANES), f32),
            dma((4,)),
            dma((2,)),
            dma((STEPS, 2, 2, 2)),
            dma((2,)),
            dma((STEPS, 2, 2)),
            dma((1,)),
            dma((6,)),
        ],
        compiler_params=pltpu.CompilerParams(
            collective_id=0, has_side_effects=True, vmem_limit_bytes=32 << 20
        ),
        name="wave",
    )(*[pltpu.with_memory_space_constraint(a, pltpu.HBM) for a in args])
    fout, cout, fker, cker = pl.pallas_call(
        put_body,
        out_shape=tuple(jax.ShapeDtypeStruct(s, f32) for s in shapes),
        in_specs=[vm] * 4,
        out_specs=(hbm,) * 4,
        scratch_shapes=[dma((4,))],
        compiler_params=pltpu.CompilerParams(vmem_limit_bytes=1 << 20),
        name="put",
    )(*[pltpu.with_memory_space_constraint(a, pltpu.VMEM) for a in inner])
    return (
        rows_back(fout, fold.shape),
        cout.reshape(cold.shape),
        rows_back(fker, shf.shape),
        cker.reshape(shc.shape),
    )


def solution(mesh):
    field, coef = P(None, None, None, "gx", "gy"), P(None, "gx", "gy")
    return jax.shard_map(
        on_device,
        mesh=mesh,
        in_specs=(field,) * 4 + (coef,) * 4 + (P("gx", "gy"),),
        out_specs=(field, field, coef, coef),
        check_vma=False,
    )
```

```python
import functools

import jax
import jax.numpy as jnp
from jax import lax
from jax.experimental import pallas as pl
from jax.experimental.pallas import tpu as pltpu
from jax.sharding import PartitionSpec as P

STEPS = 2
STEP_SQUARED = 0.04
LANES = 128
TOP = 8


def body(
    nx, ny, fz, cz,
    fold, fnow, cold, cnow, shf, laf, shc, lac, topo,
    fout, cout, fker, cker,
    fin, fo, co, sf, lf, sc, lc, tp,
    fn, cn, xf, xc, jm, jx, pk, yr, xk,
    rj, rj2, rjh, rjl, qs, gt, tt, gs, cor, span, via_f, via_c,
    ins, xs, xr, ys, yrs, vs, vr,
):
    f32 = jnp.float32
    gx, gy = lax.axis_index("gx"), lax.axis_index("gy")
    has_x = (gx > 0, gx < nx - 1)
    has_y = (gy > 0, gy < ny - 1)
    rows_c = cz + 8
    rows_f = fz + 8
    low_c, low_f = TOP + cz, TOP + fz

    def each(flags, action):
        for d in range(2):
            pl.when(flags[d])(functools.partial(action, d))

    def half(f):
        return pl.ds(3 * f, 3)

    loads = {
        "f0": (fnow.at[half(0)], fin.at[half(0)]),
        "c0": (cnow.at[half(0)], cn.at[0, half(0), pl.ds(TOP, cz)]),
        "topo": (topo, tp),
        "f1": (fnow.at[half(1)], fin.at[half(1)]),
        "c1": (cnow.at[half(1)], cn.at[0, half(1), pl.ds(TOP, cz)]),
        "co": (cold, co),
        "sc": (shc, sc),
        "lc": (lac, lc),
        "fo": (fold, fo),
        "sf": (shf, sf),
        "lf": (laf, lf),
    }
    slots = {"f0": 0, "c0": 0, "topo": 0, "f1": 1, "c1": 1, "co": 2, "sc": 2, "lc": 2}

    def drain(sem, rows):
        part = span.at[pl.ds(0, rows)]
        pltpu.make_async_copy(part, part, sem).wait()

    planes = nx // 4 if nx % 4 == 0 else 0
    share = [min(3, (8 * (planes - 1 - z) + planes) // (2 * planes)) for z in range(planes - 1)]
    route = (
        (0, 0, 2, 3, 3), (0, 1, 0, 3, 3), (0, 2, 0, 3, 2), (0, 3, 0, 3, 1),
        (1, 0, 0, 1, 3), (1, 0, 1, 3, 2), (1, 1, 0, 3, 1),
    )
    reach = [sum(n >= least for n in share) for *_, least in route]
    at4, plane = lax.rem(gx, 4), gx // 4
    rank = jnp.where((at4 == 1) | (at4 == 3), plane, planes - 1 - plane)
    outer = ((at4 == 0), (at4 == 3))
    middle = (at4 == 1) | (at4 == 2)
    detour = [[outer[d] & (rank < r) for d in range(2)] for r in reach]
    passes = [middle & (rank < r) for r in reach]

    def parts(t, m):
        cut = [(lo, hi, k) for k, (a, b, lo, hi, _) in enumerate(route) if (a, b) == (t, m)]
        at, out = 0, []
        for lo, hi, k in cut + [(3, 3, None)]:
            out += [(at, lo, None)] if at < lo else []
            out += [(lo, hi, k)] if lo < hi else []
            at = hi
        return out
    from_left = at4 == 2
    odd_x = lax.rem(gx, 2) == 1

    barrier = pltpu.get_barrier_semaphore()
    each(has_x, lambda d: pl.semaphore_signal(barrier, inc=1, device_id={"gx": gx + 2 * d - 1}))
    each(has_y, lambda d: pl.semaphore_signal(barrier, inc=1, device_id={"gy": gy + 2 * d - 1}))

    @pl.when(middle & (rank < len(share)))
    def _():
        source = gx + jnp.where(from_left, -2, 2)
        pl.semaphore_signal(barrier, inc=1, device_id={"gx": source})

    for k, (a, b) in loads.items():
        pltpu.make_async_copy(a, b, ins.at[slots.get(k, 3)]).start()

    def x_copy(t, f, kind, d, land, lo=0, hi=3):
        some = pl.ds(3 * f + lo, hi - lo)
        if kind == 0:
            rows = pl.ds(TOP - 1, cz + 1)
            src, dst = cn.at[t, some, rows], xc.at[t, land, some, rows]
        elif kind == 1:
            rows = pl.ds(TOP, fz)
            src, dst = fn.at[t, d, some, :, rows], xf.at[t, land, some, :, rows]
        else:
            src, dst = yr.at[t, f, :, pl.ds(8 * d, 4)], xk.at[t, f, land, :, pl.ds(0, 4)]
        return pltpu.make_async_remote_copy(
            src, dst, xs.at[d], xr.at[t, f, kind % 2, land], device_id={"gx": gx + 2 * d - 1}
        )

    def ends_of(k, d, land):
        t, m, lo, hi, _ = route[k]
        some = pl.ds(3 * (m // 2) + lo, hi - lo)
        if m % 2 == 0:
            rows, stop = pl.ds(TOP - 1, cz + 1), via_c.at[t, m // 2, pl.ds(lo, hi - lo), pl.ds(0, cz + 1)]
            return cn.at[t, some, rows], stop, xc.at[t, land, some, rows]
        rows, stop = pl.ds(TOP, fz), via_f.at[t, m // 2, pl.ds(lo, hi - lo)]
        return fn.at[t, d, some, :, rows], stop, xf.at[t, land, some, :, rows]

    def detour_copy(k, d):
        src, stop, _ = ends_of(k, d, 0)
        return pltpu.make_async_remote_copy(
            src, stop, xs.at[d], vr.at[k], device_id={"gx": gx + 2 - 4 * d}
        )

    def pass_copy(k, land):
        t, m, *_ = route[k]
        _, stop, dst = ends_of(k, 0, land)
        return pltpu.make_async_remote_copy(
            stop, dst, vs.at[0], xr.at[t, m // 2, m % 2, land],
            device_id={"gx": gx + 3 - 6 * land},
        )

    def pass_on(t, m):
        for k, (a, b, *_) in enumerate(route):
            if (a, b) == (t, m):

                @pl.when(passes[k])
                def _():
                    _, stop, _ = ends_of(k, 0, 0)
                    pltpu.make_async_copy(stop, stop, vr.at[k]).wait()
                    for land in range(2):
                        pl.when(at4 == 1 + land)(pass_copy(k, land).start)

    def y_copy(t, f, d, land):
        return pltpu.make_async_remote_copy(
            pk.at[t, f, pl.ds(16 * d, 16)], yr.at[t, f, land], ys.at[d], yrs.at[t, f, land],
            device_id={"gy": gy + 2 * d - 1},
        )

    def j_copy(d, land):
        return pltpu.make_async_remote_copy(
            jm.at[d], jx.at[land], xs.at[d], xr.at[0, 0, 0, land], device_id={"gx": gx + 2 * d - 1}
        )

    def x_send(t, f, *kinds, where=True):
        def go(d):
            for kind in kinds:
                if kind == 2:
                    x_copy(t, f, kind, d, 1 - d).start()
                    continue
                for lo, hi, k in parts(t, 2 * f + kind):
                    copy = x_copy(t, f, kind, d, 1 - d, lo, hi)
                    if k is None:
                        copy.start()
                    else:
                        pl.when(detour[k][d])(detour_copy(k, d).start)
                        pl.when(jnp.logical_not(detour[k][d]))(copy.start)

        pl.when(has_x[1] & odd_x & where)(functools.partial(go, 1))
        pl.when(has_x[0] & where)(functools.partial(go, 0))
        pl.when(has_x[1] & jnp.logical_not(odd_x) & where)(functools.partial(go, 1))

    def x_wait(t, f, kind):
        rows = 6 * fz if kind else 3 * (cz + 1) + 8 + (8 if t == 0 and f == 0 else 0)
        each(has_x, lambda d: drain(xr.at[t, f, kind, d], rows))

    def y_send(t, f):
        each(has_y, lambda d: y_copy(t, f, d, 1 - d).start())

    def y_wait(t, f):
        each(has_y, lambda d: y_copy(t, f, d, d).wait_recv())

    lane = lax.broadcasted_iota(jnp.int32, (8, LANES), 1)
    sub = lax.broadcasted_iota(jnp.int32, (8, LANES), 0)
    first, last = lane == 0, lane == LANES - 1
    left = lane < LANES // 2
    even = lane - 2 * (lane // 2) == 0
    pair_of = lane * 2 - jnp.where(left, 0, LANES)
    half_of = (lane // 2, lane // 2 + LANES // 2)
    y_edge = (first & has_y[0]) | (last & has_y[1])

    def north(v):
        return pltpu.roll(v, LANES - 1, 1)

    def south(v):
        return pltpu.roll(v, 1, 1)

    def take(v, index):
        return jnp.take_along_axis(v, index, axis=1, mode="promise_in_bounds")

    def spread(v, at, rows):
        return jnp.broadcast_to(v[:, at : at + 1], (rows, LANES))

    for t in range(STEPS):
        for i in range(6):
            row = jnp.zeros((1, LANES), f32)
            cn[t, i, low_c : low_c + 1, :] = row
            xc[t, 0, i, low_c : low_c + 1, :] = row
            xc[t, 1, i, low_c : low_c + 1, :] = row
    cor[...] = jnp.zeros(cor.shape, f32)
    gt[...] = jnp.zeros(gt.shape, f32)
    qs[...] = jnp.zeros(qs.shape, f32)
    gs[...] = jnp.zeros(gs.shape, f32)
    jm[...] = jnp.ones(jm.shape, f32)
    for d in range(2):

        @pl.when(jnp.logical_not(has_x[d]))
        def _():
            for t in range(STEPS):
                xf[t, d] = jnp.zeros(xf.shape[2:], f32)
                xc[t, d] = jnp.zeros(xc.shape[2:], f32)
                for f in range(2):
                    xk[t, f, d] = jnp.zeros(xk.shape[3:], f32)
            jx[d] = jnp.ones(jx.shape[1:], f32)

        @pl.when(jnp.logical_not(has_y[d]))
        def _():
            for t in range(STEPS):
                for f in range(2):
                    yr[t, f, d] = jnp.zeros(yr.shape[3:], f32)

    def ridge(t, f):
        for c in range(3):
            i = 3 * f + c
            for y in range(2):
                gs[y, c : c + 1] = (
                    fn[t, 0, i, y, low_f - 1 : low_f, :] + fn[t, 1, i, y, low_f - 1 : low_f, :]
                )
        a, b = gs[0], gs[1]
        a, b = take(a + north(a), pair_of), take(b + north(b), pair_of)
        mean = 0.25 * jnp.where(left, a, b)
        for c in range(3):
            cn[t, 3 * f + c, TOP - 1 : TOP, :] = mean[c : c + 1]

    def copy_top(t, x, i):
        for y in range(2):
            fn[t, x, i, y, TOP - 1 : TOP, :] = fn[t, x, i, y, TOP : TOP + 1, :]

    def pack(t, f):
        wide = lax.broadcasted_iota(jnp.int32, (rows_c, LANES), 1)
        one = lax.broadcasted_iota(jnp.int32, (1, LANES), 1)
        spare = jnp.zeros((1, LANES), f32)
        thin = lax.broadcasted_iota(jnp.int32, (rows_f, LANES), 1)
        out = jnp.zeros((rows_c, LANES), f32)
        fine = jnp.zeros((rows_f, LANES), f32)
        for d in range(2):
            at = (0, LANES - 1)[d]
            for c in range(3):
                i, j = 3 * f + c, 16 * d + (2, 3, 5)[c]
                v = spread(cn[t, i, TOP - 1 : TOP - 1 + rows_c, :], at, rows_c)
                out = jnp.where((wide == j) | (wide == j + 8), v, out)
                for x in range(2):
                    v = spread(fn[t, x, i, d, TOP - 1 : TOP - 1 + rows_f, :], at, rows_f)
                    fine = jnp.where(thin == 16 * d + 8 * x + (0, 1, 4)[c], v, fine)
            j, v = 16 * d, spread(cn[t, 3 * f + 2, TOP : TOP + 1, :], at, 1)
            spare = jnp.where((one == j) | (one == j + 8), v, spare)
            if t == 0 and f == 0:
                for x in range(2):
                    v = jnp.broadcast_to(jm[x, d : d + 1, at : at + 1], (rows_f, LANES))
                    fine = jnp.where(thin == 16 * d + 8 * x + 6, v, fine)
        of_fine = thin - 8 * (thin // 8)
        of_fine = (of_fine < 2) | (of_fine == 4) | (of_fine == 6)
        qs[0:rows_f, :] = jnp.where(of_fine, fine, out[0:rows_f])
        qs[rows_f:rows_c, :] = out[rows_f:]
        qs[LANES - 1 :, :] = spare
        pk[t, f] = jnp.transpose(qs[...])[0:32]

    def begin(f):
        drain(ins.at[f], 12 * fz + 3 * cz + (0 if f else 4))
        for c in range(3):
            i = 3 * f + c
            for x in range(2):
                for y in range(2):
                    fn[0, x, i, y, TOP : TOP + fz, :] = fin[i, pl.ds(2 * y + x, fz, stride=4), :]
                copy_top(0, x, i)
        ridge(0, f)

    begin(0)
    for x in range(2):
        for y in range(2):
            jm[x, y : y + 1] = 1.0 + tp[x : x + 1, y * LANES : (y + 1) * LANES].astype(f32) * (1.0 / 1024.0)
    count = sum(h.astype(jnp.int32) for h in has_x + has_y + tuple(side & (rank < len(share)) for side in outer))
    pl.semaphore_wait(barrier, count)
    each(has_x, lambda d: j_copy(d, 1 - d).start())
    x_send(0, 0, 0, 1)
    pack(0, 0)
    y_send(0, 0)
    begin(1)
    pack(0, 1)
    y_send(0, 1)
    y_wait(0, 0)
    x_send(0, 0, 2)
    x_send(0, 1, 0, 1)
    y_wait(0, 1)
    x_send(0, 1, 2)

    def spacings():
        for q in range(4):
            for y in range(2):
                row = jx[q // 3, y : y + 1] if q in (0, 3) else jm[q - 1, y : y + 1]
                inv = jnp.broadcast_to(1.0 / row, (8, LANES))
                rj[q, y] = inv
                if q in (1, 2):
                    rj2[q - 1, y] = inv * inv
        for x in range(2):
            sides = []
            for s in range(2):
                row = yr[0, 0, s, 8 * x + 6 : 8 * x + 7, 0:1]
                row = jnp.broadcast_to(1.0 / jnp.where(row == 0.0, 1.0, row), (8, LANES))
                rjh[s, x] = row
                sides.append(row)
            rjl[x] = jnp.where(left, sides[0], sides[1])

    def halos(t, f):
        inside = lane <= fz
        for s in range(2):
            own = [yr[t, f, s, 8 * x : 8 * x + 8] for x in range(2)]
            west, east = xk[t, f, 0, s], xk[t, f, 1, s]
            cross = (own[1] - west, east - own[0], east - west)

            def put(k, row):
                at = 2 * k + 1 - s
                gt[at : at + 1, :] = row

            d = north(own[0]) - south(own[0])
            for c in range(3):
                put(c, own[0][(2, 3, 5)[c] :][0:1])
            put(3, cross[2][3:4])
            put(4, cross[2][2:3] + d[5:6])
            put(5, d[3:4])
            for x in range(2):
                v = jnp.where(inside, own[x], 0.0)
                d = (north(v) - south(v)) * rjh[s, x]
                k = 6 + 6 * x
                for c in range(3):
                    put(k + c, own[x][(0, 1, 4)[c] :][0:1])
                put(k + 3, cross[x][1:2])
                put(k + 4, cross[x][0:1] + d[4:5])
                put(k + 5, d[1:2])
        tt[...] = jnp.transpose(gt[...])

    def item(v, k):
        return pltpu.roll(v, LANES - 1 - 2 * k, 1)

    def coarse(t, f, other):
        for v in range(cz // 8):
            r = TOP + 8 * v
            th = tt[8 * v + 1 : 8 * v + 9, :]
            mu = (0.25 * STEP_SQUARED) * sc[8 * v : 8 * v + 8, :]
            both = (0.25 * STEP_SQUARED) * lc[8 * v : 8 * v + 8, :] + mu
            xx, yy, zz, cross, rise, tilt, twice = [], [], [], [], [], [], []
            for c in range(3):
                i = 3 * f + c
                u = cn[t, i, r : r + 8, :]
                e, w = xc[t, 1, i, r : r + 8, :], xc[t, 0, i, r : r + 8, :]
                dn, up = cn[t, i, r + 1 : r + 9, :], cn[t, i, r - 1 : r + 7, :]
                h = item(th, c)
                u2 = 2.0 * u
                twice.append(u2)
                xx.append(e + w - u2)
                yy.append(jnp.where(last, h, north(u)) + jnp.where(first, h, south(u)) - u2)
                zz.append(dn + up - u2)
                cross.append(e - w)
                rise.append(dn - up)
                if c == 1:
                    tilt.append(None)
                else:
                    ed, eu = xc[t, 1, i, r + 1 : r + 9, :], xc[t, 1, i, r - 1 : r + 7, :]
                    wd, wu = xc[t, 0, i, r + 1 : r + 9, :], xc[t, 0, i, r - 1 : r + 7, :]
                    tilt.append((ed - eu) - (wd - wu))
            ac = []
            for k, a in enumerate((cross[1], cross[0] + rise[2], rise[1])):
                h = item(th, 3 + k)
                ac.append(jnp.where(last, h, north(a)) - jnp.where(first, h, south(a)))
            grad = (
                xx[0] + 0.25 * (ac[0] + tilt[2]),
                yy[1] + 0.25 * ac[1],
                zz[2] + 0.25 * (ac[2] + tilt[0]),
            )
            prod = None
            for c in range(3):
                i = 3 * f + c
                before = co[i, 8 * v : 8 * v + 8, :] if t == 0 else cn[t - 1, i, r : r + 8, :]
                new = (twice[c] - before) + (mu * (xx[c] + yy[c] + zz[c]) + both * grad[c])
                if t < STEPS - 1:
                    cn[t + 1, i, r : r + 8, :] = new
                else:
                    cout[i, 8 * v : 8 * v + 8, :] = new
                if other is not None:
                    o = 3 * other + c
                    if t < STEPS - 1:
                        pair = cn[t + 1, o, r : r + 8, :]
                    else:
                        pair = cout[o, 8 * v : 8 * v + 8, :]
                    prod = pair * new if prod is None else prod + pair * new
            if other is not None:
                if t > 0:
                    prod = prod + cker[8 * v : 8 * v + 8, :]
                cker[8 * v : 8 * v + 8, :] = prod

    def ghost(t, f):
        at = (2, 3, 0)
        for c in range(3):
            i = 3 * f + c
            gs[0, at[c] : at[c] + 1] = xc[t, 0, i, TOP : TOP + 1, :]
            gs[1, at[c] : at[c] + 1] = cn[t, i, TOP : TOP + 1, :]
            gs[2, at[c] : at[c] + 1] = xc[t, 1, i, TOP : TOP + 1, :]
        flat = [gs[k] for k in range(3)]
        rim = []
        for tiles in (
            [xk[t, f, 0, s] for s in range(2)],
            [yr[t, f, s, 0:8] for s in range(2)],
            [xk[t, f, 1, s] for s in range(2)],
        ):
            ends = [
                jnp.where(sub == 0, spread(v, LANES - 1, 8), spread(v, 1, 8)) for v in tiles
            ]
            rim.append(jnp.where(left, ends[0], ends[1]))

        def mix(v):
            lo, mid, hi = v
            return (
                0.75 * lo + 0.25 * mid,
                0.75 * mid + 0.25 * lo,
                0.75 * mid + 0.25 * hi,
                0.75 * hi + 0.25 * mid,
            )

        for q, (v, h) in enumerate(zip(mix(flat), mix(rim))):
            a = 0.75 * v + 0.25 * jnp.where(first, h, south(v))
            b = 0.75 * v + 0.25 * jnp.where(last, h, north(v))
            for y in range(2):
                g = jnp.where(even, take(a, half_of[y]), take(b, half_of[y]))
                if q in (0, 3):
                    g = jnp.where(has_x[q // 3], g, 0.0)
                for c in range(3):
                    i = 3 * f + c
                    if q in (0, 3):
                        xf[t, q // 3, i, y, low_f : low_f + 1, :] = g[at[c] : at[c] + 1]
                    else:
                        fn[t, q - 1, i, y, low_f : low_f + 1, :] = g[at[c] : at[c] + 1]
            if q in (1, 2):
                g = jnp.where(y_edge, 0.75 * h + 0.25 * v, 0.0) * rjl[q - 1]
                cor[q - 1, 0, 7:8] = g[0:1]
                cor[q - 1, 1, 7:8] = g[3:4]

    def fine(t, f, other):
        for side in range(2):
            for c in (0, 2):
                for y in range(2):
                    xf[t, side, 3 * f + c, y, TOP - 1 : TOP, :] = xf[
                        t, side, 3 * f + c, y, TOP : TOP + 1, :
                    ]

        def plane(q, i, y, r):
            if q in (0, 3):
                return xf[t, q // 3, i, y, r : r + 8, :]
            return fn[t, q - 1, i, y, r : r + 8, :]

        for v in range(fz // 8):
            r = TOP + 8 * v
            th = tt[8 * v + 1 : 8 * v + 9, :]
            for x in range(2):
                q = x + 1
                xx, yy, zz, up_down, twice = {}, {}, {}, {}, {}
                va = [[None, None] for _ in range(3)]
                tilt = {}
                mid = {}
                for y in range(2):
                    inv = rj[q, y]
                    cross, rise = [], []
                    for c in range(3):
                        i = 3 * f + c
                        u = plane(q, i, y, r)
                        e, w = plane(q + 1, i, y, r), plane(q - 1, i, y, r)
                        dn, up = plane(q, i, y, r + 1), plane(q, i, y, r - 1)
                        mid[c, y] = u
                        u2 = 2.0 * u
                        twice[c, y] = u2
                        xx[c, y] = e + w - u2
                        zz[c, y] = (dn + up - u2) * rj2[x, y]
                        cross.append(e - w)
                        rise.append((dn - up) * inv if c else None)
                        if c != 1:
                            ed, eu = plane(q + 1, i, y, r + 1), plane(q + 1, i, y, r - 1)
                            wd, wu = plane(q - 1, i, y, r + 1), plane(q - 1, i, y, r - 1)
                            tilt[c, y] = (ed - eu) * rj[q + 1, y] - (wd - wu) * rj[q - 1, y]
                    va[0][y] = cross[1]
                    va[1][y] = cross[0] + rise[2]
                    va[2][y] = rise[1]

                def ends(a, b, h):
                    na, nb, sa, sb = north(a), north(b), south(a), south(b)
                    return (
                        (jnp.where(last, nb, na), jnp.where(first, h, sa)),
                        (jnp.where(last, h, nb), jnp.where(first, sa, sb)),
                    )

                k = 6 + 6 * x
                for c in range(3):
                    for y, (n, s) in enumerate(ends(mid[c, 0], mid[c, 1], item(th, k + c))):
                        yy[c, y] = n + s - twice[c, y]
                ac = {}
                for c in range(3):
                    h = item(th, k + 3 + c)
                    if c and v == fz // 8 - 1:
                        h = h + cor[x, c - 1]
                    for y, (n, s) in enumerate(ends(va[c][0], va[c][1], h)):
                        ac[c, y] = n - s
                for y in range(2):
                    pick = pl.ds(32 * v + 2 * y + x, 8, stride=4)
                    mu = STEP_SQUARED * sf[pick, :]
                    both = STEP_SQUARED * lf[pick, :] + mu
                    grad = (
                        xx[0, y] + 0.25 * (ac[0, y] + tilt[2, y]),
                        yy[1, y] + 0.25 * ac[1, y],
                        zz[2, y] + 0.25 * (ac[2, y] + tilt[0, y]),
                    )
                    prod = None
                    for c in range(3):
                        i = 3 * f + c
                        before = fo[i, pick, :] if t == 0 else fn[t - 1, x, i, y, r : r + 8, :]
                        new = (twice[c, y] - before) + (
                            mu * (xx[c, y] + yy[c, y] + zz[c, y]) + both * grad[c]
                        )
                        if t < STEPS - 1:
                            fn[t + 1, x, i, y, r : r + 8, :] = new
                        else:
                            fout[i, pick, :] = new
                        if other is not None:
                            o = 3 * other + c
                            if t < STEPS - 1:
                                pair = fn[t + 1, x, o, y, r : r + 8, :]
                            else:
                                pair = fout[o, pick, :]
                            prod = pair * new if prod is None else prod + pair * new
                    if other is not None:
                        if t > 0:
                            prod = prod + fker[pick, :]
                        fker[pick, :] = prod

    def finish_level(t, f):
        for c in range(3):
            for x in range(2):
                copy_top(t, x, 3 * f + c)
        ridge(t, f)
        x_send(t, f, 0)
        x_send(t, f, 1, where=f == 0 or jnp.logical_not(middle))
        pack(t, f)
        y_send(t, f)

    for t in range(STEPS):
        for n in range(2):
            for m in {(0, 0): (0, 1), (0, 1): (2, 3), (1, 0): (0,), (1, 1): ()}[t, n]:
                pass_on(t, m)
            if t > 0 and n == 0:
                y_wait(t, 1)
                x_send(t, 1, 2)
                x_send(t, 1, 1, where=middle)
                pass_on(1, 1)
            f, other = n, None if n == 0 else 0
            x_wait(t, f, 0)
            if t == 0 and n == 0:
                spacings()
                drain(ins.at[2], 8 * cz)
            halos(t, f)
            coarse(t, f, other)
            if t < STEPS - 1 and n == 1:
                y_wait(t + 1, 0)
                x_send(t + 1, 0, 2)
            ghost(t, f)
            x_wait(t, f, 1)
            if t == 0 and n == 0:
                drain(ins.at[3], 32 * fz)
            fine(t, f, other)
            if t < STEPS - 1:
                finish_level(t + 1, f)

    sent = 8 + 2 * STEPS * (3 * (cz + 1) + 6 * fz + 8)
    each(has_x, lambda d: drain(xs.at[d], sent))
    each(has_y, lambda d: drain(ys.at[d], 32 * STEPS))
    for k, n in enumerate(share):
        rows = sum(
            (hi - lo) * (2 * fz if m % 2 else cz + 1) for _, m, lo, hi, least in route if n >= least
        )
        pl.when(middle & (rank == k))(functools.partial(drain, vs.at[0], rows))


def put_body(*refs):
    ins, outs, sem = refs[:4], refs[4:8], refs[8]
    copies = [
        pltpu.make_async_copy(a, b, sem.at[i]) for i, (a, b) in enumerate(zip(ins, outs))
    ]
    for copy in copies:
        copy.start()
    for copy in copies:
        copy.wait()


def rows_view(a):
    lead = a.shape[:-3]
    fz, fx, fy = a.shape[-3:]
    n = len(lead)
    a = a.reshape(lead + (fz, fx, fy // LANES, LANES))
    a = a.transpose(tuple(range(n)) + (n, n + 2, n + 1, n + 3))
    return a.reshape(((6,) if lead else ()) + (fz * fx * fy // LANES, LANES))


def rows_back(a, shape):
    lead = shape[:-3]
    fz, fx, fy = shape[-3:]
    n = len(lead)
    a = a.reshape(lead + (fz, fy // LANES, fx, LANES))
    a = a.transpose(tuple(range(n)) + (n, n + 2, n + 1, n + 3))
    return a.reshape(shape)


def on_device(fold, fnow, cold, cnow, shf, laf, shc, lac, topo):
    nx, ny = lax.axis_size("gx"), lax.axis_size("gy")
    fz, fx, fy = shf.shape
    cz, cx, cy = shc.shape
    if fx != 2 or cx != 1 or cy != LANES or fy != 2 * cy or fz % 8 or cz % 8 or cz + 8 > LANES:
        raise ValueError("unsupported tile")
    f32 = jnp.float32
    dma = pltpu.SemaphoreType.DMA
    nrows = fz * fx * fy // LANES
    vm = pl.BlockSpec(memory_space=pltpu.VMEM)
    hbm = pl.BlockSpec(memory_space=pl.ANY)
    shapes = ((6, nrows, LANES), (6, cz, cy), (nrows, LANES), (cz, cy))
    args = (
        rows_view(fold),
        rows_view(fnow),
        cold.reshape(6, cz, cy),
        cnow.reshape(6, cz, cy),
        rows_view(shf),
        rows_view(laf),
        shc.reshape(cz, cy),
        lac.reshape(cz, cy),
        topo,
    )
    inner = pl.pallas_call(
        functools.partial(body, nx, ny, fz, cz),
        out_shape=tuple(pltpu.VMEM(s, f32) for s in shapes),
        in_specs=[hbm] * 9,
        out_specs=(vm,) * 4,
        scratch_shapes=[
            pltpu.VMEM((6, nrows, LANES), f32),
            pltpu.VMEM((6, nrows, LANES), f32),
            pltpu.VMEM((6, cz, cy), f32),
            pltpu.VMEM((nrows, LANES), f32),
            pltpu.VMEM((nrows, LANES), f32),
            pltpu.VMEM((cz, cy), f32),
            pltpu.VMEM((cz, cy), f32),
            pltpu.VMEM((fx, fy), jnp.int32),
            pltpu.VMEM((STEPS, 2, 6, 2, fz + 16, LANES), f32),
            pltpu.VMEM((STEPS, 6, cz + 16, LANES), f32),
            pltpu.VMEM((STEPS, 2, 6, 2, fz + 16, LANES), f32),
            pltpu.VMEM((STEPS, 2, 6, cz + 16, LANES), f32),
            pltpu.VMEM((2, 8, LANES), f32),
            pltpu.VMEM((2, 8, LANES), f32),
            pltpu.VMEM((STEPS, 2, 32, LANES), f32),
            pltpu.VMEM((STEPS, 2, 2, 16, LANES), f32),
            pltpu.VMEM((STEPS, 2, 2, 2, 8, LANES), f32),
            pltpu.VMEM((4, 2, 8, LANES), f32),
            pltpu.VMEM((2, 2, 8, LANES), f32),
            pltpu.VMEM((2, 2, 8, LANES), f32),
            pltpu.VMEM((2, 8, LANES), f32),
            pltpu.VMEM((LANES, LANES), f32),
            pltpu.VMEM((LANES, LANES), f32),
            pltpu.VMEM((LANES, LANES), f32),
            pltpu.VMEM((3, 8, LANES), f32),
            pltpu.VMEM((2, 2, 8, LANES), f32),
            pltpu.VMEM((4 * STEPS * (3 * cz + 6 * fz + 32), LANES), f32),
            pltpu.VMEM((STEPS, 2, 3, 2, fz, LANES), f32),
            pltpu.VMEM((STEPS, 2, 3, cz + 8, LANES), f32),
            dma((4,)),
            dma((2,)),
            dma((STEPS, 2, 2, 2)),
            dma((2,)),
            dma((STEPS, 2, 2)),
            dma((1,)),
            dma((7,)),
        ],
        compiler_params=pltpu.CompilerParams(
            collective_id=0, has_side_effects=True, vmem_limit_bytes=32 << 20
        ),
        name="wave",
    )(*[pltpu.with_memory_space_constraint(a, pltpu.HBM) for a in args])
    fout, cout, fker, cker = pl.pallas_call(
        put_body,
        out_shape=tuple(jax.ShapeDtypeStruct(s, f32) for s in shapes),
        in_specs=[vm] * 4,
        out_specs=(hbm,) * 4,
        scratch_shapes=[dma((4,))],
        compiler_params=pltpu.CompilerParams(vmem_limit_bytes=1 << 20),
        name="put",
    )(*[pltpu.with_memory_space_constraint(a, pltpu.VMEM) for a in inner])
    return (
        rows_back(fout, fold.shape),
        cout.reshape(cold.shape),
        rows_back(fker, shf.shape),
        cker.reshape(shc.shape),
    )


def solution(mesh):
    field, coef = P(None, None, None, "gx", "gy"), P(None, "gx", "gy")
    return jax.shard_map(
        on_device,
        mesh=mesh,
        in_specs=(field,) * 4 + (coef,) * 4 + (P("gx", "gy"),),
        out_specs=(field, field, coef, coef),
        check_vma=False,
    )
```

```python
import functools

import jax
import jax.numpy as jnp
from jax import lax
from jax.experimental import pallas as pl
from jax.experimental.pallas import tpu as pltpu
from jax.sharding import PartitionSpec as P

STEPS = 2
STEP_SQUARED = 0.04
LANES = 128
TOP = 8


def body(
    nx, ny, fz, cz,
    fold, fnow, cold, cnow, shf, laf, shc, lac, topo,
    fout, cout, fker, cker, fn, xf, tt, rj, rj2, cor, sf, lf,
    fin, fo, co, sc, lc, tp,
    cn, xc, jm, jx, pk, yr, xk,
    rjh, rjl, qs, gt, gs, span, via_f, via_c,
    ins, xs, xr, ys, yrs, vs, vr,
):
    f32 = jnp.float32
    gx, gy = lax.axis_index("gx"), lax.axis_index("gy")
    has_x = (gx > 0, gx < nx - 1)
    has_y = (gy > 0, gy < ny - 1)
    rows_c = cz + 8
    rows_f = fz + 8
    low_c, low_f = TOP + cz, TOP + fz

    def each(flags, action):
        for d in range(2):
            pl.when(flags[d])(functools.partial(action, d))

    def half(f):
        return pl.ds(3 * f, 3)

    loads = {
        "f0": (fnow.at[half(0)], fin.at[half(0)]),
        "c0": (cnow.at[half(0)], cn.at[0, half(0), pl.ds(TOP, cz)]),
        "topo": (topo, tp),
        "f1": (fnow.at[half(1)], fin.at[half(1)]),
        "c1": (cnow.at[half(1)], cn.at[0, half(1), pl.ds(TOP, cz)]),
        "co": (cold, co),
        "sc": (shc, sc),
        "lc": (lac, lc),
        "fo": (fold, fo),
        "sf": (shf, sf),
        "lf": (laf, lf),
    }
    slots = {"f0": 0, "c0": 0, "topo": 0, "f1": 1, "c1": 1, "co": 2, "sc": 2, "lc": 2}

    def drain(sem, rows):
        part = span.at[pl.ds(0, rows)]
        pltpu.make_async_copy(part, part, sem).wait()

    planes = nx // 4 if nx % 4 == 0 else 0
    share = [min(3, (8 * (planes - 1 - z) + planes) // (2 * planes)) for z in range(planes - 1)]
    route = (
        (0, 0, 2, 3, 3), (0, 1, 0, 3, 3), (0, 2, 0, 3, 2), (0, 3, 0, 3, 1),
        (1, 0, 0, 1, 3), (1, 0, 1, 3, 2), (1, 1, 0, 3, 1),
    )
    reach = [sum(n >= least for n in share) for *_, least in route]
    at4, plane = lax.rem(gx, 4), gx // 4
    rank = jnp.where((at4 == 1) | (at4 == 3), plane, planes - 1 - plane)
    outer = ((at4 == 0), (at4 == 3))
    middle = (at4 == 1) | (at4 == 2)
    detour = [[outer[d] & (rank < r) for d in range(2)] for r in reach]
    passes = [middle & (rank < r) for r in reach]

    def parts(t, m):
        cut = [(lo, hi, k) for k, (a, b, lo, hi, _) in enumerate(route) if (a, b) == (t, m)]
        at, out = 0, []
        for lo, hi, k in cut + [(3, 3, None)]:
            out += [(at, lo, None)] if at < lo else []
            out += [(lo, hi, k)] if lo < hi else []
            at = hi
        return out
    from_left = at4 == 2
    odd_x = lax.rem(gx, 2) == 1

    barrier = pltpu.get_barrier_semaphore()
    each(has_x, lambda d: pl.semaphore_signal(barrier, inc=1, device_id={"gx": gx + 2 * d - 1}))
    each(has_y, lambda d: pl.semaphore_signal(barrier, inc=1, device_id={"gy": gy + 2 * d - 1}))

    @pl.when(middle & (rank < len(share)))
    def _():
        source = gx + jnp.where(from_left, -2, 2)
        pl.semaphore_signal(barrier, inc=1, device_id={"gx": source})

    for k, (a, b) in loads.items():
        pltpu.make_async_copy(a, b, ins.at[slots.get(k, 3)]).start()

    def x_copy(t, f, kind, d, land, lo=0, hi=3):
        some = pl.ds(3 * f + lo, hi - lo)
        if kind == 0:
            rows = pl.ds(TOP - 1, cz + 1)
            src, dst = cn.at[t, some, rows], xc.at[t, land, some, rows]
        elif kind == 1:
            rows = pl.ds(TOP, fz)
            src, dst = fn.at[t, d, some, :, rows], xf.at[t, land, some, :, rows]
        else:
            src, dst = yr.at[t, f, :, pl.ds(8 * d, 4)], xk.at[t, f, land, :, pl.ds(0, 4)]
        return pltpu.make_async_remote_copy(
            src, dst, xs.at[d], xr.at[t, f, kind % 2, land], device_id={"gx": gx + 2 * d - 1}
        )

    def ends_of(k, d, land):
        t, m, lo, hi, _ = route[k]
        some = pl.ds(3 * (m // 2) + lo, hi - lo)
        if m % 2 == 0:
            rows, stop = pl.ds(TOP - 1, cz + 1), via_c.at[t, m // 2, pl.ds(lo, hi - lo), pl.ds(0, cz + 1)]
            return cn.at[t, some, rows], stop, xc.at[t, land, some, rows]
        rows, stop = pl.ds(TOP, fz), via_f.at[t, m // 2, pl.ds(lo, hi - lo)]
        return fn.at[t, d, some, :, rows], stop, xf.at[t, land, some, :, rows]

    def detour_copy(k, d):
        src, stop, _ = ends_of(k, d, 0)
        return pltpu.make_async_remote_copy(
            src, stop, xs.at[d], vr.at[k], device_id={"gx": gx + 2 - 4 * d}
        )

    def pass_copy(k, land):
        t, m, *_ = route[k]
        _, stop, dst = ends_of(k, 0, land)
        return pltpu.make_async_remote_copy(
            stop, dst, vs.at[0], xr.at[t, m // 2, m % 2, land],
            device_id={"gx": gx + 3 - 6 * land},
        )

    def pass_on(t, m):
        for k, (a, b, *_) in enumerate(route):
            if (a, b) == (t, m):

                @pl.when(passes[k])
                def _():
                    _, stop, _ = ends_of(k, 0, 0)
                    pltpu.make_async_copy(stop, stop, vr.at[k]).wait()
                    for land in range(2):
                        pl.when(at4 == 1 + land)(pass_copy(k, land).start)

    def y_copy(t, f, d, land):
        return pltpu.make_async_remote_copy(
            pk.at[t, f, pl.ds(16 * d, 16)], yr.at[t, f, land], ys.at[d], yrs.at[t, f, land],
            device_id={"gy": gy + 2 * d - 1},
        )

    def j_copy(d, land):
        return pltpu.make_async_remote_copy(
            jm.at[d], jx.at[land], xs.at[d], xr.at[0, 0, 0, land], device_id={"gx": gx + 2 * d - 1}
        )

    def x_send(t, f, *kinds, where=True):
        def go(d):
            for kind in kinds:
                if kind == 2:
                    x_copy(t, f, kind, d, 1 - d).start()
                    continue
                for lo, hi, k in parts(t, 2 * f + kind):
                    copy = x_copy(t, f, kind, d, 1 - d, lo, hi)
                    if k is None:
                        copy.start()
                    else:
                        pl.when(detour[k][d])(detour_copy(k, d).start)
                        pl.when(jnp.logical_not(detour[k][d]))(copy.start)

        pl.when(has_x[1] & odd_x & where)(functools.partial(go, 1))
        pl.when(has_x[0] & where)(functools.partial(go, 0))
        pl.when(has_x[1] & jnp.logical_not(odd_x) & where)(functools.partial(go, 1))

    def x_wait(t, f, kind):
        rows = 6 * fz if kind else 3 * (cz + 1) + 8 + (8 if t == 0 and f == 0 else 0)
        each(has_x, lambda d: drain(xr.at[t, f, kind, d], rows))

    def y_send(t, f):
        each(has_y, lambda d: y_copy(t, f, d, 1 - d).start())

    def y_wait(t, f):
        each(has_y, lambda d: y_copy(t, f, d, d).wait_recv())

    lane = lax.broadcasted_iota(jnp.int32, (8, LANES), 1)
    sub = lax.broadcasted_iota(jnp.int32, (8, LANES), 0)
    first, last = lane == 0, lane == LANES - 1
    left = lane < LANES // 2
    even = lane - 2 * (lane // 2) == 0
    pair_of = lane * 2 - jnp.where(left, 0, LANES)
    half_of = (lane // 2, lane // 2 + LANES // 2)
    y_edge = (first & has_y[0]) | (last & has_y[1])

    def north(v):
        return pltpu.roll(v, LANES - 1, 1)

    def south(v):
        return pltpu.roll(v, 1, 1)

    def take(v, index):
        return jnp.take_along_axis(v, index, axis=1, mode="promise_in_bounds")

    def spread(v, at, rows):
        return jnp.broadcast_to(v[:, at : at + 1], (rows, LANES))

    for t in range(STEPS):
        for i in range(6):
            row = jnp.zeros((1, LANES), f32)
            cn[t, i, low_c : low_c + 1, :] = row
            xc[t, 0, i, low_c : low_c + 1, :] = row
            xc[t, 1, i, low_c : low_c + 1, :] = row
    cor[...] = jnp.zeros(cor.shape, f32)
    gt[...] = jnp.zeros(gt.shape, f32)
    qs[...] = jnp.zeros(qs.shape, f32)
    gs[...] = jnp.zeros(gs.shape, f32)
    jm[...] = jnp.ones(jm.shape, f32)
    for d in range(2):

        @pl.when(jnp.logical_not(has_x[d]))
        def _():
            for t in range(STEPS):
                xf[t, d] = jnp.zeros(xf.shape[2:], f32)
                xc[t, d] = jnp.zeros(xc.shape[2:], f32)
                for f in range(2):
                    xk[t, f, d] = jnp.zeros(xk.shape[3:], f32)
            jx[d] = jnp.ones(jx.shape[1:], f32)

        @pl.when(jnp.logical_not(has_y[d]))
        def _():
            for t in range(STEPS):
                for f in range(2):
                    yr[t, f, d] = jnp.zeros(yr.shape[3:], f32)

    def ridge(t, f):
        for c in range(3):
            i = 3 * f + c
            for y in range(2):
                gs[y, c : c + 1] = (
                    fn[t, 0, i, y, low_f - 1 : low_f, :] + fn[t, 1, i, y, low_f - 1 : low_f, :]
                )
        a, b = gs[0], gs[1]
        a, b = take(a + north(a), pair_of), take(b + north(b), pair_of)
        mean = 0.25 * jnp.where(left, a, b)
        for c in range(3):
            cn[t, 3 * f + c, TOP - 1 : TOP, :] = mean[c : c + 1]

    def copy_top(t, x, i):
        for y in range(2):
            fn[t, x, i, y, TOP - 1 : TOP, :] = fn[t, x, i, y, TOP : TOP + 1, :]

    def pack(t, f):
        wide = lax.broadcasted_iota(jnp.int32, (rows_c, LANES), 1)
        one = lax.broadcasted_iota(jnp.int32, (1, LANES), 1)
        spare = jnp.zeros((1, LANES), f32)
        thin = lax.broadcasted_iota(jnp.int32, (rows_f, LANES), 1)
        out = jnp.zeros((rows_c, LANES), f32)
        fine = jnp.zeros((rows_f, LANES), f32)
        for d in range(2):
            at = (0, LANES - 1)[d]
            for c in range(3):
                i, j = 3 * f + c, 16 * d + (2, 3, 5)[c]
                v = spread(cn[t, i, TOP - 1 : TOP - 1 + rows_c, :], at, rows_c)
                out = jnp.where((wide == j) | (wide == j + 8), v, out)
                for x in range(2):
                    v = spread(fn[t, x, i, d, TOP - 1 : TOP - 1 + rows_f, :], at, rows_f)
                    fine = jnp.where(thin == 16 * d + 8 * x + (0, 1, 4)[c], v, fine)
            j, v = 16 * d, spread(cn[t, 3 * f + 2, TOP : TOP + 1, :], at, 1)
            spare = jnp.where((one == j) | (one == j + 8), v, spare)
            if t == 0 and f == 0:
                for x in range(2):
                    v = jnp.broadcast_to(jm[x, d : d + 1, at : at + 1], (rows_f, LANES))
                    fine = jnp.where(thin == 16 * d + 8 * x + 6, v, fine)
        of_fine = thin - 8 * (thin // 8)
        of_fine = (of_fine < 2) | (of_fine == 4) | (of_fine == 6)
        qs[0:rows_f, :] = jnp.where(of_fine, fine, out[0:rows_f])
        qs[rows_f:rows_c, :] = out[rows_f:]
        qs[LANES - 1 :, :] = spare
        pk[t, f] = jnp.transpose(qs[...])[0:32]

    def begin(f):
        drain(ins.at[f], 12 * fz + 3 * cz + (0 if f else 4))
        for c in range(3):
            i = 3 * f + c
            for x in range(2):
                for y in range(2):
                    fn[0, x, i, y, TOP : TOP + fz, :] = fin[i, pl.ds(2 * y + x, fz, stride=4), :]
                copy_top(0, x, i)
        ridge(0, f)

    begin(0)
    for x in range(2):
        for y in range(2):
            jm[x, y : y + 1] = 1.0 + tp[x : x + 1, y * LANES : (y + 1) * LANES].astype(f32) * (1.0 / 1024.0)
    count = sum(h.astype(jnp.int32) for h in has_x + has_y + tuple(side & (rank < len(share)) for side in outer))
    pl.semaphore_wait(barrier, count)
    each(has_x, lambda d: j_copy(d, 1 - d).start())
    x_send(0, 0, 0, 1)
    pack(0, 0)
    y_send(0, 0)
    begin(1)
    pack(0, 1)
    y_send(0, 1)
    y_wait(0, 0)
    x_send(0, 0, 2)
    x_send(0, 1, 0, 1)
    y_wait(0, 1)
    x_send(0, 1, 2)

    def spacings():
        for q in range(4):
            for y in range(2):
                row = jx[q // 3, y : y + 1] if q in (0, 3) else jm[q - 1, y : y + 1]
                inv = jnp.broadcast_to(1.0 / row, (8, LANES))
                rj[q, y] = inv
                if q in (1, 2):
                    rj2[q - 1, y] = inv * inv
        for x in range(2):
            sides = []
            for s in range(2):
                row = yr[0, 0, s, 8 * x + 6 : 8 * x + 7, 0:1]
                row = jnp.broadcast_to(1.0 / jnp.where(row == 0.0, 1.0, row), (8, LANES))
                rjh[s, x] = row
                sides.append(row)
            rjl[x] = jnp.where(left, sides[0], sides[1])

    def halos(t, f):
        inside = lane <= fz
        for s in range(2):
            own = [yr[t, f, s, 8 * x : 8 * x + 8] for x in range(2)]
            west, east = xk[t, f, 0, s], xk[t, f, 1, s]
            cross = (own[1] - west, east - own[0], east - west)

            def put(k, row):
                at = 2 * k + 1 - s
                gt[at : at + 1, :] = row

            d = north(own[0]) - south(own[0])
            for c in range(3):
                put(c, own[0][(2, 3, 5)[c] :][0:1])
            put(3, cross[2][3:4])
            put(4, cross[2][2:3] + d[5:6])
            put(5, d[3:4])
            for x in range(2):
                v = jnp.where(inside, own[x], 0.0)
                d = (north(v) - south(v)) * rjh[s, x]
                k = 6 + 6 * x
                for c in range(3):
                    put(k + c, own[x][(0, 1, 4)[c] :][0:1])
                put(k + 3, cross[x][1:2])
                put(k + 4, cross[x][0:1] + d[4:5])
                put(k + 5, d[1:2])
        tt[...] = jnp.transpose(gt[...])

    def item(v, k):
        return pltpu.roll(v, LANES - 1 - 2 * k, 1)

    def coarse(t, f, other):
        for v in range(cz // 8):
            r = TOP + 8 * v
            th = tt[8 * v + 1 : 8 * v + 9, :]
            mu = (0.25 * STEP_SQUARED) * sc[8 * v : 8 * v + 8, :]
            both = (0.25 * STEP_SQUARED) * lc[8 * v : 8 * v + 8, :] + mu
            xx, yy, zz, cross, rise, tilt, twice = [], [], [], [], [], [], []
            for c in range(3):
                i = 3 * f + c
                u = cn[t, i, r : r + 8, :]
                e, w = xc[t, 1, i, r : r + 8, :], xc[t, 0, i, r : r + 8, :]
                dn, up = cn[t, i, r + 1 : r + 9, :], cn[t, i, r - 1 : r + 7, :]
                h = item(th, c)
                u2 = 2.0 * u
                twice.append(u2)
                xx.append(e + w - u2)
                yy.append(jnp.where(last, h, north(u)) + jnp.where(first, h, south(u)) - u2)
                zz.append(dn + up - u2)
                cross.append(e - w)
                rise.append(dn - up)
                if c == 1:
                    tilt.append(None)
                else:
                    ed, eu = xc[t, 1, i, r + 1 : r + 9, :], xc[t, 1, i, r - 1 : r + 7, :]
                    wd, wu = xc[t, 0, i, r + 1 : r + 9, :], xc[t, 0, i, r - 1 : r + 7, :]
                    tilt.append((ed - eu) - (wd - wu))
            ac = []
            for k, a in enumerate((cross[1], cross[0] + rise[2], rise[1])):
                h = item(th, 3 + k)
                ac.append(jnp.where(last, h, north(a)) - jnp.where(first, h, south(a)))
            grad = (
                xx[0] + 0.25 * (ac[0] + tilt[2]),
                yy[1] + 0.25 * ac[1],
                zz[2] + 0.25 * (ac[2] + tilt[0]),
            )
            prod = None
            for c in range(3):
                i = 3 * f + c
                before = co[i, 8 * v : 8 * v + 8, :] if t == 0 else cn[t - 1, i, r : r + 8, :]
                new = (twice[c] - before) + (mu * (xx[c] + yy[c] + zz[c]) + both * grad[c])
                if t < STEPS - 1:
                    cn[t + 1, i, r : r + 8, :] = new
                else:
                    cout[i, 8 * v : 8 * v + 8, :] = new
                if other is not None:
                    o = 3 * other + c
                    if t < STEPS - 1:
                        pair = cn[t + 1, o, r : r + 8, :]
                    else:
                        pair = cout[o, 8 * v : 8 * v + 8, :]
                    prod = pair * new if prod is None else prod + pair * new
            if other is not None:
                if t > 0:
                    prod = prod + cker[8 * v : 8 * v + 8, :]
                cker[8 * v : 8 * v + 8, :] = prod

    def ghost(t, f):
        at = (2, 3, 0)
        for c in range(3):
            i = 3 * f + c
            gs[0, at[c] : at[c] + 1] = xc[t, 0, i, TOP : TOP + 1, :]
            gs[1, at[c] : at[c] + 1] = cn[t, i, TOP : TOP + 1, :]
            gs[2, at[c] : at[c] + 1] = xc[t, 1, i, TOP : TOP + 1, :]
        flat = [gs[k] for k in range(3)]
        rim = []
        for tiles in (
            [xk[t, f, 0, s] for s in range(2)],
            [yr[t, f, s, 0:8] for s in range(2)],
            [xk[t, f, 1, s] for s in range(2)],
        ):
            ends = [
                jnp.where(sub == 0, spread(v, LANES - 1, 8), spread(v, 1, 8)) for v in tiles
            ]
            rim.append(jnp.where(left, ends[0], ends[1]))

        def mix(v):
            lo, mid, hi = v
            return (
                0.75 * lo + 0.25 * mid,
                0.75 * mid + 0.25 * lo,
                0.75 * mid + 0.25 * hi,
                0.75 * hi + 0.25 * mid,
            )

        for q, (v, h) in enumerate(zip(mix(flat), mix(rim))):
            a = 0.75 * v + 0.25 * jnp.where(first, h, south(v))
            b = 0.75 * v + 0.25 * jnp.where(last, h, north(v))
            for y in range(2):
                g = jnp.where(even, take(a, half_of[y]), take(b, half_of[y]))
                if q in (0, 3):
                    g = jnp.where(has_x[q // 3], g, 0.0)
                for c in range(3):
                    i = 3 * f + c
                    if q in (0, 3):
                        xf[t, q // 3, i, y, low_f : low_f + 1, :] = g[at[c] : at[c] + 1]
                    else:
                        fn[t, q - 1, i, y, low_f : low_f + 1, :] = g[at[c] : at[c] + 1]
            if q in (1, 2):
                g = jnp.where(y_edge, 0.75 * h + 0.25 * v, 0.0) * rjl[q - 1]
                cor[q - 1, 0, 7:8] = g[0:1]
                cor[q - 1, 1, 7:8] = g[3:4]

    def sides_top(t, f):
        for side in range(2):
            for c in (0, 2):
                for y in range(2):
                    xf[t, side, 3 * f + c, y, TOP - 1 : TOP, :] = xf[
                        t, side, 3 * f + c, y, TOP : TOP + 1, :
                    ]

    def fine(t, f):
        def plane(q, c, y, r):
            i = 3 * f + c
            if q in (0, 3):
                return xf[t, q // 3, i, y, r : r + 8, :]
            return fn[t, q - 1, i, y, r : r + 8, :]

        def before(c, x, y, r, pick):
            if t == 0:
                return fo[3 * f + c, pick, :]
            return fn[t - 1, x, 3 * f + c, y, r : r + 8, :]

        def store(c, x, y, r, pick, new):
            if t < STEPS - 1:
                fn[t + 1, x, 3 * f + c, y, r : r + 8, :] = new
            else:
                fout[c, pick, :] = new

        def product(x, y, r, pick, new):
            if f == 1:
                fker[pick, :] = sum(fn[t + 1, x, c, y, r : r + 8, :] * new[c] for c in range(3))

        fine_update(fz, plane, before, store, product, tt, rj, rj2, cor, sf, lf)

    def finish_level(t, f):
        for c in range(3):
            for x in range(2):
                copy_top(t, x, 3 * f + c)
        ridge(t, f)
        x_send(t, f, 0)
        x_send(t, f, 1, where=f == 0 or jnp.logical_not(middle))
        pack(t, f)
        y_send(t, f)

    for t in range(STEPS):
        for n in range(2):
            for m in {(0, 0): (0, 1), (0, 1): (2, 3), (1, 0): (0,), (1, 1): ()}[t, n]:
                if (t, m) == (0, 3):
                    pl.when(rank != len(share) - 1)(functools.partial(pass_on, t, m))
                else:
                    pass_on(t, m)
            if t > 0 and n == 0:
                pass_on(1, 1)
                y_wait(t, 1)
                x_send(t, 1, 2)
                x_send(t, 1, 1, where=middle)
            f, other = n, None if n == 0 else 0
            x_wait(t, f, 0)
            if t == 0 and n == 0:
                spacings()
                drain(ins.at[2], 8 * cz)
            halos(t, f)
            coarse(t, f, other)
            if t < STEPS - 1 and n == 1:
                y_wait(t + 1, 0)
                x_send(t + 1, 0, 2)
            ghost(t, f)
            if t == 0 and n == 0:
                pl.when(rank == len(share) - 1)(functools.partial(pass_on, 0, 3))
            x_wait(t, f, 1)
            if t == 0 and n == 0:
                drain(ins.at[3], 32 * fz)
            sides_top(t, f)
            if (t, n) != (STEPS - 1, 1):
                fine(t, f)
            if t < STEPS - 1:
                finish_level(t + 1, f)

    sent = 8 + 2 * STEPS * (3 * (cz + 1) + 6 * fz + 8)
    each(has_x, lambda d: drain(xs.at[d], sent))
    each(has_y, lambda d: drain(ys.at[d], 32 * STEPS))
    for k, n in enumerate(share):
        rows = sum(
            (hi - lo) * (2 * fz if m % 2 else cz + 1) for _, m, lo, hi, least in route if n >= least
        )
        pl.when(middle & (rank == k))(functools.partial(drain, vs.at[0], rows))


def fine_update(fz, plane, before, store, product, tt, rj, rj2, cor, sf, lf, done=None):
    lane = lax.broadcasted_iota(jnp.int32, (8, LANES), 1)
    first, last = lane == 0, lane == LANES - 1

    def ends(a, b, h):
        na, nb = pltpu.roll(a, LANES - 1, 1), pltpu.roll(b, LANES - 1, 1)
        sa, sb = pltpu.roll(a, 1, 1), pltpu.roll(b, 1, 1)
        return (
            (jnp.where(last, nb, na), jnp.where(first, h, sa)),
            (jnp.where(last, h, nb), jnp.where(first, sa, sb)),
        )

    for v in range(fz // 8):
        r = TOP + 8 * v
        th = tt[8 * v + 1 : 8 * v + 9, :]
        for x in range(2):
            q, k = x + 1, 6 + 6 * x
            mid, xx, yy, zz, twice, tilt, ac = {}, {}, {}, {}, {}, {}, {}
            va = [[None, None] for _ in range(3)]
            for y in range(2):
                inv = rj[q, y]
                cross, rise = [], []
                for c in range(3):
                    u = plane(q, c, y, r)
                    e, w = plane(q + 1, c, y, r), plane(q - 1, c, y, r)
                    dn, up = plane(q, c, y, r + 1), plane(q, c, y, r - 1)
                    mid[c, y] = u
                    u2 = 2.0 * u
                    twice[c, y] = u2
                    xx[c, y] = e + w - u2
                    zz[c, y] = (dn + up - u2) * rj2[x, y]
                    cross.append(e - w)
                    rise.append((dn - up) * inv if c else None)
                    if c != 1:
                        ed, eu = plane(q + 1, c, y, r + 1), plane(q + 1, c, y, r - 1)
                        wd, wu = plane(q - 1, c, y, r + 1), plane(q - 1, c, y, r - 1)
                        tilt[c, y] = (ed - eu) * rj[q + 1, y] - (wd - wu) * rj[q - 1, y]
                va[0][y] = cross[1]
                va[1][y] = cross[0] + rise[2]
                va[2][y] = rise[1]
            for c in range(3):
                h = pltpu.roll(th, LANES - 1 - 2 * (k + c), 1)
                for y, (n, s) in enumerate(ends(mid[c, 0], mid[c, 1], h)):
                    yy[c, y] = n + s - twice[c, y]
            for c in range(3):
                h = pltpu.roll(th, LANES - 1 - 2 * (k + 3 + c), 1)
                if c and v == fz // 8 - 1:
                    h = h + cor[x, c - 1]
                for y, (n, s) in enumerate(ends(va[c][0], va[c][1], h)):
                    ac[c, y] = n - s
            for y in range(2):
                pick = pl.ds(32 * v + 2 * y + x, 8, stride=4)
                mu = STEP_SQUARED * sf[pick, :]
                both = STEP_SQUARED * lf[pick, :] + mu
                grad = (
                    xx[0, y] + 0.25 * (ac[0, y] + tilt[2, y]),
                    yy[1, y] + 0.25 * ac[1, y],
                    zz[2, y] + 0.25 * (ac[2, y] + tilt[0, y]),
                )
                new = []
                for c in range(3):
                    new.append(
                        (twice[c, y] - before(c, x, y, r, pick))
                        + (mu * (xx[c, y] + yy[c, y] + zz[c, y]) + both * grad[c])
                    )
                    store(c, x, y, r, pick, new[c])
                product(x, y, r, pick, new)
        if done is not None:
            done(v)


def put_body(
    fz, cz,
    fa, ca, fk, ck, fn, xf, tt, rj, rj2, cor, sf, lf,
    fout, cout, fker, cker,
    fb, kb, span, sem,
):
    t = STEPS - 1

    def write(a, b):
        pltpu.make_async_copy(a, b, sem.at[0]).start()

    write(fa, fout.at[pl.ds(0, 3)])
    write(ca, cout)
    write(ck, cker)

    def plane(q, c, y, r):
        if q in (0, 3):
            return xf[t, q // 3, 3 + c, y, r : r + 8, :]
        return fn[t, q - 1, 3 + c, y, r : r + 8, :]

    def before(c, x, y, r, pick):
        return fn[t - 1, x, 3 + c, y, r : r + 8, :]

    def store(c, x, y, r, pick, new):
        fb[c, pick, :] = new

    def product(x, y, r, pick, new):
        kb[pick, :] = fk[pick, :] + sum(fa[c, pick, :] * new[c] for c in range(3))

    def done(v):
        rows = pl.ds(32 * v, 32)
        write(fb.at[:, rows], fout.at[pl.ds(3, 3), rows])

    fine_update(fz, plane, before, store, product, tt, rj, rj2, cor, sf, lf, done)
    write(kb, fker)
    part = span.at[pl.ds(0, 28 * fz + 7 * cz)]
    pltpu.make_async_copy(part, part, sem.at[0]).wait()


def rows_view(a):
    lead = a.shape[:-3]
    fz, fx, fy = a.shape[-3:]
    n = len(lead)
    a = a.reshape(lead + (fz, fx, fy // LANES, LANES))
    a = a.transpose(tuple(range(n)) + (n, n + 2, n + 1, n + 3))
    return a.reshape(((6,) if lead else ()) + (fz * fx * fy // LANES, LANES))


def rows_back(a, shape):
    lead = shape[:-3]
    fz, fx, fy = shape[-3:]
    n = len(lead)
    a = a.reshape(lead + (fz, fy // LANES, fx, LANES))
    a = a.transpose(tuple(range(n)) + (n, n + 2, n + 1, n + 3))
    return a.reshape(shape)


def on_device(fold, fnow, cold, cnow, shf, laf, shc, lac, topo):
    nx, ny = lax.axis_size("gx"), lax.axis_size("gy")
    fz, fx, fy = shf.shape
    cz, cx, cy = shc.shape
    if fx != 2 or cx != 1 or cy != LANES or fy != 2 * cy or fz % 8 or cz % 8 or cz + 8 > LANES:
        raise ValueError("unsupported tile")
    f32 = jnp.float32
    dma = pltpu.SemaphoreType.DMA
    nrows = fz * fx * fy // LANES
    vm = pl.BlockSpec(memory_space=pltpu.VMEM)
    hbm = pl.BlockSpec(memory_space=pl.ANY)
    shapes = ((6, nrows, LANES), (6, cz, cy), (nrows, LANES), (cz, cy))
    planes = (STEPS, 2, 6, 2, fz + 16, LANES)
    passed = ((3, nrows, LANES),) + shapes[1:] + (planes, planes, (LANES, LANES))
    passed += ((4, 2, 8, LANES), (2, 2, 8, LANES), (2, 2, 8, LANES), shapes[2], shapes[2])
    args = (
        rows_view(fold),
        rows_view(fnow),
        cold.reshape(6, cz, cy),
        cnow.reshape(6, cz, cy),
        rows_view(shf),
        rows_view(laf),
        shc.reshape(cz, cy),
        lac.reshape(cz, cy),
        topo,
    )
    inner = pl.pallas_call(
        functools.partial(body, nx, ny, fz, cz),
        out_shape=tuple(pltpu.VMEM(s, f32) for s in passed),
        in_specs=[hbm] * 9,
        out_specs=(vm,) * len(passed),
        scratch_shapes=[
            pltpu.VMEM((6, nrows, LANES), f32),
            pltpu.VMEM((6, nrows, LANES), f32),
            pltpu.VMEM((6, cz, cy), f32),
            pltpu.VMEM((cz, cy), f32),
            pltpu.VMEM((cz, cy), f32),
            pltpu.VMEM((fx, fy), jnp.int32),
            pltpu.VMEM((STEPS, 6, cz + 16, LANES), f32),
            pltpu.VMEM((STEPS, 2, 6, cz + 16, LANES), f32),
            pltpu.VMEM((2, 8, LANES), f32),
            pltpu.VMEM((2, 8, LANES), f32),
            pltpu.VMEM((STEPS, 2, 32, LANES), f32),
            pltpu.VMEM((STEPS, 2, 2, 16, LANES), f32),
            pltpu.VMEM((STEPS, 2, 2, 2, 8, LANES), f32),
            pltpu.VMEM((2, 2, 8, LANES), f32),
            pltpu.VMEM((2, 8, LANES), f32),
            pltpu.VMEM((LANES, LANES), f32),
            pltpu.VMEM((LANES, LANES), f32),
            pltpu.VMEM((3, 8, LANES), f32),
            pltpu.VMEM((4 * STEPS * (3 * cz + 6 * fz + 32), LANES), f32),
            pltpu.VMEM((STEPS, 2, 3, 2, fz, LANES), f32),
            pltpu.VMEM((STEPS, 2, 3, cz + 8, LANES), f32),
            dma((4,)),
            dma((2,)),
            dma((STEPS, 2, 2, 2)),
            dma((2,)),
            dma((STEPS, 2, 2)),
            dma((1,)),
            dma((7,)),
        ],
        compiler_params=pltpu.CompilerParams(
            collective_id=0, has_side_effects=True, vmem_limit_bytes=32 << 20
        ),
        name="wave",
    )(*[pltpu.with_memory_space_constraint(a, pltpu.HBM) for a in args])
    fout, cout, fker, cker = pl.pallas_call(
        functools.partial(put_body, fz, cz),
        out_shape=tuple(jax.ShapeDtypeStruct(s, f32) for s in shapes),
        in_specs=[vm] * len(passed),
        out_specs=(hbm,) * 4,
        scratch_shapes=[
            pltpu.VMEM((3, nrows, LANES), f32),
            pltpu.VMEM((nrows, LANES), f32),
            pltpu.VMEM((28 * fz + 7 * cz, LANES), f32),
            dma((1,)),
        ],
        compiler_params=pltpu.CompilerParams(vmem_limit_bytes=4 << 20),
        name="put",
    )(*[pltpu.with_memory_space_constraint(a, pltpu.VMEM) for a in inner])
    return (
        rows_back(fout, fold.shape),
        cout.reshape(cold.shape),
        rows_back(fker, shf.shape),
        cker.reshape(shc.shape),
    )


def solution(mesh):
    field, coef = P(None, None, None, "gx", "gy"), P(None, "gx", "gy")
    return jax.shard_map(
        on_device,
        mesh=mesh,
        in_specs=(field,) * 4 + (coef,) * 4 + (P("gx", "gy"),),
        out_specs=(field, field, coef, coef),
        check_vma=False,
    )
```

```python
import functools

import jax
import jax.numpy as jnp
from jax import lax
from jax.experimental import pallas as pl
from jax.experimental.pallas import tpu as pltpu
from jax.sharding import PartitionSpec as P

STEPS = 2
STEP_SQUARED = 0.04
LANES = 128
TOP = 8


def body(
    nx, ny, fz, cz,
    fold, fnow, cold, cnow, shf, laf, shc, lac, topo,
    fout, cout, fker, cker, fn, xf, tt, rj, rj2, cor, sf, lf,
    fin, fo, co, sc, lc, tp,
    cn, xc, jm, jx, pk, yr, xk,
    rjh, rjl, qs, gt, gs, span, via_f, via_c,
    ins, xs, xr, ys, yrs, vs, vr,
):
    f32 = jnp.float32
    gx, gy = lax.axis_index("gx"), lax.axis_index("gy")
    has_x = (gx > 0, gx < nx - 1)
    has_y = (gy > 0, gy < ny - 1)
    rows_c = cz + 8
    rows_f = fz + 8
    low_c, low_f = TOP + cz, TOP + fz

    def each(flags, action):
        for d in range(2):
            pl.when(flags[d])(functools.partial(action, d))

    def half(f):
        return pl.ds(3 * f, 3)

    loads = {
        "f0": (fnow.at[half(0)], fin.at[half(0)]),
        "c0": (cnow.at[half(0)], cn.at[0, half(0), pl.ds(TOP, cz)]),
        "topo": (topo, tp),
        "f1": (fnow.at[half(1)], fin.at[half(1)]),
        "c1": (cnow.at[half(1)], cn.at[0, half(1), pl.ds(TOP, cz)]),
        "co": (cold, co),
        "sc": (shc, sc),
        "lc": (lac, lc),
        "fo": (fold, fo),
        "sf": (shf, sf),
        "lf": (laf, lf),
    }
    slots = {"f0": 0, "c0": 0, "topo": 0, "f1": 1, "c1": 1, "co": 2, "sc": 2, "lc": 2}

    def drain(sem, rows):
        part = span.at[pl.ds(0, rows)]
        pltpu.make_async_copy(part, part, sem).wait()

    planes = nx // 4 if nx % 4 == 0 else 0
    share = [min(3, (8 * (planes - 1 - z) + planes) // (2 * planes)) for z in range(planes - 1)]
    route = (
        (0, 0, 2, 3, 3), (0, 1, 0, 3, 3), (0, 2, 0, 3, 2), (0, 3, 0, 3, 1),
        (1, 0, 0, 1, 3), (1, 0, 1, 3, 2), (1, 1, 0, 3, 1),
    )
    reach = [sum(n >= least for n in share) for *_, least in route]
    at4, plane = lax.rem(gx, 4), gx // 4
    rank = jnp.where((at4 == 1) | (at4 == 3), plane, planes - 1 - plane)
    outer = ((at4 == 0), (at4 == 3))
    middle = (at4 == 1) | (at4 == 2)
    detour = [[outer[d] & (rank < r) for d in range(2)] for r in reach]
    passes = [middle & (rank < r) for r in reach]

    def parts(t, m):
        cut = [(lo, hi, k) for k, (a, b, lo, hi, _) in enumerate(route) if (a, b) == (t, m)]
        at, out = 0, []
        for lo, hi, k in cut + [(3, 3, None)]:
            out += [(at, lo, None)] if at < lo else []
            out += [(lo, hi, k)] if lo < hi else []
            at = hi
        return out
    from_left = at4 == 2
    odd_x = lax.rem(gx, 2) == 1

    barrier = pltpu.get_barrier_semaphore()
    each(has_x, lambda d: pl.semaphore_signal(barrier, inc=1, device_id={"gx": gx + 2 * d - 1}))
    each(has_y, lambda d: pl.semaphore_signal(barrier, inc=1, device_id={"gy": gy + 2 * d - 1}))

    @pl.when(middle & (rank < len(share)))
    def _():
        source = gx + jnp.where(from_left, -2, 2)
        pl.semaphore_signal(barrier, inc=1, device_id={"gx": source})

    for k, (a, b) in loads.items():
        pltpu.make_async_copy(a, b, ins.at[slots.get(k, 3)]).start()

    def x_copy(t, f, kind, d, land, lo=0, hi=3):
        some = pl.ds(3 * f + lo, hi - lo)
        if kind == 0:
            rows = pl.ds(TOP - 1, cz + 1)
            src, dst = cn.at[t, some, rows], xc.at[t, land, some, rows]
        elif kind == 1:
            rows = pl.ds(TOP, fz)
            src, dst = fn.at[t, d, some, :, rows], xf.at[t, land, some, :, rows]
        else:
            src, dst = yr.at[t, f, :, pl.ds(8 * d, 4)], xk.at[t, f, land, :, pl.ds(0, 4)]
        return pltpu.make_async_remote_copy(
            src, dst, xs.at[d], xr.at[t, f, kind % 2, land], device_id={"gx": gx + 2 * d - 1}
        )

    def ends_of(k, d, land):
        t, m, lo, hi, _ = route[k]
        some = pl.ds(3 * (m // 2) + lo, hi - lo)
        if m % 2 == 0:
            rows, stop = pl.ds(TOP - 1, cz + 1), via_c.at[t, m // 2, pl.ds(lo, hi - lo), pl.ds(0, cz + 1)]
            return cn.at[t, some, rows], stop, xc.at[t, land, some, rows]
        rows, stop = pl.ds(TOP, fz), via_f.at[t, m // 2, pl.ds(lo, hi - lo)]
        return fn.at[t, d, some, :, rows], stop, xf.at[t, land, some, :, rows]

    def detour_copy(k, d):
        src, stop, _ = ends_of(k, d, 0)
        return pltpu.make_async_remote_copy(
            src, stop, xs.at[d], vr.at[k], device_id={"gx": gx + 2 - 4 * d}
        )

    def pass_copy(k, land):
        t, m, *_ = route[k]
        _, stop, dst = ends_of(k, 0, land)
        return pltpu.make_async_remote_copy(
            stop, dst, vs.at[0], xr.at[t, m // 2, m % 2, land],
            device_id={"gx": gx + 3 - 6 * land},
        )

    def pass_on(t, m):
        for k, (a, b, *_) in enumerate(route):
            if (a, b) == (t, m):

                @pl.when(passes[k])
                def _():
                    _, stop, _ = ends_of(k, 0, 0)
                    pltpu.make_async_copy(stop, stop, vr.at[k]).wait()
                    for land in range(2):
                        pl.when(at4 == 1 + land)(pass_copy(k, land).start)

    def corner_copy(t, f, d, e):
        return pltpu.make_async_remote_copy(
            pk.at[t, f, pl.ds(16 * e + 8 * d, 4)], xk.at[t, f, 1 - d, 1 - e, pl.ds(0, 4)],
            xs.at[d], xr.at[t, f, 0, 1 - d],
            device_id={"gx": gx + 2 * d - 1, "gy": gy + 2 * e - 1},
        )

    def corner_send(t, f):
        for d in range(2):
            for e in range(2):
                pl.when(has_x[d] & has_y[e])(corner_copy(t, f, d, e).start)

    def drain_y(sem, rows, more):
        both, some = has_y[0] & has_y[1], has_y[0] | has_y[1]
        pl.when(both)(functools.partial(drain, sem, rows + 2 * more))
        pl.when(some & jnp.logical_not(both))(functools.partial(drain, sem, rows + more))
        pl.when(jnp.logical_not(some))(functools.partial(drain, sem, rows))

    def y_copy(t, f, d, land):
        return pltpu.make_async_remote_copy(
            pk.at[t, f, pl.ds(16 * d, 16)], yr.at[t, f, land], ys.at[d], yrs.at[t, f, land],
            device_id={"gy": gy + 2 * d - 1},
        )

    def j_copy(d, land):
        return pltpu.make_async_remote_copy(
            jm.at[d], jx.at[land], xs.at[d], xr.at[0, 0, 0, land], device_id={"gx": gx + 2 * d - 1}
        )

    def x_send(t, f, *kinds):
        def go(d):
            for kind in kinds:
                if kind == 2:
                    x_copy(t, f, kind, d, 1 - d).start()
                    continue
                for lo, hi, k in parts(t, 2 * f + kind):
                    copy = x_copy(t, f, kind, d, 1 - d, lo, hi)
                    if k is None:
                        copy.start()
                    else:
                        pl.when(detour[k][d])(detour_copy(k, d).start)
                        pl.when(jnp.logical_not(detour[k][d]))(copy.start)

        pl.when(has_x[1] & odd_x)(functools.partial(go, 1))
        pl.when(has_x[0])(functools.partial(go, 0))
        pl.when(has_x[1] & jnp.logical_not(odd_x))(functools.partial(go, 1))

    def x_wait(t, f, kind):
        rows = 6 * fz if kind else 3 * (cz + 1) + (0 if t else 8) + (8 if t == 0 and f == 0 else 0)
        if t > 0 and kind == 0:
            each(has_x, lambda d: drain_y(xr.at[t, f, kind, d], rows, 4))
        else:
            each(has_x, lambda d: drain(xr.at[t, f, kind, d], rows))

    def y_send(t, f):
        each(has_y, lambda d: y_copy(t, f, d, 1 - d).start())

    def y_wait(t, f):
        each(has_y, lambda d: y_copy(t, f, d, d).wait_recv())

    lane = lax.broadcasted_iota(jnp.int32, (8, LANES), 1)
    sub = lax.broadcasted_iota(jnp.int32, (8, LANES), 0)
    first, last = lane == 0, lane == LANES - 1
    left = lane < LANES // 2
    even = lane - 2 * (lane // 2) == 0
    pair_of = lane * 2 - jnp.where(left, 0, LANES)
    half_of = (lane // 2, lane // 2 + LANES // 2)
    y_edge = (first & has_y[0]) | (last & has_y[1])

    def north(v):
        return pltpu.roll(v, LANES - 1, 1)

    def south(v):
        return pltpu.roll(v, 1, 1)

    def take(v, index):
        return jnp.take_along_axis(v, index, axis=1, mode="promise_in_bounds")

    def spread(v, at, rows):
        return jnp.broadcast_to(v[:, at : at + 1], (rows, LANES))

    for t in range(STEPS):
        for i in range(6):
            row = jnp.zeros((1, LANES), f32)
            cn[t, i, low_c : low_c + 1, :] = row
            xc[t, 0, i, low_c : low_c + 1, :] = row
            xc[t, 1, i, low_c : low_c + 1, :] = row
    cor[...] = jnp.zeros(cor.shape, f32)
    gt[...] = jnp.zeros(gt.shape, f32)
    qs[...] = jnp.zeros(qs.shape, f32)
    gs[...] = jnp.zeros(gs.shape, f32)
    jm[...] = jnp.ones(jm.shape, f32)
    for d in range(2):

        @pl.when(jnp.logical_not(has_x[d]))
        def _():
            for t in range(STEPS):
                xf[t, d] = jnp.zeros(xf.shape[2:], f32)
                xc[t, d] = jnp.zeros(xc.shape[2:], f32)
                for f in range(2):
                    xk[t, f, d] = jnp.zeros(xk.shape[3:], f32)
            jx[d] = jnp.ones(jx.shape[1:], f32)

        @pl.when(jnp.logical_not(has_y[d]))
        def _():
            for t in range(STEPS):
                for f in range(2):
                    yr[t, f, d] = jnp.zeros(yr.shape[3:], f32)
                    if t > 0:
                        for side in range(2):
                            xk[t, f, side, d] = jnp.zeros(xk.shape[4:], f32)

    def ridge(t, f):
        for c in range(3):
            i = 3 * f + c
            for y in range(2):
                gs[y, c : c + 1] = (
                    fn[t, 0, i, y, low_f - 1 : low_f, :] + fn[t, 1, i, y, low_f - 1 : low_f, :]
                )
        a, b = gs[0], gs[1]
        a, b = take(a + north(a), pair_of), take(b + north(b), pair_of)
        mean = 0.25 * jnp.where(left, a, b)
        for c in range(3):
            cn[t, 3 * f + c, TOP - 1 : TOP, :] = mean[c : c + 1]

    def copy_top(t, x, i):
        for y in range(2):
            fn[t, x, i, y, TOP - 1 : TOP, :] = fn[t, x, i, y, TOP : TOP + 1, :]

    def pack(t, f):
        wide = lax.broadcasted_iota(jnp.int32, (rows_c, LANES), 1)
        one = lax.broadcasted_iota(jnp.int32, (1, LANES), 1)
        spare = jnp.zeros((1, LANES), f32)
        thin = lax.broadcasted_iota(jnp.int32, (rows_f, LANES), 1)
        out = jnp.zeros((rows_c, LANES), f32)
        fine = jnp.zeros((rows_f, LANES), f32)
        for d in range(2):
            at = (0, LANES - 1)[d]
            for c in range(3):
                i, j = 3 * f + c, 16 * d + (2, 3, 5)[c]
                v = spread(cn[t, i, TOP - 1 : TOP - 1 + rows_c, :], at, rows_c)
                out = jnp.where((wide == j) | (wide == j + 8), v, out)
                for x in range(2):
                    v = spread(fn[t, x, i, d, TOP - 1 : TOP - 1 + rows_f, :], at, rows_f)
                    fine = jnp.where(thin == 16 * d + 8 * x + (0, 1, 4)[c], v, fine)
            j, v = 16 * d, spread(cn[t, 3 * f + 2, TOP : TOP + 1, :], at, 1)
            spare = jnp.where((one == j) | (one == j + 8), v, spare)
            if t == 0 and f == 0:
                for x in range(2):
                    v = jnp.broadcast_to(jm[x, d : d + 1, at : at + 1], (rows_f, LANES))
                    fine = jnp.where(thin == 16 * d + 8 * x + 6, v, fine)
        of_fine = thin - 8 * (thin // 8)
        of_fine = (of_fine < 2) | (of_fine == 4) | (of_fine == 6)
        qs[0:rows_f, :] = jnp.where(of_fine, fine, out[0:rows_f])
        qs[rows_f:rows_c, :] = out[rows_f:]
        qs[LANES - 1 :, :] = spare
        pk[t, f] = jnp.transpose(qs[...])[0:32]

    def begin(f):
        drain(ins.at[f], 12 * fz + 3 * cz + (0 if f else 4))
        for c in range(3):
            i = 3 * f + c
            for x in range(2):
                for y in range(2):
                    fn[0, x, i, y, TOP : TOP + fz, :] = fin[i, pl.ds(2 * y + x, fz, stride=4), :]
                copy_top(0, x, i)
        ridge(0, f)

    begin(0)
    for x in range(2):
        for y in range(2):
            jm[x, y : y + 1] = 1.0 + tp[x : x + 1, y * LANES : (y + 1) * LANES].astype(f32) * (1.0 / 1024.0)
    count = sum(h.astype(jnp.int32) for h in has_x + has_y + tuple(side & (rank < len(share)) for side in outer))
    pl.semaphore_wait(barrier, count)
    each(has_x, lambda d: j_copy(d, 1 - d).start())
    x_send(0, 0, 0, 1)
    pack(0, 0)
    y_send(0, 0)
    begin(1)
    pack(0, 1)
    y_send(0, 1)
    y_wait(0, 0)
    x_send(0, 0, 2)
    x_send(0, 1, 0, 1)
    y_wait(0, 1)
    x_send(0, 1, 2)

    def spacings():
        for q in range(4):
            for y in range(2):
                row = jx[q // 3, y : y + 1] if q in (0, 3) else jm[q - 1, y : y + 1]
                inv = jnp.broadcast_to(1.0 / row, (8, LANES))
                rj[q, y] = inv
                if q in (1, 2):
                    rj2[q - 1, y] = inv * inv
        for x in range(2):
            sides = []
            for s in range(2):
                row = yr[0, 0, s, 8 * x + 6 : 8 * x + 7, 0:1]
                row = jnp.broadcast_to(1.0 / jnp.where(row == 0.0, 1.0, row), (8, LANES))
                rjh[s, x] = row
                sides.append(row)
            rjl[x] = jnp.where(left, sides[0], sides[1])

    def halos(t, f):
        inside = lane <= fz
        for s in range(2):
            own = [yr[t, f, s, 8 * x : 8 * x + 8] for x in range(2)]
            west, east = xk[t, f, 0, s], xk[t, f, 1, s]
            cross = (own[1] - west, east - own[0], east - west)

            def put(k, row):
                at = 2 * k + 1 - s
                gt[at : at + 1, :] = row

            d = north(own[0]) - south(own[0])
            for c in range(3):
                put(c, own[0][(2, 3, 5)[c] :][0:1])
            put(3, cross[2][3:4])
            put(4, cross[2][2:3] + d[5:6])
            put(5, d[3:4])
            for x in range(2):
                v = jnp.where(inside, own[x], 0.0)
                d = (north(v) - south(v)) * rjh[s, x]
                k = 6 + 6 * x
                for c in range(3):
                    put(k + c, own[x][(0, 1, 4)[c] :][0:1])
                put(k + 3, cross[x][1:2])
                put(k + 4, cross[x][0:1] + d[4:5])
                put(k + 5, d[1:2])
        tt[...] = jnp.transpose(gt[...])

    def item(v, k):
        return pltpu.roll(v, LANES - 1 - 2 * k, 1)

    def coarse(t, f, other):
        for v in range(cz // 8):
            r = TOP + 8 * v
            th = tt[8 * v + 1 : 8 * v + 9, :]
            mu = (0.25 * STEP_SQUARED) * sc[8 * v : 8 * v + 8, :]
            both = (0.25 * STEP_SQUARED) * lc[8 * v : 8 * v + 8, :] + mu
            xx, yy, zz, cross, rise, tilt, twice = [], [], [], [], [], [], []
            for c in range(3):
                i = 3 * f + c
                u = cn[t, i, r : r + 8, :]
                e, w = xc[t, 1, i, r : r + 8, :], xc[t, 0, i, r : r + 8, :]
                dn, up = cn[t, i, r + 1 : r + 9, :], cn[t, i, r - 1 : r + 7, :]
                h = item(th, c)
                u2 = 2.0 * u
                twice.append(u2)
                xx.append(e + w - u2)
                yy.append(jnp.where(last, h, north(u)) + jnp.where(first, h, south(u)) - u2)
                zz.append(dn + up - u2)
                cross.append(e - w)
                rise.append(dn - up)
                if c == 1:
                    tilt.append(None)
                else:
                    ed, eu = xc[t, 1, i, r + 1 : r + 9, :], xc[t, 1, i, r - 1 : r + 7, :]
                    wd, wu = xc[t, 0, i, r + 1 : r + 9, :], xc[t, 0, i, r - 1 : r + 7, :]
                    tilt.append((ed - eu) - (wd - wu))
            ac = []
            for k, a in enumerate((cross[1], cross[0] + rise[2], rise[1])):
                h = item(th, 3 + k)
                ac.append(jnp.where(last, h, north(a)) - jnp.where(first, h, south(a)))
            grad = (
                xx[0] + 0.25 * (ac[0] + tilt[2]),
                yy[1] + 0.25 * ac[1],
                zz[2] + 0.25 * (ac[2] + tilt[0]),
            )
            prod = None
            for c in range(3):
                i = 3 * f + c
                before = co[i, 8 * v : 8 * v + 8, :] if t == 0 else cn[t - 1, i, r : r + 8, :]
                new = (twice[c] - before) + (mu * (xx[c] + yy[c] + zz[c]) + both * grad[c])
                if t < STEPS - 1:
                    cn[t + 1, i, r : r + 8, :] = new
                else:
                    cout[i, 8 * v : 8 * v + 8, :] = new
                if other is not None:
                    o = 3 * other + c
                    if t < STEPS - 1:
                        pair = cn[t + 1, o, r : r + 8, :]
                    else:
                        pair = cout[o, 8 * v : 8 * v + 8, :]
                    prod = pair * new if prod is None else prod + pair * new
            if other is not None:
                if t > 0:
                    prod = prod + cker[8 * v : 8 * v + 8, :]
                cker[8 * v : 8 * v + 8, :] = prod

    def ghost(t, f):
        at = (2, 3, 0)
        for c in range(3):
            i = 3 * f + c
            gs[0, at[c] : at[c] + 1] = xc[t, 0, i, TOP : TOP + 1, :]
            gs[1, at[c] : at[c] + 1] = cn[t, i, TOP : TOP + 1, :]
            gs[2, at[c] : at[c] + 1] = xc[t, 1, i, TOP : TOP + 1, :]
        flat = [gs[k] for k in range(3)]
        rim = []
        for tiles in (
            [xk[t, f, 0, s] for s in range(2)],
            [yr[t, f, s, 0:8] for s in range(2)],
            [xk[t, f, 1, s] for s in range(2)],
        ):
            ends = [
                jnp.where(sub == 0, spread(v, LANES - 1, 8), spread(v, 1, 8)) for v in tiles
            ]
            rim.append(jnp.where(left, ends[0], ends[1]))

        def mix(v):
            lo, mid, hi = v
            return (
                0.75 * lo + 0.25 * mid,
                0.75 * mid + 0.25 * lo,
                0.75 * mid + 0.25 * hi,
                0.75 * hi + 0.25 * mid,
            )

        for q, (v, h) in enumerate(zip(mix(flat), mix(rim))):
            a = 0.75 * v + 0.25 * jnp.where(first, h, south(v))
            b = 0.75 * v + 0.25 * jnp.where(last, h, north(v))
            for y in range(2):
                g = jnp.where(even, take(a, half_of[y]), take(b, half_of[y]))
                if q in (0, 3):
                    g = jnp.where(has_x[q // 3], g, 0.0)
                for c in range(3):
                    i = 3 * f + c
                    if q in (0, 3):
                        xf[t, q // 3, i, y, low_f : low_f + 1, :] = g[at[c] : at[c] + 1]
                    else:
                        fn[t, q - 1, i, y, low_f : low_f + 1, :] = g[at[c] : at[c] + 1]
            if q in (1, 2):
                g = jnp.where(y_edge, 0.75 * h + 0.25 * v, 0.0) * rjl[q - 1]
                cor[q - 1, 0, 7:8] = g[0:1]
                cor[q - 1, 1, 7:8] = g[3:4]

    def sides_top(t, f):
        for side in range(2):
            for c in (0, 2):
                for y in range(2):
                    xf[t, side, 3 * f + c, y, TOP - 1 : TOP, :] = xf[
                        t, side, 3 * f + c, y, TOP : TOP + 1, :
                    ]

    def fine(t, f):
        def plane(q, c, y, r):
            i = 3 * f + c
            if q in (0, 3):
                return xf[t, q // 3, i, y, r : r + 8, :]
            return fn[t, q - 1, i, y, r : r + 8, :]

        def before(c, x, y, r, pick):
            if t == 0:
                return fo[3 * f + c, pick, :]
            return fn[t - 1, x, 3 * f + c, y, r : r + 8, :]

        def store(c, x, y, r, pick, new):
            if t < STEPS - 1:
                fn[t + 1, x, 3 * f + c, y, r : r + 8, :] = new
            else:
                fout[c, pick, :] = new

        def product(x, y, r, pick, new):
            if f == 1:
                fker[pick, :] = sum(fn[t + 1, x, c, y, r : r + 8, :] * new[c] for c in range(3))

        fine_update(fz, plane, before, store, product, tt, rj, rj2, cor, sf, lf)

    def finish_level(t, f):
        for c in range(3):
            for x in range(2):
                copy_top(t, x, 3 * f + c)
        ridge(t, f)
        x_send(t, f, 0)
        pack(t, f)
        y_send(t, f)
        corner_send(t, f)
        x_send(t, f, 1)

    for t in range(STEPS):
        for n in range(2):
            for m in {(0, 0): (0, 1), (0, 1): (2, 3), (1, 0): (0,), (1, 1): ()}[t, n]:
                if (t, m) == (0, 3):
                    pl.when(rank != len(share) - 1)(functools.partial(pass_on, t, m))
                else:
                    pass_on(t, m)
            if t > 0 and n == 0:
                pass_on(1, 1)
            f, other = n, None if n == 0 else 0
            x_wait(t, f, 0)
            if t == 0 and n == 0:
                spacings()
                drain(ins.at[2], 8 * cz)
            if t > 0:
                y_wait(t, f)
            halos(t, f)
            coarse(t, f, other)
            ghost(t, f)
            if t == 0 and n == 0:
                pl.when(rank == len(share) - 1)(functools.partial(pass_on, 0, 3))
            x_wait(t, f, 1)
            if t == 0 and n == 0:
                drain(ins.at[3], 32 * fz)
            sides_top(t, f)
            if (t, n) != (STEPS - 1, 1):
                fine(t, f)
            if t < STEPS - 1:
                finish_level(t + 1, f)

    sent = 8 + 16 + 2 * STEPS * (3 * (cz + 1) + 6 * fz)
    each(has_x, lambda d: drain_y(xs.at[d], sent, 8 * (STEPS - 1)))
    each(has_y, lambda d: drain(ys.at[d], 32 * STEPS))
    for k, n in enumerate(share):
        rows = sum(
            (hi - lo) * (2 * fz if m % 2 else cz + 1) for _, m, lo, hi, least in route if n >= least
        )
        pl.when(middle & (rank == k))(functools.partial(drain, vs.at[0], rows))


def fine_update(fz, plane, before, store, product, tt, rj, rj2, cor, sf, lf, done=None):
    lane = lax.broadcasted_iota(jnp.int32, (8, LANES), 1)
    first, last = lane == 0, lane == LANES - 1

    def ends(a, b, h):
        na, nb = pltpu.roll(a, LANES - 1, 1), pltpu.roll(b, LANES - 1, 1)
        sa, sb = pltpu.roll(a, 1, 1), pltpu.roll(b, 1, 1)
        return (
            (jnp.where(last, nb, na), jnp.where(first, h, sa)),
            (jnp.where(last, h, nb), jnp.where(first, sa, sb)),
        )

    for v in range(fz // 8):
        r = TOP + 8 * v
        th = tt[8 * v + 1 : 8 * v + 9, :]
        for x in range(2):
            q, k = x + 1, 6 + 6 * x
            mid, xx, yy, zz, twice, tilt, ac = {}, {}, {}, {}, {}, {}, {}
            va = [[None, None] for _ in range(3)]
            for y in range(2):
                inv = rj[q, y]
                cross, rise = [], []
                for c in range(3):
                    u = plane(q, c, y, r)
                    e, w = plane(q + 1, c, y, r), plane(q - 1, c, y, r)
                    dn, up = plane(q, c, y, r + 1), plane(q, c, y, r - 1)
                    mid[c, y] = u
                    u2 = 2.0 * u
                    twice[c, y] = u2
                    xx[c, y] = e + w - u2
                    zz[c, y] = (dn + up - u2) * rj2[x, y]
                    cross.append(e - w)
                    rise.append((dn - up) * inv if c else None)
                    if c != 1:
                        ed, eu = plane(q + 1, c, y, r + 1), plane(q + 1, c, y, r - 1)
                        wd, wu = plane(q - 1, c, y, r + 1), plane(q - 1, c, y, r - 1)
                        tilt[c, y] = (ed - eu) * rj[q + 1, y] - (wd - wu) * rj[q - 1, y]
                va[0][y] = cross[1]
                va[1][y] = cross[0] + rise[2]
                va[2][y] = rise[1]
            for c in range(3):
                h = pltpu.roll(th, LANES - 1 - 2 * (k + c), 1)
                for y, (n, s) in enumerate(ends(mid[c, 0], mid[c, 1], h)):
                    yy[c, y] = n + s - twice[c, y]
            for c in range(3):
                h = pltpu.roll(th, LANES - 1 - 2 * (k + 3 + c), 1)
                if c and v == fz // 8 - 1:
                    h = h + cor[x, c - 1]
                for y, (n, s) in enumerate(ends(va[c][0], va[c][1], h)):
                    ac[c, y] = n - s
            for y in range(2):
                pick = pl.ds(32 * v + 2 * y + x, 8, stride=4)
                mu = STEP_SQUARED * sf[pick, :]
                both = STEP_SQUARED * lf[pick, :] + mu
                grad = (
                    xx[0, y] + 0.25 * (ac[0, y] + tilt[2, y]),
                    yy[1, y] + 0.25 * ac[1, y],
                    zz[2, y] + 0.25 * (ac[2, y] + tilt[0, y]),
                )
                new = []
                for c in range(3):
                    new.append(
                        (twice[c, y] - before(c, x, y, r, pick))
                        + (mu * (xx[c, y] + yy[c, y] + zz[c, y]) + both * grad[c])
                    )
                    store(c, x, y, r, pick, new[c])
                product(x, y, r, pick, new)
        if done is not None:
            done(v)


def put_body(
    fz, cz,
    fa, ca, fk, ck, fn, xf, tt, rj, rj2, cor, sf, lf,
    fout, cout, fker, cker,
    fb, kb, span, sem,
):
    t = STEPS - 1

    def write(a, b):
        pltpu.make_async_copy(a, b, sem.at[0]).start()

    write(fa, fout.at[pl.ds(0, 3)])
    write(ca, cout)
    write(ck, cker)

    def plane(q, c, y, r):
        if q in (0, 3):
            return xf[t, q // 3, 3 + c, y, r : r + 8, :]
        return fn[t, q - 1, 3 + c, y, r : r + 8, :]

    def before(c, x, y, r, pick):
        return fn[t - 1, x, 3 + c, y, r : r + 8, :]

    def store(c, x, y, r, pick, new):
        fb[c, pick, :] = new

    def product(x, y, r, pick, new):
        kb[pick, :] = fk[pick, :] + sum(fa[c, pick, :] * new[c] for c in range(3))

    def done(v):
        rows = pl.ds(32 * v, 32)
        write(fb.at[:, rows], fout.at[pl.ds(3, 3), rows])

    fine_update(fz, plane, before, store, product, tt, rj, rj2, cor, sf, lf, done)
    write(kb, fker)
    part = span.at[pl.ds(0, 28 * fz + 7 * cz)]
    pltpu.make_async_copy(part, part, sem.at[0]).wait()


def rows_view(a):
    lead = a.shape[:-3]
    fz, fx, fy = a.shape[-3:]
    n = len(lead)
    a = a.reshape(lead + (fz, fx, fy // LANES, LANES))
    a = a.transpose(tuple(range(n)) + (n, n + 2, n + 1, n + 3))
    return a.reshape(((6,) if lead else ()) + (fz * fx * fy // LANES, LANES))


def rows_back(a, shape):
    lead = shape[:-3]
    fz, fx, fy = shape[-3:]
    n = len(lead)
    a = a.reshape(lead + (fz, fy // LANES, fx, LANES))
    a = a.transpose(tuple(range(n)) + (n, n + 2, n + 1, n + 3))
    return a.reshape(shape)


def on_device(fold, fnow, cold, cnow, shf, laf, shc, lac, topo):
    nx, ny = lax.axis_size("gx"), lax.axis_size("gy")
    fz, fx, fy = shf.shape
    cz, cx, cy = shc.shape
    if fx != 2 or cx != 1 or cy != LANES or fy != 2 * cy or fz % 8 or cz % 8 or cz + 8 > LANES:
        raise ValueError("unsupported tile")
    f32 = jnp.float32
    dma = pltpu.SemaphoreType.DMA
    nrows = fz * fx * fy // LANES
    vm = pl.BlockSpec(memory_space=pltpu.VMEM)
    hbm = pl.BlockSpec(memory_space=pl.ANY)
    shapes = ((6, nrows, LANES), (6, cz, cy), (nrows, LANES), (cz, cy))
    planes = (STEPS, 2, 6, 2, fz + 16, LANES)
    passed = ((3, nrows, LANES),) + shapes[1:] + (planes, planes, (LANES, LANES))
    passed += ((4, 2, 8, LANES), (2, 2, 8, LANES), (2, 2, 8, LANES), shapes[2], shapes[2])
    args = (
        rows_view(fold),
        rows_view(fnow),
        cold.reshape(6, cz, cy),
        cnow.reshape(6, cz, cy),
        rows_view(shf),
        rows_view(laf),
        shc.reshape(cz, cy),
        lac.reshape(cz, cy),
        topo,
    )
    inner = pl.pallas_call(
        functools.partial(body, nx, ny, fz, cz),
        out_shape=tuple(pltpu.VMEM(s, f32) for s in passed),
        in_specs=[hbm] * 9,
        out_specs=(vm,) * len(passed),
        scratch_shapes=[
            pltpu.VMEM((6, nrows, LANES), f32),
            pltpu.VMEM((6, nrows, LANES), f32),
            pltpu.VMEM((6, cz, cy), f32),
            pltpu.VMEM((cz, cy), f32),
            pltpu.VMEM((cz, cy), f32),
            pltpu.VMEM((fx, fy), jnp.int32),
            pltpu.VMEM((STEPS, 6, cz + 16, LANES), f32),
            pltpu.VMEM((STEPS, 2, 6, cz + 16, LANES), f32),
            pltpu.VMEM((2, 8, LANES), f32),
            pltpu.VMEM((2, 8, LANES), f32),
            pltpu.VMEM((STEPS, 2, 32, LANES), f32),
            pltpu.VMEM((STEPS, 2, 2, 16, LANES), f32),
            pltpu.VMEM((STEPS, 2, 2, 2, 8, LANES), f32),
            pltpu.VMEM((2, 2, 8, LANES), f32),
            pltpu.VMEM((2, 8, LANES), f32),
            pltpu.VMEM((LANES, LANES), f32),
            pltpu.VMEM((LANES, LANES), f32),
            pltpu.VMEM((3, 8, LANES), f32),
            pltpu.VMEM((4 * STEPS * (3 * cz + 6 * fz + 32), LANES), f32),
            pltpu.VMEM((STEPS, 2, 3, 2, fz, LANES), f32),
            pltpu.VMEM((STEPS, 2, 3, cz + 8, LANES), f32),
            dma((4,)),
            dma((2,)),
            dma((STEPS, 2, 2, 2)),
            dma((2,)),
            dma((STEPS, 2, 2)),
            dma((1,)),
            dma((7,)),
        ],
        compiler_params=pltpu.CompilerParams(
            collective_id=0, has_side_effects=True, vmem_limit_bytes=32 << 20
        ),
        name="wave",
    )(*[pltpu.with_memory_space_constraint(a, pltpu.HBM) for a in args])
    fout, cout, fker, cker = pl.pallas_call(
        functools.partial(put_body, fz, cz),
        out_shape=tuple(jax.ShapeDtypeStruct(s, f32) for s in shapes),
        in_specs=[vm] * len(passed),
        out_specs=(hbm,) * 4,
        scratch_shapes=[
            pltpu.VMEM((3, nrows, LANES), f32),
            pltpu.VMEM((nrows, LANES), f32),
            pltpu.VMEM((28 * fz + 7 * cz, LANES), f32),
            dma((1,)),
        ],
        compiler_params=pltpu.CompilerParams(vmem_limit_bytes=4 << 20),
        name="put",
    )(*[pltpu.with_memory_space_constraint(a, pltpu.VMEM) for a in inner])
    return (
        rows_back(fout, fold.shape),
        cout.reshape(cold.shape),
        rows_back(fker, shf.shape),
        cker.reshape(shc.shape),
    )


def solution(mesh):
    field, coef = P(None, None, None, "gx", "gy"), P(None, "gx", "gy")
    return jax.shard_map(
        on_device,
        mesh=mesh,
        in_specs=(field,) * 4 + (coef,) * 4 + (P("gx", "gy"),),
        out_specs=(field, field, coef, coef),
        check_vma=False,
    )
```
